256 devices in a mesh: gx: 8 (over z_hi, x), gy: 32 (over z_lo, y, core).
Axes of the slice: x: 4, y: 4, z: 8 (z_hi: 2, z_lo: 4; z = z_hi * 4 + z_lo), core: 2. Of those that a mesh axis runs over, the one named last changes fastest.
Arguments:
- residual_in: float32 [8, 32, 1024, 256], P('gx', 'gy'), may hold values from -6 to 6
- neumann: float32 [8, 32, 1024, 1024], P('gx', 'gy'), may hold values from -0.1875 to 0.1875
- dirichlet: float32 [8, 32, 1024, 1024], P('gx', 'gy'), may hold values from -0.1875 to 0.1875
- coarse: float32 [8, 2048, 2048], P('gx', 'gy'), may hold values from -0.125 to 0.125
- decay: float32 [8, 32, 64], P('gx', 'gy'), may hold values from 0.4 to 1
- face_rows: int32 [8, 32, 1024], P('gx', 'gy'), may hold values from 0 to 1023, each once within a row
- primal: int32 [8, 32, 64], P('gx', 'gy'), may hold values from 0 to 1023, as said below
Outputs:
- solution: float32 [8, 32, 1024, 256], P('gx', 'gy')
- residual: float32 [8, 32, 1024, 256], P('gx', 'gy')
The draws below stay inside these ranges and needn't reach their ends.
Inputs may be any that keep to these rules, and one draw needn't show every extreme that they name: `primal`: each subdomain's 64 entries are distinct rows of its interface. `face_rows`: each subdomain's entries name every interface row once.
All inputs are finite; a program needn't handle non-finite values.
Results may differ from the reference program's by a relative error of at most 0.0001.
Values sent between devices are 32-bit elements; how exact they have to be, the bound alone decides.
No kernel may reach another device: no remote copies, remote signals or barrier semaphores. Data moves between devices by JAX's collectives and lax.ppermute only.
A program may use at most 64 MiB of HBM per device.

```python
import jax
import jax.numpy as jnp
from jax import lax

M = 1024
P_SIZE = 64
R = 256
STEPS = 2
SUBX = 8
SUBY = 32
FACE = 256
COARSE = 2048


def draw_primal(key, part):
    keys = jax.random.split(jax.random.fold_in(key, 17), SUBX * SUBY)
    perms = jax.vmap(lambda single: jax.random.permutation(single, M))(keys)
    picked = perms[:, :P_SIZE]
    top_shift = M - 1 - picked[0, 0]
    bottom_shift = (M - picked[1, 0]) % M
    which = jnp.arange(SUBX * SUBY, dtype=jnp.int32)
    offsets = jnp.where(which == 0, top_shift, jnp.where(which == 1, bottom_shift, 0))
    picked = (picked + offsets[:, None]) % M
    return picked.reshape(SUBX, SUBY, P_SIZE).astype(jnp.int32)


def level_of(stream_key, extent, cuts, least, largest):
    level, own = 1.0, jax.random.fold_in(stream_key, 6)
    for axis_at, shards_of in cuts:
        heights = jnp.exp(jax.random.uniform(jax.random.fold_in(own, axis_at), (shards_of,), jnp.float32, least / len(cuts), largest / len(cuts)))
        level = level * jnp.repeat(heights, extent[axis_at] // shards_of).reshape([-1 if axis == axis_at else 1 for axis in range(len(extent))])
    return level


def normal_values(stream_key, shape, width, reach, cuts=(), kind=jnp.bfloat16):
    values = width * jax.random.normal(stream_key, shape, jnp.float32)
    if cuts:
        values = values * level_of(stream_key, shape, cuts, -0.22, 0.18)
    return jnp.clip(values, -reach, reach).astype(kind)


def setup_inputs(seed: int = 0) -> dict:
    key_of = jax.random.split(jax.random.key(seed), 8)
    return {
        "residual_in": normal_values(key_of[0], (SUBX, SUBY, M, R), 1.0, 6.0, ((0, 8), (1, 32)), jnp.float32),
        "neumann": normal_values(key_of[1], (SUBX, SUBY, M, M), M ** -0.5, 0.1875, ((0, 8), (1, 32)), jnp.float32),
        "dirichlet": normal_values(key_of[2], (SUBX, SUBY, M, M), M ** -0.5, 0.1875, ((0, 8), (1, 32)), jnp.float32),
        "coarse": normal_values(key_of[3], (SUBX, COARSE, COARSE), COARSE ** -0.5, 0.125, ((0, 8), (1, 32)), jnp.float32),
        "decay": jnp.clip(0.4 + 0.6 * jax.random.uniform(key_of[4], (SUBX, SUBY, P_SIZE), jnp.float32) ** level_of(key_of[4], (SUBX, SUBY, P_SIZE), ((0, 8), (1, 32)), -0.2, 0.2), 0.4, 1.0),
        "face_rows": jax.vmap(lambda own: jax.random.permutation(own, M))(jax.random.split(key_of[5], SUBX * SUBY)).reshape((SUBX, SUBY, M)).astype(jnp.int32),
        "primal": draw_primal(jax.random.fold_in(key_of[7], 71), 0),
    }


def neighbours(field, face_rows, inverse):
    faces = jnp.take_along_axis(field, face_rows[..., None], axis=2)
    low_row = faces[:, :, 0:FACE]
    high_row = faces[:, :, FACE:2 * FACE]
    low_col = faces[:, :, 2 * FACE:3 * FACE]
    high_col = faces[:, :, 3 * FACE:4 * FACE]
    zero_row = jnp.zeros_like(low_row[:1])
    zero_col = jnp.zeros_like(low_row[:, :1])
    recv_zero = jnp.concatenate([zero_row, high_row[:-1]], axis=0)
    recv_one = jnp.concatenate([low_row[1:], zero_row], axis=0)
    recv_two = jnp.concatenate([zero_col, high_col[:, :-1]], axis=1)
    recv_three = jnp.concatenate([low_col[:, 1:], zero_col], axis=1)
    stacked = jnp.concatenate([recv_zero, recv_one, recv_two, recv_three], axis=2)
    return jnp.take_along_axis(stacked, inverse[..., None], axis=2)


def reference(residual_in, neumann, dirichlet, coarse, decay, face_rows, primal):
    high = lax.Precision.HIGHEST
    inverse = jnp.argsort(face_rows, axis=-1).astype(jnp.int32)
    onehot = (jnp.arange(M, dtype=jnp.int32)[None, None, :, None] == primal[:, :, None, :]).astype(jnp.float32)
    residual = residual_in
    solution = jnp.zeros_like(residual_in)
    for step in range(STEPS):
        jump = residual - neighbours(residual, face_rows, inverse)
        work = jnp.einsum("xymn,xynr->xymr", neumann, jump, precision=high)
        prim_val = jnp.take_along_axis(work, primal[..., None], axis=2)
        cvec = prim_val.reshape(SUBX, COARSE, R)
        cq = jnp.einsum("xab,xbr->xar", coarse, cvec, precision=high).reshape(SUBX, SUBY, P_SIZE, R)

        def link(prev, item):
            rate, value = item
            current = value + rate[:, :, None] * prev
            return current, current

        start_val = jnp.zeros((SUBY, P_SIZE, R), jnp.float32)
        unused, chain = lax.scan(link, start_val, (decay, cq))
        corrected = work + jnp.einsum("xymp,xypr->xymr", onehot, chain, precision=high)
        update = jnp.einsum("xymn,xynr->xymr", dirichlet, corrected, precision=high)
        solution = solution + update
        residual = jump - 0.5 * update
    return solution, residual
```

```python
import jax
import jax.numpy as jnp
from jax import lax
from jax.sharding import PartitionSpec as P

NZ, NY, NC, NX, NH = 4, 4, 2, 4, 2
GY = NZ * NY * NC
GX = NX * NH
HIGH = lax.Precision.HIGH


def gy_index(z, y, c):
    return (z * NY + y) * NC + c


def pull_y(v, k):
    return lax.ppermute(v, "gy", [(gy_index(z, (y + k) % NY, c), gy_index(z, y, c)) for z in range(NZ) for y in range(NY) for c in range(NC)])


def pull_z(v, k):
    return lax.ppermute(v, "gy", [(gy_index((z + k) % NZ, y, c), gy_index(z, y, c)) for z in range(NZ) for y in range(NY) for c in range(NC)])


def pull_core(v):
    return lax.ppermute(v, "gy", [(i, i ^ 1) for i in range(GY)])


def pull_x(v, k):
    return lax.ppermute(v, "gx", [(h * NX + (x + k) % NX, h * NX + x) for h in range(NH) for x in range(NX)])


def pull_half(v):
    return lax.ppermute(v, "gx", [(i, (i + NX) % GX) for i in range(GX)])


def ring(v, axis, by):
    n = GX if axis == "gx" else GY
    return lax.ppermute(v, axis, [(i, (i + by) % n) for i in range(n)])


def dot(a, b, dims=((1,), (0,))):
    return lax.dot_general(a, b, (dims, ((), ())), precision=HIGH, preferred_element_type=jnp.float32)


def halves(v):
    hi = lax.reduce_precision(v, 8, 7)
    return hi.astype(jnp.bfloat16), (v - hi).astype(jnp.bfloat16)


def pick(onehot, v, dims):
    hi, lo = halves(v)
    g = lambda p: lax.dot_general(onehot, p, (dims, ((), ())), preferred_element_type=jnp.float32)
    return g(hi) + g(lo)


def local(residual_in, neumann, dirichlet, coarse, decay, face_rows, primal):
    f32 = jnp.float32
    r0 = residual_in[0, 0]
    nmat = neumann[0, 0]
    dmat = dirichlet[0, 0]
    crow = coarse[0]
    dec = decay[0, 0]
    fr = face_rows[0, 0]
    pr = primal[0, 0]
    m, r = r0.shape
    face = m // 4
    p = pr.shape[0]
    gx = lax.axis_index("gx")
    gy = lax.axis_index("gy")
    h, x = gx // NX, gx % NX
    z, y, c = gy // (NY * NC), (gy // NC) % NY, gy % NC
    has = (gx > 0, gx < GX - 1, gy > 0, gy < GY - 1)

    def exchange(blocks):
        got = (ring(blocks[1], "gx", 1), ring(blocks[0], "gx", -1), ring(blocks[3], "gy", 1), ring(blocks[2], "gy", -1))
        return [jnp.where(ok, g, jnp.zeros_like(g)) for ok, g in zip(has, got)]

    def split_rows(v):
        return [v[k * face:(k + 1) * face] for k in range(4)]

    def split_cols(v):
        return [v[:, k * face:(k + 1) * face] for k in range(4)]

    perm = (lax.broadcasted_iota(jnp.int32, (m, m), 0) == fr[None, :]).astype(jnp.bfloat16)
    recv0 = jnp.concatenate(exchange(split_rows(pick(perm, r0, ((0,), (0,))))), axis=0)

    dx = jnp.stack([dec] + [pull_x(dec[None], k)[0] for k in range(1, NX)])
    dx = jnp.stack([jnp.take(dx, (j - x) % NX, axis=0) for j in range(NX)])
    other = pull_half(dx)
    dlo = jnp.where(h == 0, dx, other)
    dhi = jnp.where(h == 0, other, dx)

    width = NC * p
    c4 = crow.reshape(p, NZ, NY * width)
    c4 = lax.dynamic_slice_in_dim(jnp.concatenate([c4, c4], axis=2), y * width, NY * width, axis=2)
    cblk = []
    for k in range(NZ):
        part = lax.dynamic_index_in_dim(c4, (z - k) % NZ, axis=1, keepdims=False)
        cblk.append(part if k == 0 else pull_z(part, k))
    cblk = jnp.concatenate(cblk, axis=0)

    sel = (pr[:, None] == lax.broadcasted_iota(jnp.int32, (p, m), 1)).astype(jnp.bfloat16)
    npr = jnp.take(nmat, pr, axis=0)
    nprf = lax.dot_general(npr, perm.astype(f32), (((1,), (0,)), ((), ())), precision=HIGH, preferred_element_type=f32)
    dpt = pick(sel, dmat, ((1,), (1,)))
    dptf = lax.dot_general(dpt, perm.astype(f32), (((1,), (0,)), ((), ())), precision=HIGH, preferred_element_type=f32)
    ends = exchange(split_cols(dptf))
    gmat = [dot(npr, dpt, ((1,), (1,)))] + [-dot(a, b, ((1,), (1,))) for a, b in zip(split_cols(nprf), ends)]
    gcat = -0.5 * jnp.concatenate(gmat, axis=1)

    mine = jnp.where(h == 0, dlo, dhi)

    def weights(t):
        absolute = []
        for j in range(NX):
            w = jnp.ones((p,), f32)
            for i in range(j + 1, NX):
                w = w * jnp.where(i <= t, mine[i], 1.0)
            absolute.append(jnp.where(j <= t, w, 0.0))
        absolute = jnp.stack(absolute)
        return jnp.stack([jnp.take(absolute, (x + k) % NX, axis=0) for k in range(NX)])

    def through(t):
        w = jnp.ones((p,), f32)
        for i in range(NX):
            w = w * jnp.where(i <= t, dhi[i], 1.0)
        return jnp.where(h == 0, 0.0, w)

    zero_at = jnp.stack([jnp.where((x + k) % NX == 0, jnp.ones((p,), f32), 0.0) for k in range(NX)])
    w_last = weights(NX - 1)
    w_send = jnp.where(h == 0, w_last, zero_at)
    w_own, v_own = weights(x), through(x)
    w_low, v_low = weights(x - 1), through(x - 1)
    edge = jnp.logical_and(h == 0, x == NX - 1)
    w_high = jnp.where(edge, dhi[0] * w_last, weights(x + 1))
    v_high = jnp.where(edge, 1.0, through(x + 1))

    def mix(w, parts):
        total = w[0][:, None] * parts[0]
        for k in range(1, len(parts)):
            total = total + w[k][:, None] * parts[k]
        return total

    def coarse_chain(cvec, near):
        own = [cvec] + [pull_y(cvec, k) for k in range(1, NY)]
        twin = [pull_core(v) for v in own]
        rows = []
        for a, b in zip(own, twin):
            rows += [jnp.where(c == 0, a, b), jnp.where(c == 0, b, a)]
        part = dot(cblk, jnp.concatenate(rows, axis=0))
        cq = part[:p]
        for k in range(1, NZ):
            cq = cq + pull_z(part[k * p:(k + 1) * p], NZ - k)
        pieces = [cq] + [pull_x(cq, k) for k in range(1, NX)]
        over = pull_half(mix(w_send, pieces))
        chain = mix(w_own, pieces) + v_own[:, None] * over
        if not near:
            return chain
        low = mix(w_low, pieces) + v_low[:, None] * over
        high = mix(w_high, pieces) + v_high[:, None] * over
        return chain, low, high

    cvec = dot(npr, r0) - dot(nprf, recv0)
    jump0 = r0 - pick(perm, recv0, ((1,), (0,)))
    dw0 = dot(dmat, dot(nmat, jump0))
    base = jump0 - 0.5 * dw0
    recvb = jnp.concatenate(exchange(split_rows(pick(perm, base, ((0,), (0,))))), axis=0)
    cbase = dot(npr, base) - dot(nprf, recvb)

    chain0, low, high = coarse_chain(cvec, True)
    near = [low, high, ring(chain0, "gy", 1), ring(chain0, "gy", -1)]
    cvec1 = cbase + dot(gcat, jnp.concatenate([chain0] + near, axis=0))

    recv1 = recvb - 0.5 * jnp.concatenate([dot(e, n, ((0,), (0,))) for e, n in zip(ends, near)], axis=0)
    dc0 = dot(dpt, chain0, ((0,), (0,)))
    jump1 = base - 0.5 * dc0 - pick(perm, recv1, ((1,), (0,)))
    dw1 = dot(dmat, dot(nmat, jump1))
    chain1 = coarse_chain(cvec1, False)
    update1 = dw1 + dot(dpt, chain1, ((0,), (0,)))
    solution = dw0 + dc0 + update1
    residual = jump1 - 0.5 * update1
    return (solution[None, None], residual[None, None])


def solution(mesh):
    lead = P("gx", "gy", None, None)
    vec = P("gx", "gy", None)
    return jax.shard_map(
        local,
        mesh=mesh,
        in_specs=(lead, lead, lead, vec, vec, vec, vec),
        out_specs=(lead, lead),
        check_vma=False,
    )
```

```python
import functools

import jax
import jax.numpy as jnp
from jax import lax
from jax.experimental import pallas as pl
from jax.experimental.pallas import tpu as pltpu
from jax.sharding import PartitionSpec as P

NZ, NY, NC, NX, NH = 4, 4, 2, 4, 2
GY = NZ * NY * NC
GX = NX * NH
F32, BF16 = jnp.float32, jnp.bfloat16
COST = 1
VMEM, SMEM = pltpu.VMEM, pltpu.SMEM
NN, NT, TN = ((1,), (0,)), ((1,), (1,)), ((0,), (0,))


def gy_index(z, y, c):
    return (z * NY + y) * NC + c


def pull_y(v, k):
    return lax.ppermute(v, "gy", [(gy_index(z, (y + k) % NY, c), gy_index(z, y, c)) for z in range(NZ) for y in range(NY) for c in range(NC)])


def pull_z(v, k):
    return lax.ppermute(v, "gy", [(gy_index((z + k) % NZ, y, c), gy_index(z, y, c)) for z in range(NZ) for y in range(NY) for c in range(NC)])


def pull_core(v):
    return lax.ppermute(v, "gy", [(i, i ^ 1) for i in range(GY)])


def pull_x(v, k):
    return lax.ppermute(v, "gx", [(h * NX + (x + k) % NX, h * NX + x) for h in range(NH) for x in range(NX)])


def pull_half(v):
    return lax.ppermute(v, "gx", [(i, (i + NX) % GX) for i in range(GX)])


def ring(v, axis, by):
    n = GX if axis == "gx" else GY
    return lax.ppermute(v, axis, [(i, (i + by) % n) for i in range(n)])


def dot(a, b, dims=NN):
    return lax.dot_general(a, b, (dims, ((), ())), precision=lax.Precision.HIGH, preferred_element_type=F32)


def one_pass(a, b, dims):
    return lax.dot_general(a, b, (dims, ((), ())), preferred_element_type=F32)


def halves(v):
    hi = v.astype(BF16)
    return hi, (v - hi.astype(F32)).astype(BF16)


def three(a, b, dims=NN):
    ah, al = a if isinstance(a, tuple) else halves(a)
    bh, bl = b if isinstance(b, tuple) else halves(b)
    return one_pass(ah, bh, dims) + (one_pass(ah, bl, dims) + one_pass(al, bh, dims))


def after(values, *earlier):
    return lax.optimization_barrier((values, earlier))[0]


def call(body, outs, ins, *, grid=None, in_specs=None, out_specs=None, scratch=(), flops=0, name=None):
    whole = pl.BlockSpec(memory_space=VMEM)
    nbytes = sum(4 * v.size for v in ins) + sum(4 * o.size for o in outs)
    kwargs = {} if grid is None else {"grid": grid}
    return pl.pallas_call(
        body,
        out_shape=outs,
        in_specs=in_specs or [whole] * len(ins),
        out_specs=out_specs or [whole] * len(outs),
        scratch_shapes=list(scratch),
        compiler_params=pltpu.CompilerParams(vmem_limit_bytes=40 * 2**20),
        cost_estimate=pl.CostEstimate(flops=flops // COST, bytes_accessed=nbytes // COST, transcendentals=0),
        name=name,
        **kwargs,
    )(*ins)


def out(*shape):
    return jax.ShapeDtypeStruct(shape, F32)


def perm_block(fr_ref, at, face):
    m = fr_ref.shape[1]
    blocks = []
    for j in range(face // 128):
        ids = fr_ref[:, pl.ds(pl.multiple_of(at + j * 128, 128), 128)].astype(F32)
        ids = jnp.transpose(jnp.broadcast_to(ids, (128, 128)))
        lane = lax.broadcasted_iota(jnp.int32, (128, 128), 1).astype(F32)
        blocks.append(jnp.concatenate([(ids == lane + 128.0 * i).astype(F32).astype(BF16) for i in range(m // 128)], axis=1))
    return jnp.concatenate(blocks, axis=0)


def scatter_block(fr_ref, at, rows):
    m = fr_ref.shape[1]
    ids = lax.broadcasted_iota(jnp.int32, (rows, m), 0) + at
    return (ids == fr_ref[...]).astype(F32).astype(BF16)


def gather_faces(fr, v):
    m, r = v.shape
    face = m // 4

    def body(fr_ref, v_ref, *refs):
        outs, (hi, lo, got) = refs[:4], refs[4:]
        hi[...], lo[...] = halves(v_ref[...])

        @pl.loop(0, 4)
        def _(k):
            pb = perm_block(fr_ref, k * face, face)
            got[k] = one_pass(pb, hi[...], NN) + one_pass(pb, lo[...], NN)

        for k in range(4):
            outs[k][...] = got[k]

    return call(body, [out(face, r)] * 4, [fr, v], scratch=[VMEM((m, r), BF16)] * 2 + [VMEM((4, face, r), F32)], flops=4 * m * m * r, name="gather_faces")


def scatter_neumann(flags, fr, v, recv, nmat):
    m, r = v.shape
    face = m // 4
    step = 256

    def body(flags_ref, fr_ref, v_ref, a_ref, b_ref, c_ref, d_ref, n_ref, jump_ref, work_ref, hi, lo, fh, fl):
        i = pl.program_id(0)

        @pl.when(i == 0)
        def _():
            for k, ref in enumerate((a_ref, b_ref, c_ref, d_ref)):
                fh[k * face:(k + 1) * face], fl[k * face:(k + 1) * face] = halves(ref[...] * flags_ref[k])

            @pl.loop(0, m // step)
            def _(j):
                rows = pl.ds(pl.multiple_of(j * step, step), step)
                sb = scatter_block(fr_ref, j * step, step)
                jump = v_ref[rows, :] - (one_pass(sb, fh[...], NN) + one_pass(sb, fl[...], NN))
                jump_ref[rows, :] = jump
                hi[rows, :], lo[rows, :] = halves(jump)

        work_ref[...] = three(n_ref[...], (hi[...], lo[...]))

    whole = lambda shape: pl.BlockSpec(shape, lambda i: (0, 0), pipeline_mode=pl.Buffered(1))
    return call(
        body, [out(m, r), out(m, r)], [flags, fr, v, *recv, nmat], grid=(m // step,),
        in_specs=[pl.BlockSpec(memory_space=SMEM), whole(fr.shape), whole(v.shape)] + [whole((face, r))] * 4 + [pl.BlockSpec((step, m), lambda i: (i, 0))],
        out_specs=[whole((m, r)), pl.BlockSpec((step, r), lambda i: (i, 0))],
        scratch=[VMEM((m, r), BF16)] * 4, flops=10 * m * m * r, name="scatter_neumann",
    )


def dirichlet_gather(fr, work, jump, dmat, dptf, npr):
    m, r = work.shape
    face, p = m // 4, npr.shape[0]
    step = 256

    def body(fr_ref, w_ref, j_ref, d_ref, t_ref, n_ref, dw_ref, base_ref, a_ref, b_ref, c_ref, e_ref, np_ref, hi, lo, got):
        i = pl.program_id(0)

        @pl.when(i == 0)
        def _():
            hi[...], lo[...] = halves(w_ref[...])

        rows = pl.ds(pl.multiple_of(i * step, step), step)
        dw = three(d_ref[...], (hi[...], lo[...]))
        dw_ref[rows, :] = dw
        base_ref[rows, :] = j_ref[rows, :] - 0.5 * dw

        @pl.when(i == m // step - 1)
        def _():
            hi[...], lo[...] = halves(base_ref[...])

            @pl.loop(0, 4)
            def _(k):
                pb = perm_block(fr_ref, k * face, face)
                got[k] = one_pass(pb, hi[...], NN) + one_pass(pb, lo[...], NN)

            for k, ref in enumerate((a_ref, b_ref, c_ref, e_ref)):
                ref[:face] = got[k]
                ref[face:] = t_ref[:, k * face:(k + 1) * face]
            np_ref[...] = three(n_ref[...], (hi[...], lo[...]))

    whole = lambda shape: pl.BlockSpec(shape, lambda i: (0, 0), pipeline_mode=pl.Buffered(1))
    res = call(
        body, [out(m, r), out(m, r)] + [out(face + p, r)] * 4 + [out(p, r)], [fr, work, jump, dmat, dptf, npr], grid=(m // step,),
        in_specs=[whole(fr.shape), whole((m, r)), whole((m, r)), pl.BlockSpec((step, m), lambda i: (i, 0)), whole(dptf.shape), whole(npr.shape)],
        out_specs=[whole((m, r))] * 2 + [whole((face + p, r))] * 4 + [whole((p, r))],
        scratch=[VMEM((m, r), BF16)] * 2 + [VMEM((4, face, r), F32)], flops=10 * m * m * r, name="dirichlet_gather",
    )
    return res[0], res[1], res[2:6], res[6]


def first_cvec(flags, nprr, nprf, recv):
    p, r = nprr.shape
    face = recv[0].shape[0]

    def body(flags_ref, b_ref, n_ref, *refs):
        total = b_ref[...]
        for k in range(4):
            total = total - flags_ref[k] * three(n_ref[:, k * face:(k + 1) * face], refs[k][...])
        refs[4][...] = total

    return call(body, [out(p, r)], [flags, nprr, nprf, *recv], in_specs=[pl.BlockSpec(memory_space=SMEM)] + [pl.BlockSpec(memory_space=VMEM)] * 6,
                flops=6 * p * 4 * face * r, name="first_cvec")[0]


def coarse_product(core, cblk, blocks):
    width = cblk[0].shape[1]
    p, r = blocks[0].shape
    rows = NZ * p

    def body(core_ref, c0, c1, c2, c3, *refs):
        ins, outs, (hi, lo, ch, cl) = refs[:len(blocks)], refs[len(blocks):len(blocks) + NZ], refs[len(blocks) + NZ:]
        for k, ref in enumerate((c0, c1, c2, c3)):
            ch[k * p:(k + 1) * p], cl[k * p:(k + 1) * p] = halves(ref[...])
        second = core_ref[0] == 1
        for k in range(NY):
            a, b = halves(ins[2 * k][...]), halves(ins[2 * k + 1][...])
            for ref, u, w in zip((hi, lo), a, b):
                u, w = u.astype(F32), w.astype(F32)
                ref[2 * k * p:(2 * k + 1) * p] = jnp.where(second, w, u).astype(BF16)
                ref[(2 * k + 1) * p:(2 * k + 2) * p] = jnp.where(second, u, w).astype(BF16)
        total = three((ch[...], cl[...]), (hi[...], lo[...]))
        for k in range(NZ):
            outs[k][...] = total[k * p:(k + 1) * p]

    return call(body, [out(p, r)] * NZ, [core, *cblk, *blocks],
                in_specs=[pl.BlockSpec(memory_space=SMEM)] + [pl.BlockSpec(memory_space=VMEM)] * (NZ + len(blocks)),
                scratch=[VMEM((width, r), BF16)] * 2 + [VMEM((rows, width), BF16)] * 2, flops=6 * rows * width * r, name="coarse_product")


def couplings(flags, nprf, got, base_part, own):
    p, r = base_part.shape
    face = got[0].shape[0] - p

    def body(flags_ref, n_ref, b_ref, o_ref, *refs):
        total = b_ref[...]
        refs[5][0] = -0.5 * o_ref[...]
        for k in range(4):
            nk = halves(n_ref[:, k * face:(k + 1) * face])
            total = total - flags_ref[k] * three(nk, refs[k][:face])
            refs[5][k + 1] = (0.5 * flags_ref[k]) * three(nk, refs[k][face:], NT)
        refs[4][...] = total

    return call(body, [out(p, r), out(5, p, p)], [flags, nprf, base_part, own, *got],
                in_specs=[pl.BlockSpec(memory_space=SMEM)] + [pl.BlockSpec(memory_space=VMEM)] * 7,
                flops=6 * p * 4 * (face + p) * r, name="couplings")


def next_cvec(cbase, gmat, chains):
    p, r = cbase.shape

    def body(c_ref, g_ref, *refs):
        total = c_ref[...]
        for k in range(5):
            total = total + three(g_ref[k], refs[k][...])
        refs[5][...] = total

    return call(body, [out(p, r)], [cbase, gmat, *chains], flops=30 * p * p * r, name="next_cvec")[0]


def second_neumann(flags, fr, base, got, dpt, chains, nmat):
    m, r = base.shape
    p = dpt.shape[0]
    face = m // 4
    step = 256

    def body(flags_ref, fr_ref, v_ref, a_ref, b_ref, c_ref, d_ref, t_ref, own_ref, q0, q1, q2, q3, n_ref, jump_ref, dc_ref, work_ref, hi, lo, fh, fl):
        i = pl.program_id(0)

        @pl.when(i == 0)
        def _():
            for k, (ref, q) in enumerate(zip((a_ref, b_ref, c_ref, d_ref), (q0, q1, q2, q3))):
                got_k = ref[:face] - 0.5 * three(ref[face:], q[...], TN)
                fh[k * face:(k + 1) * face], fl[k * face:(k + 1) * face] = halves(got_k * flags_ref[k])
                rows = slice(k * face, (k + 1) * face)
                dc_ref[rows, :] = three(t_ref[:, rows], own_ref[...], TN)

            @pl.loop(0, m // step)
            def _(j):
                rows = pl.ds(pl.multiple_of(j * step, step), step)
                sb = scatter_block(fr_ref, j * step, step)
                jump = v_ref[rows, :] - 0.5 * dc_ref[rows, :] - (one_pass(sb, fh[...], NN) + one_pass(sb, fl[...], NN))
                jump_ref[rows, :] = jump
                hi[rows, :], lo[rows, :] = halves(jump)

        work_ref[...] = three(n_ref[...], (hi[...], lo[...]))

    whole = lambda shape: pl.BlockSpec(shape, lambda i: (0, 0), pipeline_mode=pl.Buffered(1))
    return call(
        body, [out(m, r)] * 3, [flags, fr, base, *got, dpt, *chains, nmat], grid=(m // step,),
        in_specs=[pl.BlockSpec(memory_space=SMEM), whole(fr.shape), whole(base.shape)] + [whole((face + p, r))] * 4 + [whole(dpt.shape)]
        + [whole((p, r))] * 5 + [pl.BlockSpec((step, m), lambda i: (i, 0))],
        out_specs=[whole((m, r)), whole((m, r)), pl.BlockSpec((step, r), lambda i: (i, 0))],
        scratch=[VMEM((m, r), BF16)] * 4, flops=11 * m * m * r, name="second_neumann",
    )


def second_dirichlet(work, jump, dw, dc, dmat):
    m, r = work.shape
    step = 256

    def body(w_ref, j_ref, p_ref, c_ref, d_ref, s_ref, r_ref, hi, lo):
        @pl.when(pl.program_id(0) == 0)
        def _():
            hi[...], lo[...] = halves(w_ref[...])

        dw1 = three(d_ref[...], (hi[...], lo[...]))
        s_ref[...] = p_ref[...] + c_ref[...] + dw1
        r_ref[...] = j_ref[...] - 0.5 * dw1

    blk = pl.BlockSpec((step, r), lambda i: (i, 0))
    return call(
        body, [out(m, r)] * 2, [work, jump, dw, dc, dmat], grid=(m // step,),
        in_specs=[pl.BlockSpec((m, r), lambda i: (0, 0), pipeline_mode=pl.Buffered(1)), blk, blk, blk, pl.BlockSpec((step, m), lambda i: (i, 0))],
        out_specs=[blk, blk], scratch=[VMEM((m, r), BF16)] * 2, flops=6 * m * m * r, name="second_dirichlet",
    )


def last_update(dpt, own, over, v, sol, res):
    p, m = dpt.shape
    r = own.shape[1]
    step = 256

    def body(t_ref, a_ref, o_ref, v_ref, s_ref, r_ref, so_ref, ro_ref, hi, lo):
        @pl.when(pl.program_id(0) == 0)
        def _():
            for k in range(r // 128):
                lanes = slice(k * 128, (k + 1) * 128)
                hi[:, lanes], lo[:, lanes] = halves(a_ref[:, lanes] + v_ref[0] * o_ref[:, lanes])

        u = three(t_ref[...], (hi[...], lo[...]), TN)
        so_ref[...] = s_ref[...] + u
        ro_ref[...] = r_ref[...] - 0.5 * u

    blk = pl.BlockSpec((step, r), lambda i: (i, 0))
    small = pl.BlockSpec((p, r), lambda i: (0, 0))
    return call(
        body, [out(m, r)] * 2, [dpt, own, over, v, sol, res], grid=(m // step,),
        in_specs=[pl.BlockSpec((p, step), lambda i: (0, i)), small, small, pl.BlockSpec(v.shape, lambda i: (0, 0, 0)), blk, blk],
        out_specs=[blk, blk], scratch=[VMEM((p, r), BF16)] * 2, flops=6 * m * p * r, name="last_update",
    )


def primal_rows(pr, nmat, fr, r0):
    m, r = r0.shape
    p = pr.shape[0]
    face = m // 4

    def body(pr_ref, n_ref, fr_ref, r_ref, rows_ref, moved_ref, prod_ref, group, sems):
        def fetch(i):
            return pltpu.make_async_copy(n_ref.at[pl.ds(pl.multiple_of(pr_ref[i] // 8 * 8, 8), 8), :], group.at[i], sems.at[i])

        @pl.loop(0, p)
        def _(i):
            fetch(i).start()

        @pl.loop(0, p)
        def _(i):
            fetch(i).wait()
            rows_ref[pl.ds(i, 1), :] = group[i, pl.ds(pr_ref[i] % 8, 1), :]

        both = halves(rows_ref[...])
        for k in range(4):
            cols = slice(k * face, (k + 1) * face)
            ids = lax.broadcasted_iota(jnp.int32, (m, face), 0)
            sb = (ids == fr_ref[:, cols]).astype(F32).astype(BF16)
            moved_ref[:, cols] = one_pass(both[0], sb, NN) + one_pass(both[1], sb, NN)
        prod_ref[...] = three(both, r_ref[...])

    return call(
        body, [out(p, m), out(p, m), out(p, r)], [pr, nmat, fr, r0],
        in_specs=[pl.BlockSpec(memory_space=SMEM), pl.BlockSpec(memory_space=pl.ANY)] + [pl.BlockSpec(memory_space=VMEM)] * 2,
        scratch=[VMEM((p, 8, m), F32), pltpu.SemaphoreType.DMA((p,))], flops=4 * p * m * m, name="primal_rows",
    )


def primal_columns(prow, dmat, fr, npr):
    m = dmat.shape[0]
    p = npr.shape[0]
    step = 256

    def body(pr_ref, d_ref, fr_ref, n_ref, t_ref, f_ref, g_ref, sel):
        i = pl.program_id(0)

        @pl.when(i == 0)
        def _():
            ids = jnp.transpose(jnp.broadcast_to(pr_ref[...].astype(F32), (128, 128)))[:p]
            lane = lax.broadcasted_iota(jnp.int32, (p, 128), 1).astype(F32)
            for k in range(m // 128):
                sel[:, k * 128:(k + 1) * 128] = (ids == lane + 128.0 * k).astype(F32).astype(BF16)

        dh, dl = halves(d_ref[...])
        t_ref[:, pl.ds(pl.multiple_of(i * step, step), step)] = one_pass(sel[...], dh, NT) + one_pass(sel[...], dl, NT)

        @pl.when(i == m // step - 1)
        def _():
            both = halves(t_ref[...])
            for k in range(m // step):
                cols = slice(k * step, (k + 1) * step)
                ids = lax.broadcasted_iota(jnp.int32, (m, step), 0)
                sb = (ids == fr_ref[:, cols]).astype(F32).astype(BF16)
                f_ref[:, cols] = one_pass(both[0], sb, NN) + one_pass(both[1], sb, NN)
            g_ref[...] = three(n_ref[...], both, NT)

    whole = lambda shape: pl.BlockSpec(shape, lambda i: (0, 0), pipeline_mode=pl.Buffered(1))
    return call(
        body, [out(p, m), out(p, m), out(p, p)], [prow, dmat, fr, npr], grid=(m // step,),
        in_specs=[whole(prow.shape), pl.BlockSpec((step, m), lambda i: (i, 0)), whole(fr.shape), whole(npr.shape)],
        out_specs=[whole((p, m)), whole((p, m)), whole((p, p))], scratch=[VMEM((p, m), BF16)], flops=8 * p * m * m, name="primal_columns",
    )


def coarse_cut(place, crow):
    p, total = crow.shape
    width = total // (NZ * NY)

    def body(place_ref, c_ref, *refs):
        z, y = place_ref[0], place_ref[1]
        for k in range(NZ):
            for j in range(NY):
                at = (lax.rem(z + NZ - k, NZ) * NY + lax.rem(y + j, NY)) * width
                refs[k][:, j * width:(j + 1) * width] = c_ref[:, pl.ds(pl.multiple_of(at, width), width)]

    return call(body, [out(p, NY * width)] * NZ, [place, crow],
                in_specs=[pl.BlockSpec(memory_space=SMEM), pl.BlockSpec(memory_space=VMEM)], name="coarse_cut")


def column(row, p):
    return jnp.transpose(jnp.broadcast_to(row, (128, 128)))[:p]


def sweep(ref, cols, loc, p, r):
    loc[0] = jnp.zeros((p, r), F32)
    for j in range(NX):
        for b in range(r // 128):
            lanes = slice(b * 128, (b + 1) * 128)
            loc[j + 1, :, lanes] = ref[j, :p, lanes] + cols[j] * loc[j, :, lanes]


def first_half(place, pieces, p):
    rows, r = pieces[0].shape

    def body(place_ref, a, b, c, d, send_ref, own_ref, low_ref, high_ref, v_ref, col_ref, q, loc, pv):
        h, x = place_ref[2], place_ref[3]
        for k, ref in enumerate((a, b, c, d)):
            q[lax.rem(x + k, NX)] = ref[...]
        pv[0] = jnp.ones((p, 128), F32)
        for j in range(NX):
            col_ref[j] = column(q[j, p:p + 1, :128], p)
            pv[j + 1] = pv[j] * col_ref[j]
        pv[NX + 1] = jnp.zeros((p, 128), F32)
        sweep(q, col_ref, loc, p, r)
        loc[NX + 1] = jnp.zeros((p, r), F32)
        upper = h == 1
        own_ref[...], low_ref[...], high_ref[...] = loc[x + 1], loc[x], loc[x + 2]
        for n, at in enumerate((x + 1, x, x + 2)):
            v_ref[n] = jnp.where(upper, pv[at], jnp.zeros((p, 128), F32))
        send_ref[:p] = jnp.where(upper, q[0, :p], loc[NX])
        send_ref[p:] = q[0, p:]

    return call(
        body, [out(rows, r)] + [out(p, r)] * 3 + [out(3, p, 128), out(NX, p, 128)], [place, *pieces],
        in_specs=[pl.BlockSpec(memory_space=SMEM)] + [pl.BlockSpec(memory_space=VMEM)] * 4,
        scratch=[VMEM((NX, rows, r), F32), VMEM((NX + 2, p, r), F32), VMEM((NX + 2, p, 128), F32)], name="first_half",
    )


def first_chains(place, over, own, low, high, v):
    p, r = own.shape

    def body(place_ref, over_ref, a, b, c, v_ref, ao, bo, co):
        last = jnp.logical_and(place_ref[2] == 0, place_ref[3] == NX - 1)
        rate = column(over_ref[p:p + 1, :128], p)
        for k in range(r // 128):
            lanes = slice(k * 128, (k + 1) * 128)
            came = over_ref[:p, lanes]
            ao[:, lanes] = a[:, lanes] + v_ref[0] * came
            bo[:, lanes] = b[:, lanes] + v_ref[1] * came
            co[:, lanes] = jnp.where(last, came + rate * a[:, lanes], c[:, lanes] + v_ref[2] * came)

    return call(body, [out(p, r)] * 3, [place, over, own, low, high, v],
                in_specs=[pl.BlockSpec(memory_space=SMEM)] + [pl.BlockSpec(memory_space=VMEM)] * 5, name="first_chains")


def second_half(place, pieces, cols):
    p, r = pieces[0].shape

    def body(place_ref, a, b, c, d, col_ref, send_ref, own_ref, q, loc):
        h, x = place_ref[2], place_ref[3]
        for k, ref in enumerate((a, b, c, d)):
            q[lax.rem(x + k, NX)] = ref[...]
        sweep(q, col_ref, loc, p, r)
        own_ref[...] = loc[x + 1]
        send_ref[...] = jnp.where(h == 1, q[0], loc[NX])

    return call(body, [out(p, r)] * 2, [place, *pieces, cols],
                in_specs=[pl.BlockSpec(memory_space=SMEM)] + [pl.BlockSpec(memory_space=VMEM)] * 5,
                scratch=[VMEM((NX, p, r), F32), VMEM((NX + 1, p, r), F32)], name="second_half")


def local(residual_in, neumann, dirichlet, coarse, decay, face_rows, primal):
    r0 = residual_in[0, 0]
    nmat = neumann[0, 0]
    dmat = dirichlet[0, 0]
    crow = coarse[0]
    dec = decay[0, 0]
    fr = face_rows[0]
    pr = primal[0, 0]
    m, r = r0.shape
    face = m // 4
    p = pr.shape[0]
    gx = lax.axis_index("gx")
    gy = lax.axis_index("gy")
    h, x = gx // NX, gx % NX
    z, y, c = gy // (NY * NC), (gy // NC) % NY, gy % NC
    flags = jnp.stack([gx > 0, gx < GX - 1, gy > 0, gy < GY - 1]).astype(F32)
    core = c.reshape(1).astype(jnp.int32)
    place = jnp.stack([z, y, h, x]).astype(jnp.int32)

    def exchange(blocks):
        return [ring(blocks[1], "gx", 1), ring(blocks[0], "gx", -1), ring(blocks[3], "gy", 1), ring(blocks[2], "gy", -1)]

    faces0 = gather_faces(fr, r0)
    recv0 = exchange(faces0)
    crow, pr_n = after((crow, pr), recv0[2:])
    cut = coarse_cut(place, crow)
    cblk = [cut[0]] + [pull_z(cut[k], k) for k in range(1, NZ)]
    pr_n = after(pr_n, cut)
    npr, nprf, nprr = primal_rows(pr_n, nmat, fr, r0)
    prow = jnp.pad(pr, (0, 128 - p))[None]
    dpt, dptf, g_own = primal_columns(prow, dmat, fr, npr)
    dec_rows = jnp.pad(dec[None], ((0, 7), (0, r - p)))

    def spread(cvec):
        return [cvec] + [pull_y(cvec, k) for k in range(1, NY)]

    def product(own, gate, blk):
        first = pull_core(own[0])
        rest = after(own[1:], *gate)
        own = [own[0]] + list(rest)
        twin = [first] + [pull_core(v) for v in rest]
        return coarse_product(core, blk, [b for pair in zip(own, twin) for b in pair])

    def summed(part):
        total = part[0]
        for k in range(1, NZ):
            total = total + pull_z(part[k], NZ - k)
        return total

    nprr = after(nprr, cblk)
    cvec0 = first_cvec(flags, nprr, nprf, recv0)
    own0 = spread(cvec0)
    recv_g, fr_g, dpt, dptf, g_own = after((recv0, fr, dpt, dptf, g_own), cvec0)
    jump0, work0 = scatter_neumann(flags, fr_g, r0, recv_g, nmat)
    part0 = product(own0, [work0], cblk)
    work_g = after(work0, part0)
    dw0, base, packed, base_part = dirichlet_gather(fr, work_g, jump0, dmat, dptf, npr)
    got = [ring(packed[1], "gx", 1), ring(packed[0], "gx", -1)]
    cq0 = jnp.concatenate([summed(part0), dec_rows], axis=0)
    cq0 = after(cq0, packed)
    pieces = [cq0] + [pull_x(cq0, k) for k in range(1, NX)]
    send, own, low, high, v, cols = first_half(place, pieces, p)
    later = after((packed[3], packed[2]), send)
    got += [ring(later[0], "gy", 1), ring(later[1], "gy", -1)]
    chain0, low, high = first_chains(place, pull_half(send), own, low, high, v)
    chains = [chain0, low, high, ring(chain0, "gy", 1), ring(chain0, "gy", -1)]
    cbase, gmat = couplings(flags, nprf, got, base_part, g_own)
    cvec1 = next_cvec(cbase, gmat, chains)

    own1 = spread(cvec1)
    fr_h = after(fr, cvec1)
    jump1, dc0, work1 = second_neumann(flags, fr_h, base, got, dpt, chains, nmat)
    part1 = product(own1, [work1], cblk)
    work1 = after(work1, part1)
    sol, res = second_dirichlet(work1, jump1, dw0, dc0, dmat)
    cq1 = after(summed(part1), res)
    pieces = [cq1] + [pull_x(cq1, k) for k in range(1, NX)]
    send, own = second_half(place, pieces, cols)
    solution, residual = last_update(dpt, own, pull_half(send), v, sol, res)
    return (solution[None, None], residual[None, None])


def solution(mesh):
    lead = P("gx", "gy", None, None)
    vec = P("gx", "gy", None)
    return jax.shard_map(
        local,
        mesh=mesh,
        in_specs=(lead, lead, lead, vec, vec, vec, vec),
        out_specs=(lead, lead),
        check_vma=False,
    )
```

```python
import functools

import jax
import jax.numpy as jnp
from jax import lax
from jax.experimental import pallas as pl
from jax.experimental.pallas import tpu as pltpu
from jax.sharding import PartitionSpec as P

NZ, NY, NC, NX, NH = 4, 4, 2, 4, 2
GY = NZ * NY * NC
GX = NX * NH
F32, BF16 = jnp.float32, jnp.bfloat16
COST = 1
VMEM, SMEM = pltpu.VMEM, pltpu.SMEM
NN, NT, TN = ((1,), (0,)), ((1,), (1,)), ((0,), (0,))


def gy_index(z, y, c):
    return (z * NY + y) * NC + c


def pull_y(v, k):
    return lax.ppermute(v, "gy", [(gy_index(z, (y + k) % NY, c), gy_index(z, y, c)) for z in range(NZ) for y in range(NY) for c in range(NC)])


def pull_z(v, k):
    return lax.ppermute(v, "gy", [(gy_index((z + k) % NZ, y, c), gy_index(z, y, c)) for z in range(NZ) for y in range(NY) for c in range(NC)])


def pull_core(v):
    return lax.ppermute(v, "gy", [(i, i ^ 1) for i in range(GY)])


def pull_x(v, k):
    return lax.ppermute(v, "gx", [(h * NX + (x + k) % NX, h * NX + x) for h in range(NH) for x in range(NX)])


def pull_half(v):
    return lax.ppermute(v, "gx", [(i, (i + NX) % GX) for i in range(GX)])


def ring(v, axis, by):
    n = GX if axis == "gx" else GY
    return lax.ppermute(v, axis, [(i, (i + by) % n) for i in range(n)])


def dot(a, b, dims=NN):
    return lax.dot_general(a, b, (dims, ((), ())), precision=lax.Precision.HIGH, preferred_element_type=F32)


def one_pass(a, b, dims):
    return lax.dot_general(a, b, (dims, ((), ())), preferred_element_type=F32)


def halves(v):
    hi = v.astype(BF16)
    return hi, (v - hi.astype(F32)).astype(BF16)


def three(a, b, dims=NN):
    ah, al = a if isinstance(a, tuple) else halves(a)
    bh, bl = b if isinstance(b, tuple) else halves(b)
    return one_pass(ah, bh, dims) + (one_pass(ah, bl, dims) + one_pass(al, bh, dims))


def after(values, *earlier):
    return lax.optimization_barrier((values, earlier))[0]


def call(body, outs, ins, *, grid=None, in_specs=None, out_specs=None, scratch=(), flops=0, name=None):
    whole = pl.BlockSpec(memory_space=VMEM)
    nbytes = sum(4 * v.size for v in ins) + sum(4 * o.size for o in outs)
    kwargs = {} if grid is None else {"grid": grid}
    return pl.pallas_call(
        body,
        out_shape=outs,
        in_specs=in_specs or [whole] * len(ins),
        out_specs=out_specs or [whole] * len(outs),
        scratch_shapes=list(scratch),
        compiler_params=pltpu.CompilerParams(vmem_limit_bytes=40 * 2**20),
        cost_estimate=pl.CostEstimate(flops=flops // COST, bytes_accessed=nbytes // COST, transcendentals=0),
        name=name,
        **kwargs,
    )(*ins)


def out(*shape):
    return jax.ShapeDtypeStruct(shape, F32)


def perm_block(fr_ref, at, face):
    m = fr_ref.shape[1]
    blocks = []
    for j in range(face // 128):
        ids = fr_ref[:, pl.ds(pl.multiple_of(at + j * 128, 128), 128)].astype(F32)
        ids = jnp.transpose(jnp.broadcast_to(ids, (128, 128)))
        lane = lax.broadcasted_iota(jnp.int32, (128, 128), 1).astype(F32)
        blocks.append(jnp.concatenate([(ids == lane + 128.0 * i).astype(F32).astype(BF16) for i in range(m // 128)], axis=1))
    return jnp.concatenate(blocks, axis=0)


def scatter_block(fr_ref, at, rows):
    m = fr_ref.shape[1]
    ids = lax.broadcasted_iota(jnp.int32, (rows, m), 0) + at
    return (ids == fr_ref[...]).astype(F32).astype(BF16)


def gather_faces(fr, v):
    m, r = v.shape
    face = m // 4

    def body(fr_ref, v_ref, *refs):
        outs, (hi, lo) = refs[:4], refs[4:]
        hi[...], lo[...] = halves(v_ref[...])
        for k in range(4):
            pb = perm_block(fr_ref, k * face, face)
            outs[k][...] = one_pass(pb, hi[...], NN) + one_pass(pb, lo[...], NN)

    return call(body, [out(face, r)] * 4, [fr, v], scratch=[VMEM((m, r), BF16)] * 2, flops=4 * m * m * r, name="gather_faces")


def scatter_neumann(flags, fr, v, recv, nmat):
    m, r = v.shape
    face = m // 4
    step = 256

    def body(flags_ref, fr_ref, v_ref, a_ref, b_ref, c_ref, d_ref, n_ref, jump_ref, work_ref, hi, lo, fh, fl):
        i = pl.program_id(0)

        @pl.when(i == 0)
        def _():
            for k, ref in enumerate((a_ref, b_ref, c_ref, d_ref)):
                fh[k * face:(k + 1) * face], fl[k * face:(k + 1) * face] = halves(ref[...] * flags_ref[k])

            @pl.loop(0, m // step)
            def _(j):
                rows = pl.ds(pl.multiple_of(j * step, step), step)
                sb = scatter_block(fr_ref, j * step, step)
                jump = v_ref[rows, :] - (one_pass(sb, fh[...], NN) + one_pass(sb, fl[...], NN))
                jump_ref[rows, :] = jump
                hi[rows, :], lo[rows, :] = halves(jump)

        work_ref[...] = three(n_ref[...], (hi[...], lo[...]))

    whole = lambda shape: pl.BlockSpec(shape, lambda i: (0, 0), pipeline_mode=pl.Buffered(1))
    return call(
        body, [out(m, r), out(m, r)], [flags, fr, v, *recv, nmat], grid=(m // step,),
        in_specs=[pl.BlockSpec(memory_space=SMEM), whole(fr.shape), whole(v.shape)] + [whole((face, r))] * 4 + [pl.BlockSpec((step, m), lambda i: (i, 0))],
        out_specs=[whole((m, r)), pl.BlockSpec((step, r), lambda i: (i, 0))],
        scratch=[VMEM((m, r), BF16)] * 4, flops=10 * m * m * r, name="scatter_neumann",
    )


def dirichlet_gather(fr, work, jump, dmat, npr):
    m, r = work.shape
    face, p = m // 4, npr.shape[0]
    step = 256

    def body(fr_ref, w_ref, j_ref, d_ref, n_ref, dw_ref, base_ref, a_ref, b_ref, c_ref, e_ref, np_ref, hi, lo):
        i = pl.program_id(0)

        @pl.when(i == 0)
        def _():
            hi[...], lo[...] = halves(w_ref[...])

        rows = pl.ds(pl.multiple_of(i * step, step), step)
        dw = three(d_ref[...], (hi[...], lo[...]))
        dw_ref[rows, :] = dw
        base_ref[rows, :] = j_ref[rows, :] - 0.5 * dw

        @pl.when(i == m // step - 1)
        def _():
            hi[...], lo[...] = halves(base_ref[...])
            for k, ref in enumerate((a_ref, b_ref, c_ref, e_ref)):
                pb = perm_block(fr_ref, k * face, face)
                ref[...] = one_pass(pb, hi[...], NN) + one_pass(pb, lo[...], NN)
            np_ref[...] = three(n_ref[...], (hi[...], lo[...]))

    whole = lambda shape: pl.BlockSpec(shape, lambda i: (0, 0), pipeline_mode=pl.Buffered(1))
    res = call(
        body, [out(m, r), out(m, r)] + [out(face, r)] * 4 + [out(p, r)], [fr, work, jump, dmat, npr], grid=(m // step,),
        in_specs=[whole(fr.shape), whole((m, r)), whole((m, r)), pl.BlockSpec((step, m), lambda i: (i, 0)), whole(npr.shape)],
        out_specs=[whole((m, r))] * 2 + [whole((face, r))] * 4 + [whole((p, r))],
        scratch=[VMEM((m, r), BF16)] * 2, flops=10 * m * m * r, name="dirichlet_gather",
    )
    return res[0], res[1], res[2:6], res[6]


def first_cvec(flags, nprr, nprf, recv):
    p, r = nprr.shape
    face = recv[0].shape[0]

    def body(flags_ref, b_ref, *refs):
        total = b_ref[...]
        for k in range(4):
            total = total - flags_ref[k] * three(refs[4 + k][...], refs[k][...])
        refs[8][...] = total

    return call(body, [out(p, r)], [flags, nprr, *recv, *nprf], in_specs=[pl.BlockSpec(memory_space=SMEM)] + [pl.BlockSpec(memory_space=VMEM)] * 9,
                flops=6 * p * 4 * face * r, name="first_cvec")[0]


def coarse_product(core, cblk, blocks):
    width = cblk[0].shape[1]
    p, r = blocks[0].shape
    rows = NZ * p

    def body(core_ref, c0, c1, c2, c3, *refs):
        ins, outs, (hi, lo, ch, cl) = refs[:len(blocks)], refs[len(blocks):len(blocks) + NZ], refs[len(blocks) + NZ:]
        for k, ref in enumerate((c0, c1, c2, c3)):
            ch[k * p:(k + 1) * p], cl[k * p:(k + 1) * p] = halves(ref[...])
        second = core_ref[0] == 1
        for k in range(NY):
            a, b = halves(ins[2 * k][...]), halves(ins[2 * k + 1][...])
            for ref, u, w in zip((hi, lo), a, b):
                u, w = u.astype(F32), w.astype(F32)
                ref[2 * k * p:(2 * k + 1) * p] = jnp.where(second, w, u).astype(BF16)
                ref[(2 * k + 1) * p:(2 * k + 2) * p] = jnp.where(second, u, w).astype(BF16)
        total = three((ch[...], cl[...]), (hi[...], lo[...]))
        for k in range(NZ):
            outs[k][...] = total[k * p:(k + 1) * p]

    return call(body, [out(p, r)] * NZ, [core, *cblk, *blocks],
                in_specs=[pl.BlockSpec(memory_space=SMEM)] + [pl.BlockSpec(memory_space=VMEM)] * (NZ + len(blocks)),
                scratch=[VMEM((width, r), BF16)] * 2 + [VMEM((rows, width), BF16)] * 2, flops=6 * rows * width * r, name="coarse_product")


def face_terms(asked, faces, dptf):
    p = asked[0].shape[0]
    face, r = faces[0].shape

    def body(t_ref, *refs):
        for k in range(4):
            ask = halves(refs[k][...])
            refs[8 + k][...] = three(ask, refs[4 + k][...])
            refs[12][k] = -0.5 * three(ask, t_ref[:, k * face:(k + 1) * face], NT)

    res = call(body, [out(p, r)] * 4 + [out(4, p, p)], [dptf, *asked, *faces], flops=24 * p * face * (r + p), name="face_terms")
    return res[:4], res[4]


def add_chain(terms, pairs, base_part, own, chain):
    p, r = chain.shape

    def body(pair_ref, b_ref, o_ref, c_ref, *refs):
        ch = halves(c_ref[...])
        for k in range(4):
            refs[4 + k][...] = refs[k][...] + three(pair_ref[k], ch)
        refs[8][...] = b_ref[...] - 0.5 * three(o_ref[...], ch)

    res = call(body, [out(p, r)] * 5, [pairs, base_part, own, chain, *terms], flops=30 * p * p * r, name="add_chain")
    return res[:4], res[4]


def sum_terms(flags, start, terms):
    p, r = start.shape

    def body(flags_ref, s_ref, *refs):
        total = s_ref[...]
        for k in range(4):
            total = total - flags_ref[k] * refs[k][...]
        refs[4][...] = total

    return call(body, [out(p, r)], [flags, start, *terms],
                in_specs=[pl.BlockSpec(memory_space=SMEM)] + [pl.BlockSpec(memory_space=VMEM)] * 5, name="sum_terms")[0]


def faces_with_chain(faces, dptf, chain):
    face, r = faces[0].shape

    def body(t_ref, c_ref, *refs):
        ch = halves(c_ref[...])
        for k in range(4):
            refs[4 + k][...] = refs[k][...] - 0.5 * three(halves(t_ref[:, k * face:(k + 1) * face]), ch, TN)

    return call(body, [out(face, r)] * 4, [dptf, chain, *faces], flops=24 * chain.shape[0] * face * r, name="faces_with_chain")


def residual_with_chain(base, dpt, chain):
    m, r = base.shape
    step = 256

    def body(b_ref, t_ref, c_ref, d_ref, o_ref):
        d = three(t_ref[...], c_ref[...], TN)
        d_ref[...] = d
        o_ref[...] = b_ref[...] - 0.5 * d

    blk = pl.BlockSpec((step, r), lambda i: (i, 0))
    return call(body, [out(m, r)] * 2, [base, dpt, chain], grid=(m // step,),
                in_specs=[blk, pl.BlockSpec((dpt.shape[0], step), lambda i: (0, i)), pl.BlockSpec(chain.shape, lambda i: (0, 0))],
                out_specs=[blk, blk], flops=6 * m * dpt.shape[0] * r, name="residual_with_chain")


def second_dirichlet(work, jump, dw, dc, dmat):
    m, r = work.shape
    step = 256

    def body(w_ref, j_ref, p_ref, c_ref, d_ref, s_ref, r_ref, hi, lo):
        @pl.when(pl.program_id(0) == 0)
        def _():
            hi[...], lo[...] = halves(w_ref[...])

        dw1 = three(d_ref[...], (hi[...], lo[...]))
        s_ref[...] = p_ref[...] + c_ref[...] + dw1
        r_ref[...] = j_ref[...] - 0.5 * dw1

    blk = pl.BlockSpec((step, r), lambda i: (i, 0))
    return call(
        body, [out(m, r)] * 2, [work, jump, dw, dc, dmat], grid=(m // step,),
        in_specs=[pl.BlockSpec((m, r), lambda i: (0, 0), pipeline_mode=pl.Buffered(1)), blk, blk, blk, pl.BlockSpec((step, m), lambda i: (i, 0))],
        out_specs=[blk, blk], scratch=[VMEM((m, r), BF16)] * 2, flops=6 * m * m * r, name="second_dirichlet",
    )


def last_update(dpt, own, over, v, sol, res):
    p, m = dpt.shape
    r = own.shape[1]
    step = 256

    def body(t_ref, a_ref, o_ref, v_ref, s_ref, r_ref, so_ref, ro_ref, hi, lo):
        @pl.when(pl.program_id(0) == 0)
        def _():
            for k in range(r // 128):
                lanes = slice(k * 128, (k + 1) * 128)
                hi[:, lanes], lo[:, lanes] = halves(a_ref[:, lanes] + v_ref[0] * o_ref[:, lanes])

        u = three(t_ref[...], (hi[...], lo[...]), TN)
        so_ref[...] = s_ref[...] + u
        ro_ref[...] = r_ref[...] - 0.5 * u

    blk = pl.BlockSpec((step, r), lambda i: (i, 0))
    small = pl.BlockSpec((p, r), lambda i: (0, 0))
    return call(
        body, [out(m, r)] * 2, [dpt, own, over, v, sol, res], grid=(m // step,),
        in_specs=[pl.BlockSpec((p, step), lambda i: (0, i)), small, small, pl.BlockSpec(v.shape, lambda i: (0, 0, 0)), blk, blk],
        out_specs=[blk, blk], scratch=[VMEM((p, r), BF16)] * 2, flops=6 * m * p * r, name="last_update",
    )


def one_hot_rows(pr_ref, sel, p, m):
    ids = jnp.transpose(jnp.broadcast_to(pr_ref[...].astype(F32), (128, 128)))[:p]
    lane = lax.broadcasted_iota(jnp.int32, (p, 128), 1).astype(F32)
    for k in range(m // 128):
        sel[:, k * 128:(k + 1) * 128] = (ids == lane + 128.0 * k).astype(F32).astype(BF16)


def primal_rows(prow, nmat, fr, r0, p):
    m, r = r0.shape
    face = m // 4
    step = 256

    def body(pr_ref, n_ref, fr_ref, r_ref, rows_ref, a_ref, b_ref, c_ref, d_ref, prod_ref, sel):
        i = pl.program_id(0)

        @pl.when(i == 0)
        def _():
            one_hot_rows(pr_ref, sel, p, m)
            rows_ref[...] = jnp.zeros((p, m), F32)

        nh, nl = halves(n_ref[...])
        pick = sel[:, pl.ds(pl.multiple_of(i * step, step), step)]
        rows_ref[...] += one_pass(pick, nh, NN) + one_pass(pick, nl, NN)

        @pl.when(i == m // step - 1)
        def _():
            both = halves(rows_ref[...])
            for k, ref in enumerate((a_ref, b_ref, c_ref, d_ref)):
                ids = lax.broadcasted_iota(jnp.int32, (m, face), 0)
                sb = (ids == fr_ref[:, k * face:(k + 1) * face]).astype(F32).astype(BF16)
                ref[...] = one_pass(both[0], sb, NN) + one_pass(both[1], sb, NN)
            prod_ref[...] = three(both, r_ref[...])

    whole = lambda shape: pl.BlockSpec(shape, lambda i: (0, 0), pipeline_mode=pl.Buffered(1))
    res = call(
        body, [out(p, m)] + [out(p, face)] * 4 + [out(p, r)], [prow, nmat, fr, r0], grid=(m // step,),
        in_specs=[whole(prow.shape), pl.BlockSpec((step, m), lambda i: (i, 0)), whole(fr.shape), whole(r0.shape)],
        out_specs=[whole((p, m))] + [whole((p, face))] * 4 + [whole((p, r))], scratch=[VMEM((p, m), BF16)],
        flops=8 * p * m * m, name="primal_rows",
    )
    return res[0], res[1:5], res[5]


def primal_columns(prow, dmat, fr, npr):
    m = dmat.shape[0]
    p = npr.shape[0]
    step = 256

    def body(pr_ref, d_ref, fr_ref, n_ref, t_ref, f_ref, g_ref, sel):
        i = pl.program_id(0)

        @pl.when(i == 0)
        def _():
            one_hot_rows(pr_ref, sel, p, m)

        dh, dl = halves(d_ref[...])
        t_ref[:, pl.ds(pl.multiple_of(i * step, step), step)] = one_pass(sel[...], dh, NT) + one_pass(sel[...], dl, NT)

        @pl.when(i == m // step - 1)
        def _():
            both = halves(t_ref[...])
            for k in range(m // step):
                cols = slice(k * step, (k + 1) * step)
                ids = lax.broadcasted_iota(jnp.int32, (m, step), 0)
                sb = (ids == fr_ref[:, cols]).astype(F32).astype(BF16)
                f_ref[:, cols] = one_pass(both[0], sb, NN) + one_pass(both[1], sb, NN)
            g_ref[...] = three(n_ref[...], both, NT)

    whole = lambda shape: pl.BlockSpec(shape, lambda i: (0, 0), pipeline_mode=pl.Buffered(1))
    return call(
        body, [out(p, m), out(p, m), out(p, p)], [prow, dmat, fr, npr], grid=(m // step,),
        in_specs=[whole(prow.shape), pl.BlockSpec((step, m), lambda i: (i, 0)), whole(fr.shape), whole(npr.shape)],
        out_specs=[whole((p, m)), whole((p, m)), whole((p, p))], scratch=[VMEM((p, m), BF16)], flops=8 * p * m * m, name="primal_columns",
    )


def coarse_cut(place, crow):
    p, total = crow.shape
    width = total // (NZ * NY)

    def body(place_ref, c_ref, *refs):
        z, y = place_ref[0], place_ref[1]
        for k in range(NZ):
            for j in range(NY):
                at = (lax.rem(z + NZ - k, NZ) * NY + lax.rem(y + j, NY)) * width
                refs[k][:, j * width:(j + 1) * width] = c_ref[:, pl.ds(pl.multiple_of(at, width), width)]

    return call(body, [out(p, NY * width)] * NZ, [place, crow],
                in_specs=[pl.BlockSpec(memory_space=SMEM), pl.BlockSpec(memory_space=VMEM)], name="coarse_cut")


def column(row, p):
    return jnp.transpose(jnp.broadcast_to(row, (128, 128)))[:p]


def sweep(ref, cols, loc, p, r):
    loc[0] = jnp.zeros((p, r), F32)
    for j in range(NX):
        for b in range(r // 128):
            lanes = slice(b * 128, (b + 1) * 128)
            loc[j + 1, :, lanes] = ref[j, :p, lanes] + cols[j] * loc[j, :, lanes]


def first_half(place, pieces, p):
    rows, r = pieces[0].shape

    def body(place_ref, a, b, c, d, send_ref, own_ref, v_ref, col_ref, q, loc, pv):
        h, x = place_ref[2], place_ref[3]
        for k, ref in enumerate((a, b, c, d)):
            q[lax.rem(x + k, NX)] = ref[...]
        pv[0] = jnp.ones((p, 128), F32)
        for j in range(NX):
            col_ref[j] = column(q[j, p:p + 1, :128], p)
            pv[j + 1] = pv[j] * col_ref[j]
        sweep(q, col_ref, loc, p, r)
        own_ref[...] = loc[x + 1]
        v_ref[0] = jnp.where(h == 1, pv[x + 1], jnp.zeros((p, 128), F32))
        send_ref[...] = loc[NX]

    return call(
        body, [out(p, r)] * 2 + [out(1, p, 128), out(NX, p, 128)], [place, *pieces],
        in_specs=[pl.BlockSpec(memory_space=SMEM)] + [pl.BlockSpec(memory_space=VMEM)] * 4,
        scratch=[VMEM((NX, rows, r), F32), VMEM((NX + 1, p, r), F32), VMEM((NX + 1, p, 128), F32)], name="first_half",
    )


def whole_chain(over, own, v):
    p, r = own.shape

    def body(over_ref, a, v_ref, o_ref):
        for k in range(r // 128):
            lanes = slice(k * 128, (k + 1) * 128)
            o_ref[:, lanes] = a[:, lanes] + v_ref[0] * over_ref[:, lanes]

    return call(body, [out(p, r)], [over, own, v], name="whole_chain")[0]


def second_half(place, pieces, cols):
    p, r = pieces[0].shape

    def body(place_ref, a, b, c, d, col_ref, send_ref, own_ref, q, loc):
        x = place_ref[3]
        for k, ref in enumerate((a, b, c, d)):
            q[lax.rem(x + k, NX)] = ref[...]
        sweep(q, col_ref, loc, p, r)
        own_ref[...] = loc[x + 1]
        send_ref[...] = loc[NX]

    return call(body, [out(p, r)] * 2, [place, *pieces, cols],
                in_specs=[pl.BlockSpec(memory_space=SMEM)] + [pl.BlockSpec(memory_space=VMEM)] * 5,
                scratch=[VMEM((NX, p, r), F32), VMEM((NX + 1, p, r), F32)], name="second_half")


def local(residual_in, neumann, dirichlet, coarse, decay, face_rows, primal):
    r0 = residual_in[0, 0]
    nmat = neumann[0, 0]
    dmat = dirichlet[0, 0]
    crow = coarse[0]
    dec = decay[0, 0]
    fr = face_rows[0]
    pr = primal[0, 0]
    m, r = r0.shape
    face = m // 4
    p = pr.shape[0]
    gx = lax.axis_index("gx")
    gy = lax.axis_index("gy")
    h, x = gx // NX, gx % NX
    z, y, c = gy // (NY * NC), (gy // NC) % NY, gy % NC
    flags = jnp.stack([gx > 0, gx < GX - 1, gy > 0, gy < GY - 1]).astype(F32)
    core = c.reshape(1).astype(jnp.int32)
    place = jnp.stack([z, y, h, x]).astype(jnp.int32)

    def exchange(blocks):
        return [ring(blocks[1], "gx", 1), ring(blocks[0], "gx", -1), ring(blocks[3], "gy", 1), ring(blocks[2], "gy", -1)]

    nmat = pltpu.with_memory_space_constraint(nmat, pltpu.HBM)
    dmat = pltpu.with_memory_space_constraint(dmat, pltpu.HBM)
    cut = coarse_cut(place, crow)
    fr = after(fr, cut)
    cblk = [cut[0]] + [pull_z(cut[k], k) for k in range(1, NZ)]
    faces0 = gather_faces(fr, r0)
    recv0 = exchange(faces0)
    prow = jnp.pad(pr, (0, 128 - p))[None]
    prow = after(prow, cblk)
    npr, nprf, nprr = primal_rows(prow, nmat, fr, r0, p)
    dpt, dptf, g_own = primal_columns(prow, dmat, fr, npr)
    dec_rows = jnp.pad(dec[None], ((0, 7), (0, r - p)))

    def spread(cvec):
        return [cvec] + [pull_y(cvec, k) for k in range(1, NY)]

    def product(own, gate, blk):
        first = pull_core(own[0])
        rest = after(own[1:], *gate)
        own = [own[0]] + list(rest)
        twin = [first] + [pull_core(v) for v in rest]
        return coarse_product(core, blk, [b for pair in zip(own, twin) for b in pair])

    def summed(part):
        total = part[0]
        for k in range(1, NZ):
            total = total + pull_z(part[k], NZ - k)
        return total

    cvec0 = first_cvec(flags, nprr, nprf, recv0)
    own0 = spread(cvec0)
    recv_g, fr_g, dpt, dptf, g_own, asks = after((recv0, fr, dpt, dptf, g_own, nprf), cvec0)
    jump0, work0 = scatter_neumann(flags, fr_g, r0, recv_g, nmat)
    part0 = product(own0, [work0], cblk)
    asked = [ring(asks[1], "gx", 1), ring(asks[0], "gx", -1)]
    work_g = after(work0, part0)
    dw0, base, faces1, base_part = dirichlet_gather(fr, work_g, jump0, dmat, npr)
    cq0 = jnp.concatenate([summed(part0), dec_rows], axis=0)
    cq0, asks = after((cq0, asks), faces1)
    pieces = [cq0] + [pull_x(cq0, k) for k in range(1, NX)]
    asked += [ring(asks[3], "gy", 1), ring(asks[2], "gy", -1)]
    send, own, v, cols = first_half(place, pieces, p)
    terms, pairs = face_terms(asked, faces1, dptf)
    chain0 = whole_chain(pull_half(send), own, v)
    terms, start = add_chain(terms, pairs, base_part, g_own, chain0)
    cvec1 = sum_terms(flags, start, exchange(terms))

    own1 = spread(cvec1)
    late = after((faces1, dptf, chain0), cvec1)
    faces1 = faces_with_chain(*late)
    recv1 = [ring(faces1[1], "gx", 1), ring(faces1[0], "gx", -1)]
    dc0, res1 = residual_with_chain(base, dpt, late[2])
    own1 = [after(own1[0], res1, faces1)] + own1[1:]
    part1 = product(own1, [res1, faces1], cblk)
    cq1 = summed(part1)
    pieces = [cq1] + [pull_x(cq1, k) for k in range(1, NX)]
    send, own = second_half(place, pieces, cols)
    late = after((faces1[3], faces1[2]), send)
    recv1 += [ring(late[0], "gy", 1), ring(late[1], "gy", -1)]
    jump1, work1 = scatter_neumann(flags, fr, res1, recv1, nmat)
    over = pull_half(send)
    work1 = after(work1, send)
    sol, res = second_dirichlet(work1, jump1, dw0, dc0, dmat)
    solution, residual = last_update(dpt, own, over, v, sol, res)
    return (solution[None, None], residual[None, None])


def solution(mesh):
    lead = P("gx", "gy", None, None)
    vec = P("gx", "gy", None)
    return jax.shard_map(
        local,
        mesh=mesh,
        in_specs=(lead, lead, lead, vec, vec, vec, vec),
        out_specs=(lead, lead),
        check_vma=False,
    )
```

```python
import math

import jax
import jax.numpy as jnp
from jax import lax
from jax.experimental import pallas as pl
from jax.experimental.pallas import tpu as pltpu
from jax.sharding import PartitionSpec as P

NZ, NY, NC, NX, NH = 4, 4, 2, 4, 2
GY = NZ * NY * NC
GX = NX * NH
F32, BF16 = jnp.float32, jnp.bfloat16
COST = 1
GRANT = 20 * 2**20
VMEM, SMEM = pltpu.VMEM, pltpu.SMEM
NN, NT, TN = ((1,), (0,)), ((1,), (1,)), ((0,), (0,))


def gy_index(z, y, c):
    return (z * NY + y) * NC + c


def pull_y(v, k):
    return lax.ppermute(v, "gy", [(gy_index(z, (y + k) % NY, c), gy_index(z, y, c)) for z in range(NZ) for y in range(NY) for c in range(NC)])


def pull_z(v, k):
    return lax.ppermute(v, "gy", [(gy_index((z + k) % NZ, y, c), gy_index(z, y, c)) for z in range(NZ) for y in range(NY) for c in range(NC)])


def pull_core(v):
    return lax.ppermute(v, "gy", [(i, i ^ 1) for i in range(GY)])


def pull_x(v, k):
    return lax.ppermute(v, "gx", [(h * NX + (x + k) % NX, h * NX + x) for h in range(NH) for x in range(NX)])


def pull_half(v):
    return lax.ppermute(v, "gx", [(i, (i + NX) % GX) for i in range(GX)])


def ring(v, axis, by):
    n = GX if axis == "gx" else GY
    return lax.ppermute(v, axis, [(i, (i + by) % n) for i in range(n)])


def dot(a, b, dims=NN):
    return lax.dot_general(a, b, (dims, ((), ())), precision=lax.Precision.HIGH, preferred_element_type=F32)


def one_pass(a, b, dims):
    return lax.dot_general(a, b, (dims, ((), ())), preferred_element_type=F32)


def halves(v):
    hi = v.astype(BF16)
    return hi, (v - hi.astype(F32)).astype(BF16)


def three(a, b, dims=NN):
    ah, al = a if isinstance(a, tuple) else halves(a)
    bh, bl = b if isinstance(b, tuple) else halves(b)
    return one_pass(ah, bh, dims) + (one_pass(ah, bl, dims) + one_pass(al, bh, dims))


def after(values, *earlier):
    return lax.optimization_barrier((values, earlier))[0]


def call(body, outs, ins, *, grid=None, in_specs=None, out_specs=None, scratch=(), flops=0, name=None):
    whole = pl.BlockSpec(memory_space=VMEM)
    nbytes = sum(4 * v.size for v in ins) + sum(4 * math.prod(o.shape) for o in outs)
    kwargs = {} if grid is None else {"grid": grid}
    return pl.pallas_call(
        body,
        out_shape=outs,
        in_specs=in_specs or [whole] * len(ins),
        out_specs=out_specs or [whole] * len(outs),
        scratch_shapes=list(scratch),
        compiler_params=pltpu.CompilerParams(vmem_limit_bytes=GRANT),
        cost_estimate=pl.CostEstimate(flops=flops // COST, bytes_accessed=nbytes // COST, transcendentals=0),
        name=name,
        **kwargs,
    )(*ins)


def in_hbm(v):
    return pltpu.with_memory_space_constraint(v, pltpu.HBM)


def out(*shape):
    return jax.ShapeDtypeStruct(shape, F32)


def perm_block(fr_ref, at, face):
    m = fr_ref.shape[1]
    blocks = []
    for j in range(face // 128):
        ids = fr_ref[:, pl.ds(pl.multiple_of(at + j * 128, 128), 128)].astype(F32)
        ids = jnp.transpose(jnp.broadcast_to(ids, (128, 128)))
        lane = lax.broadcasted_iota(jnp.int32, (128, 128), 1).astype(F32)
        blocks.append(jnp.concatenate([(ids == lane + 128.0 * i).astype(F32).astype(BF16) for i in range(m // 128)], axis=1))
    return jnp.concatenate(blocks, axis=0)


def scatter_block(fr_ref, at, rows):
    m = fr_ref.shape[1]
    ids = lax.broadcasted_iota(jnp.int32, (rows, m), 0) + at
    return (ids == fr_ref[...]).astype(F32).astype(BF16)


def gather_faces(fr, v):
    m, r = v.shape
    face = m // 4

    def body(fr_ref, v_ref, *refs):
        outs, (hi, lo) = refs[:4], refs[4:]
        hi[...], lo[...] = halves(v_ref[...])
        for k in range(4):
            pb = perm_block(fr_ref, k * face, face)
            outs[k][...] = one_pass(pb, hi[...], NN) + one_pass(pb, lo[...], NN)

    return call(body, [out(face, r)] * 4, [fr, v], scratch=[VMEM((m, r), BF16)] * 2, flops=4 * m * m * r, name="gather_faces")


def scatter_neumann(flags, fr, v, recv, nmat):
    m, r = v.shape
    face = m // 4
    step = 256

    def body(flags_ref, fr_ref, v_ref, a_ref, b_ref, c_ref, d_ref, n_ref, jump_ref, work_ref, hi, lo, fh, fl):
        i = pl.program_id(0)

        @pl.when(i == 0)
        def _():
            for k, ref in enumerate((a_ref, b_ref, c_ref, d_ref)):
                fh[k * face:(k + 1) * face], fl[k * face:(k + 1) * face] = halves(ref[...] * flags_ref[k])

            @pl.loop(0, m // step)
            def _(j):
                rows = pl.ds(pl.multiple_of(j * step, step), step)
                sb = scatter_block(fr_ref, j * step, step)
                jump = v_ref[rows, :] - (one_pass(sb, fh[...], NN) + one_pass(sb, fl[...], NN))
                jump_ref[rows, :] = jump
                hi[rows, :], lo[rows, :] = halves(jump)

        work_ref[...] = three(n_ref[...], (hi[...], lo[...]))

    whole = lambda shape: pl.BlockSpec(shape, lambda i: (0, 0), pipeline_mode=pl.Buffered(1))
    return call(
        body, [pltpu.HBM((m, r), F32)] * 2, [flags, fr, v, *recv, nmat], grid=(m // step,),
        in_specs=[pl.BlockSpec(memory_space=SMEM), whole(fr.shape), whole(v.shape)] + [whole((face, r))] * 4 + [pl.BlockSpec((step, m), lambda i: (i, 0))],
        out_specs=[whole((m, r)), pl.BlockSpec((step, r), lambda i: (i, 0))],
        scratch=[VMEM((m, r), BF16)] * 4, flops=10 * m * m * r, name="scatter_neumann",
    )


def dirichlet_gather(fr, work, jump, dmat, npr):
    m, r = work.shape
    face, p = m // 4, npr.shape[0]
    step = 256

    def body(fr_ref, w_ref, j_ref, d_ref, n_ref, dw_ref, base_ref, a_ref, b_ref, c_ref, e_ref, np_ref, hi, lo):
        i = pl.program_id(0)

        @pl.when(i == 0)
        def _():
            hi[...], lo[...] = halves(w_ref[...])

        rows = pl.ds(pl.multiple_of(i * step, step), step)
        dw = three(d_ref[...], (hi[...], lo[...]))
        dw_ref[rows, :] = dw
        base_ref[rows, :] = j_ref[...] - 0.5 * dw

        @pl.when(i == m // step - 1)
        def _():
            hi[...], lo[...] = halves(base_ref[...])
            for k, ref in enumerate((a_ref, b_ref, c_ref, e_ref)):
                pb = perm_block(fr_ref, k * face, face)
                ref[...] = one_pass(pb, hi[...], NN) + one_pass(pb, lo[...], NN)
            np_ref[...] = three(n_ref[...], (hi[...], lo[...]))

    whole = lambda shape: pl.BlockSpec(shape, lambda i: (0, 0), pipeline_mode=pl.Buffered(1))
    res = call(
        body, [out(m, r), out(m, r)] + [out(face, r)] * 4 + [out(p, r)], [fr, in_hbm(work), in_hbm(jump), dmat, npr], grid=(m // step,),
        in_specs=[whole(fr.shape), whole((m, r)), pl.BlockSpec((step, r), lambda i: (i, 0)), pl.BlockSpec((step, m), lambda i: (i, 0)), whole(npr.shape)],
        out_specs=[whole((m, r))] * 2 + [whole((face, r))] * 4 + [whole((p, r))],
        scratch=[VMEM((m, r), BF16)] * 2, flops=10 * m * m * r, name="dirichlet_gather",
    )
    return res[0], res[1], res[2:6], res[6]


def first_cvec(flags, nprr, nprf, recv):
    p, r = nprr.shape
    face = recv[0].shape[0]

    def body(flags_ref, b_ref, *refs):
        total = b_ref[...]
        for k in range(4):
            total = total - flags_ref[k] * three(refs[4 + k][...], refs[k][...])
        refs[8][...] = total

    return call(body, [out(p, r)], [flags, nprr, *recv, *nprf], in_specs=[pl.BlockSpec(memory_space=SMEM)] + [pl.BlockSpec(memory_space=VMEM)] * 9,
                flops=6 * p * 4 * face * r, name="first_cvec")[0]


def coarse_product(core, cblk, blocks):
    width = cblk[0].shape[1]
    p, r = blocks[0].shape
    rows = NZ * p

    def body(core_ref, c0, c1, c2, c3, *refs):
        ins, outs, (hi, lo, ch, cl) = refs[:len(blocks)], refs[len(blocks):len(blocks) + NZ], refs[len(blocks) + NZ:]
        for k, ref in enumerate((c0, c1, c2, c3)):
            ch[k * p:(k + 1) * p], cl[k * p:(k + 1) * p] = halves(ref[...])
        second = core_ref[0] == 1
        for k in range(NY):
            a, b = halves(ins[2 * k][...]), halves(ins[2 * k + 1][...])
            for ref, u, w in zip((hi, lo), a, b):
                u, w = u.astype(F32), w.astype(F32)
                ref[2 * k * p:(2 * k + 1) * p] = jnp.where(second, w, u).astype(BF16)
                ref[(2 * k + 1) * p:(2 * k + 2) * p] = jnp.where(second, u, w).astype(BF16)
        total = three((ch[...], cl[...]), (hi[...], lo[...]))
        for k in range(NZ):
            outs[k][...] = total[k * p:(k + 1) * p]

    return call(body, [out(p, r)] * NZ, [core, *cblk, *blocks],
                in_specs=[pl.BlockSpec(memory_space=SMEM)] + [pl.BlockSpec(memory_space=VMEM)] * (NZ + len(blocks)),
                scratch=[VMEM((width, r), BF16)] * 2 + [VMEM((rows, width), BF16)] * 2, flops=6 * rows * width * r, name="coarse_product")


def face_terms(asked, faces, dptf):
    p = asked[0].shape[0]
    face, r = faces[0].shape

    def body(t_ref, *refs):
        for k in range(4):
            ask = halves(refs[k][...])
            refs[8 + k][...] = three(ask, refs[4 + k][...])
            refs[12][k] = -0.5 * three(ask, t_ref[:, k * face:(k + 1) * face], NT)

    res = call(body, [out(p, r)] * 4 + [out(4, p, p)], [dptf, *asked, *faces], flops=24 * p * face * (r + p), name="face_terms")
    return res[:4], res[4]


def add_chain(terms, pairs, base_part, own, chain):
    p, r = chain.shape

    def body(pair_ref, b_ref, o_ref, c_ref, *refs):
        ch = halves(c_ref[...])
        for k in range(4):
            refs[4 + k][...] = refs[k][...] + three(pair_ref[k], ch)
        refs[8][...] = b_ref[...] - 0.5 * three(o_ref[...], ch)

    res = call(body, [out(p, r)] * 5, [pairs, base_part, own, chain, *terms], flops=30 * p * p * r, name="add_chain")
    return res[:4], res[4]


def sum_terms(flags, start, terms):
    p, r = start.shape

    def body(flags_ref, s_ref, *refs):
        total = s_ref[...]
        for k in range(4):
            total = total - flags_ref[k] * refs[k][...]
        refs[4][...] = total

    return call(body, [out(p, r)], [flags, start, *terms],
                in_specs=[pl.BlockSpec(memory_space=SMEM)] + [pl.BlockSpec(memory_space=VMEM)] * 5, name="sum_terms")[0]


def faces_with_chain(faces, dptf, chain):
    face, r = faces[0].shape

    def body(t_ref, c_ref, *refs):
        ch = halves(c_ref[...])
        for k in range(4):
            refs[4 + k][...] = refs[k][...] - 0.5 * three(halves(t_ref[:, k * face:(k + 1) * face]), ch, TN)

    return call(body, [out(face, r)] * 4, [dptf, chain, *faces], flops=24 * chain.shape[0] * face * r, name="faces_with_chain")


def residual_with_chain(base, dpt, chain):
    m, r = base.shape
    step = 256

    def body(b_ref, t_ref, c_ref, d_ref, o_ref):
        d = three(t_ref[...], c_ref[...], TN)
        d_ref[...] = d
        o_ref[...] = b_ref[...] - 0.5 * d

    blk = pl.BlockSpec((step, r), lambda i: (i, 0))
    return call(body, [out(m, r)] * 2, [base, dpt, chain], grid=(m // step,),
                in_specs=[blk, pl.BlockSpec((dpt.shape[0], step), lambda i: (0, i)), pl.BlockSpec(chain.shape, lambda i: (0, 0))],
                out_specs=[blk, blk], flops=6 * m * dpt.shape[0] * r, name="residual_with_chain")


def second_dirichlet(work, jump, dw, dc, dmat):
    m, r = work.shape
    step = 256

    def body(w_ref, j_ref, p_ref, c_ref, d_ref, s_ref, r_ref, hi, lo):
        @pl.when(pl.program_id(0) == 0)
        def _():
            hi[...], lo[...] = halves(w_ref[...])

        dw1 = three(d_ref[...], (hi[...], lo[...]))
        s_ref[...] = p_ref[...] + c_ref[...] + dw1
        r_ref[...] = j_ref[...] - 0.5 * dw1

    blk = pl.BlockSpec((step, r), lambda i: (i, 0))
    return call(
        body, [out(m, r)] * 2, [in_hbm(work), in_hbm(jump), dw, dc, dmat], grid=(m // step,),
        in_specs=[pl.BlockSpec((m, r), lambda i: (0, 0), pipeline_mode=pl.Buffered(1)), blk, blk, blk, pl.BlockSpec((step, m), lambda i: (i, 0))],
        out_specs=[blk, blk], scratch=[VMEM((m, r), BF16)] * 2, flops=6 * m * m * r, name="second_dirichlet",
    )


def last_update(dpt, own, over, v, sol, res):
    p, m = dpt.shape
    r = own.shape[1]
    step = 256

    def body(t_ref, a_ref, o_ref, v_ref, s_ref, r_ref, so_ref, ro_ref, hi, lo):
        @pl.when(pl.program_id(0) == 0)
        def _():
            for k in range(r // 128):
                lanes = slice(k * 128, (k + 1) * 128)
                hi[:, lanes], lo[:, lanes] = halves(a_ref[:, lanes] + v_ref[0] * o_ref[:, lanes])

        u = three(t_ref[...], (hi[...], lo[...]), TN)
        so_ref[...] = s_ref[...] + u
        ro_ref[...] = r_ref[...] - 0.5 * u

    blk = pl.BlockSpec((step, r), lambda i: (i, 0))
    small = pl.BlockSpec((p, r), lambda i: (0, 0))
    return call(
        body, [out(m, r)] * 2, [dpt, own, over, v, sol, res], grid=(m // step,),
        in_specs=[pl.BlockSpec((p, step), lambda i: (0, i)), small, small, pl.BlockSpec(v.shape, lambda i: (0, 0, 0)), blk, blk],
        out_specs=[blk, blk], scratch=[VMEM((p, r), BF16)] * 2, flops=6 * m * p * r, name="last_update",
    )


def one_hot_rows(pr_ref, sel, p, m):
    ids = jnp.transpose(jnp.broadcast_to(pr_ref[...].astype(F32), (128, 128)))[:p]
    lane = lax.broadcasted_iota(jnp.int32, (p, 128), 1).astype(F32)
    for k in range(m // 128):
        sel[:, k * 128:(k + 1) * 128] = (ids == lane + 128.0 * k).astype(F32).astype(BF16)


def primal_rows(prow, nmat, fr, r0, p):
    m, r = r0.shape
    face = m // 4
    step = 256

    def body(pr_ref, n_ref, fr_ref, r_ref, rows_ref, a_ref, b_ref, c_ref, d_ref, prod_ref, sel):
        i = pl.program_id(0)

        @pl.when(i == 0)
        def _():
            one_hot_rows(pr_ref, sel, p, m)
            rows_ref[...] = jnp.zeros((p, m), F32)

        nh, nl = halves(n_ref[...])
        pick = sel[:, pl.ds(pl.multiple_of(i * step, step), step)]
        rows_ref[...] += one_pass(pick, nh, NN) + one_pass(pick, nl, NN)

        @pl.when(i == m // step - 1)
        def _():
            both = halves(rows_ref[...])
            for k, ref in enumerate((a_ref, b_ref, c_ref, d_ref)):
                ids = lax.broadcasted_iota(jnp.int32, (m, face), 0)
                sb = (ids == fr_ref[:, k * face:(k + 1) * face]).astype(F32).astype(BF16)
                ref[...] = one_pass(both[0], sb, NN) + one_pass(both[1], sb, NN)
            prod_ref[...] = three(both, r_ref[...])

    whole = lambda shape: pl.BlockSpec(shape, lambda i: (0, 0), pipeline_mode=pl.Buffered(1))
    res = call(
        body, [out(p, m)] + [out(p, face)] * 4 + [out(p, r)], [prow, nmat, fr, r0], grid=(m // step,),
        in_specs=[whole(prow.shape), pl.BlockSpec((step, m), lambda i: (i, 0)), whole(fr.shape), whole(r0.shape)],
        out_specs=[whole((p, m))] + [whole((p, face))] * 4 + [whole((p, r))], scratch=[VMEM((p, m), BF16)],
        flops=8 * p * m * m, name="primal_rows",
    )
    return res[0], res[1:5], res[5]


def primal_columns(prow, dmat, fr, npr):
    m = dmat.shape[0]
    p = npr.shape[0]
    step = 256

    def body(pr_ref, d_ref, fr_ref, n_ref, t_ref, f_ref, g_ref, sel):
        i = pl.program_id(0)

        @pl.when(i == 0)
        def _():
            one_hot_rows(pr_ref, sel, p, m)

        dh, dl = halves(d_ref[...])
        t_ref[:, pl.ds(pl.multiple_of(i * step, step), step)] = one_pass(sel[...], dh, NT) + one_pass(sel[...], dl, NT)

        @pl.when(i == m // step - 1)
        def _():
            both = halves(t_ref[...])
            for k in range(m // step):
                cols = slice(k * step, (k + 1) * step)
                ids = lax.broadcasted_iota(jnp.int32, (m, step), 0)
                sb = (ids == fr_ref[:, cols]).astype(F32).astype(BF16)
                f_ref[:, cols] = one_pass(both[0], sb, NN) + one_pass(both[1], sb, NN)
            g_ref[...] = three(n_ref[...], both, NT)

    whole = lambda shape: pl.BlockSpec(shape, lambda i: (0, 0), pipeline_mode=pl.Buffered(1))
    return call(
        body, [out(p, m), out(p, m), out(p, p)], [prow, dmat, fr, npr], grid=(m // step,),
        in_specs=[whole(prow.shape), pl.BlockSpec((step, m), lambda i: (i, 0)), whole(fr.shape), whole(npr.shape)],
        out_specs=[whole((p, m)), whole((p, m)), whole((p, p))], scratch=[VMEM((p, m), BF16)], flops=8 * p * m * m, name="primal_columns",
    )


def coarse_cut(place, crow):
    p, total = crow.shape
    width = total // (NZ * NY)

    def body(place_ref, c_ref, *refs):
        z, y = place_ref[0], place_ref[1]
        for k in range(NY):
            for j in range(NZ):
                at = (lax.rem(z + j, NZ) * NY + lax.rem(y + NY - k, NY)) * width
                refs[k][:, j * width:(j + 1) * width] = c_ref[:, pl.ds(pl.multiple_of(at, width), width)]

    return call(body, [out(p, NZ * width)] * NY, [place, crow],
                in_specs=[pl.BlockSpec(memory_space=SMEM), pl.BlockSpec(memory_space=VMEM)], name="coarse_cut")


def column(row, p):
    return jnp.transpose(jnp.broadcast_to(row, (128, 128)))[:p]


def sweep(ref, cols, loc, p, r):
    loc[0] = jnp.zeros((p, r), F32)
    for j in range(NX):
        for b in range(r // 128):
            lanes = slice(b * 128, (b + 1) * 128)
            loc[j + 1, :, lanes] = ref[j, :p, lanes] + cols[j] * loc[j, :, lanes]


def first_half(place, pieces, p):
    rows, r = pieces[0].shape

    def body(place_ref, a, b, c, d, send_ref, own_ref, v_ref, col_ref, q, loc, pv):
        h, x = place_ref[2], place_ref[3]
        for k, ref in enumerate((a, b, c, d)):
            q[lax.rem(x + k, NX)] = ref[...]
        pv[0] = jnp.ones((p, 128), F32)
        for j in range(NX):
            col_ref[j] = column(q[j, p:p + 1, :128], p)
            pv[j + 1] = pv[j] * col_ref[j]
        sweep(q, col_ref, loc, p, r)
        own_ref[...] = loc[x + 1]
        v_ref[0] = jnp.where(h == 1, pv[x + 1], jnp.zeros((p, 128), F32))
        send_ref[...] = loc[NX]

    return call(
        body, [out(p, r)] * 2 + [out(1, p, 128), out(NX, p, 128)], [place, *pieces],
        in_specs=[pl.BlockSpec(memory_space=SMEM)] + [pl.BlockSpec(memory_space=VMEM)] * 4,
        scratch=[VMEM((NX, rows, r), F32), VMEM((NX + 1, p, r), F32), VMEM((NX + 1, p, 128), F32)], name="first_half",
    )


def whole_chain(over, own, v):
    p, r = own.shape

    def body(over_ref, a, v_ref, o_ref):
        for k in range(r // 128):
            lanes = slice(k * 128, (k + 1) * 128)
            o_ref[:, lanes] = a[:, lanes] + v_ref[0] * over_ref[:, lanes]

    return call(body, [out(p, r)], [over, own, v], name="whole_chain")[0]


def second_half(place, pieces, cols):
    p, r = pieces[0].shape

    def body(place_ref, a, b, c, d, col_ref, send_ref, own_ref, q, loc):
        x = place_ref[3]
        for k, ref in enumerate((a, b, c, d)):
            q[lax.rem(x + k, NX)] = ref[...]
        sweep(q, col_ref, loc, p, r)
        own_ref[...] = loc[x + 1]
        send_ref[...] = loc[NX]

    return call(body, [out(p, r)] * 2, [place, *pieces, cols],
                in_specs=[pl.BlockSpec(memory_space=SMEM)] + [pl.BlockSpec(memory_space=VMEM)] * 5,
                scratch=[VMEM((NX, p, r), F32), VMEM((NX + 1, p, r), F32)], name="second_half")


def local(residual_in, neumann, dirichlet, coarse, decay, face_rows, primal):
    r0 = residual_in[0, 0]
    nmat = neumann[0, 0]
    dmat = dirichlet[0, 0]
    crow = coarse[0]
    dec = decay[0, 0]
    fr = face_rows[0]
    pr = primal[0, 0]
    m, r = r0.shape
    face = m // 4
    p = pr.shape[0]
    gx = lax.axis_index("gx")
    gy = lax.axis_index("gy")
    h, x = gx // NX, gx % NX
    z, y, c = gy // (NY * NC), (gy // NC) % NY, gy % NC
    flags = jnp.stack([gx > 0, gx < GX - 1, gy > 0, gy < GY - 1]).astype(F32)
    core = c.reshape(1).astype(jnp.int32)
    place = jnp.stack([z, y, h, x]).astype(jnp.int32)

    def exchange(blocks):
        return [ring(blocks[1], "gx", 1), ring(blocks[0], "gx", -1), ring(blocks[3], "gy", 1), ring(blocks[2], "gy", -1)]

    cut = coarse_cut(place, crow)
    fr = after(fr, cut)
    cblk = [cut[0]] + [pull_y(cut[k], k) for k in range(1, NY)]
    faces0 = gather_faces(fr, r0)
    recv0 = exchange(faces0)
    prow = jnp.pad(pr, (0, 128 - p))[None]
    prow = after(prow, cblk)
    npr, nprf, nprr = primal_rows(prow, nmat, fr, r0, p)
    dpt, dptf, g_own = primal_columns(prow, dmat, fr, npr)
    dec_rows = jnp.pad(dec[None], ((0, 7), (0, r - p)))

    def spread(cvec):
        return [cvec] + [pull_z(cvec, k) for k in range(1, NZ)]

    def product(own, gate, blk):
        own = after(own, *gate)
        twin = [pull_core(v) for v in own]
        return coarse_product(core, blk, [b for pair in zip(own, twin) for b in pair])

    def summed(part):
        total = part[0]
        for k in range(1, NY):
            total = total + pull_y(part[k], NY - k)
        return total

    cvec0 = first_cvec(flags, nprr, nprf, recv0)
    own0 = spread(cvec0)
    recv_g, fr_g, dpt, dptf, g_own, asks = after((recv0, fr, dpt, dptf, g_own, nprf), cvec0)
    jump0, work0 = scatter_neumann(flags, fr_g, r0, recv_g, nmat)
    asked = [ring(asks[3], "gy", 1), ring(asks[2], "gy", -1)]
    part0 = product(own0, [work0], after(cblk, asked))
    work_g, asks = after((work0, asks), part0)
    asked = [ring(asks[1], "gx", 1), ring(asks[0], "gx", -1)] + asked
    dw0, base, faces1, base_part = dirichlet_gather(fr, work_g, jump0, dmat, npr)
    cq0 = jnp.concatenate([summed(part0), dec_rows], axis=0)
    cq0 = after(cq0, faces1)
    pieces = [cq0] + [pull_x(cq0, k) for k in range(1, NX)]
    send, own, v, cols = first_half(place, pieces, p)
    terms, pairs = face_terms(asked, faces1, dptf)
    chain0 = whole_chain(pull_half(send), own, v)
    terms, start = add_chain(terms, pairs, base_part, g_own, chain0)
    cvec1 = sum_terms(flags, start, exchange(terms))

    own1 = spread(cvec1)
    late = after((faces1, dptf, chain0), cvec1)
    faces1 = faces_with_chain(*late)
    recv_y = [ring(faces1[3], "gy", 1), ring(faces1[2], "gy", -1)]
    dc0, res1 = residual_with_chain(base, dpt, late[2])
    part1 = product(own1, [res1], after(cblk, recv_y))
    late = after((faces1[1], faces1[0]), part1)
    recv_x = [ring(late[0], "gx", 1), ring(late[1], "gx", -1)]
    recv1 = recv_x + recv_y
    cq1 = summed(part1)
    pieces = [cq1] + [pull_x(cq1, k) for k in range(1, NX)]
    send, own = second_half(place, pieces, after(cols, recv_x))
    jump1, work1 = scatter_neumann(flags, fr, res1, after(recv1, send), nmat)
    over = pull_half(send)
    work1 = after(work1, send)
    sol, res = second_dirichlet(work1, jump1, dw0, dc0, dmat)
    solution, residual = last_update(dpt, own, over, v, sol, res)
    return (solution[None, None], residual[None, None])


def solution(mesh):
    lead = P("gx", "gy", None, None)
    vec = P("gx", "gy", None)
    return jax.shard_map(
        local,
        mesh=mesh,
        in_specs=(lead, lead, lead, vec, vec, vec, vec),
        out_specs=(lead, lead),
        check_vma=False,
    )
```

```python
import math

import jax
import jax.numpy as jnp
from jax import lax
from jax.experimental import pallas as pl
from jax.experimental.pallas import tpu as pltpu
from jax.sharding import PartitionSpec as P

NZ, NY, NC, NX, NH = 4, 4, 2, 4, 2
GY = NZ * NY * NC
GX = NX * NH
F32, BF16 = jnp.float32, jnp.bfloat16
COST = 1
GRANT = 20 * 2**20
VMEM, SMEM = pltpu.VMEM, pltpu.SMEM
NN, NT, TN = ((1,), (0,)), ((1,), (1,)), ((0,), (0,))


def gy_index(z, y, c):
    return (z * NY + y) * NC + c


def pull_y(v, k):
    return lax.ppermute(v, "gy", [(gy_index(z, (y + k) % NY, c), gy_index(z, y, c)) for z in range(NZ) for y in range(NY) for c in range(NC)])


def pull_z(v, k):
    return lax.ppermute(v, "gy", [(gy_index((z + k) % NZ, y, c), gy_index(z, y, c)) for z in range(NZ) for y in range(NY) for c in range(NC)])


def pull_core(v):
    return lax.ppermute(v, "gy", [(i, i ^ 1) for i in range(GY)])


def pull_x(v, k):
    return lax.ppermute(v, "gx", [(h * NX + (x + k) % NX, h * NX + x) for h in range(NH) for x in range(NX)])


def pull_half(v):
    return lax.ppermute(v, "gx", [(i, (i + NX) % GX) for i in range(GX)])


def ring(v, axis, by):
    n = GX if axis == "gx" else GY
    return lax.ppermute(v, axis, [(i, (i + by) % n) for i in range(n)])


def dot(a, b, dims=NN):
    return lax.dot_general(a, b, (dims, ((), ())), precision=lax.Precision.HIGH, preferred_element_type=F32)


def one_pass(a, b, dims):
    return lax.dot_general(a, b, (dims, ((), ())), preferred_element_type=F32)


def halves(v):
    hi = v.astype(BF16)
    return hi, (v - hi.astype(F32)).astype(BF16)


def three(a, b, dims=NN):
    ah, al = a if isinstance(a, tuple) else halves(a)
    bh, bl = b if isinstance(b, tuple) else halves(b)
    return one_pass(ah, bh, dims) + (one_pass(ah, bl, dims) + one_pass(al, bh, dims))


def after(values, *earlier):
    return lax.optimization_barrier((values, earlier))[0]


def call(body, outs, ins, *, grid=None, in_specs=None, out_specs=None, scratch=(), flops=0, name=None):
    whole = pl.BlockSpec(memory_space=VMEM)
    nbytes = sum(4 * v.size for v in ins) + sum(4 * math.prod(o.shape) for o in outs)
    kwargs = {} if grid is None else {"grid": grid}
    return pl.pallas_call(
        body,
        out_shape=outs,
        in_specs=in_specs or [whole] * len(ins),
        out_specs=out_specs or [whole] * len(outs),
        scratch_shapes=list(scratch),
        compiler_params=pltpu.CompilerParams(vmem_limit_bytes=GRANT),
        cost_estimate=pl.CostEstimate(flops=flops // COST, bytes_accessed=nbytes // COST, transcendentals=0),
        name=name,
        **kwargs,
    )(*ins)


def in_hbm(v):
    return pltpu.with_memory_space_constraint(v, pltpu.HBM)


def out(*shape):
    return jax.ShapeDtypeStruct(shape, F32)


def perm_block(fr_ref, at, face):
    m = fr_ref.shape[1]
    blocks = []
    for j in range(face // 128):
        ids = fr_ref[:, pl.ds(pl.multiple_of(at + j * 128, 128), 128)].astype(F32)
        ids = jnp.transpose(jnp.broadcast_to(ids, (128, 128)))
        lane = lax.broadcasted_iota(jnp.int32, (128, 128), 1).astype(F32)
        blocks.append(jnp.concatenate([(ids == lane + 128.0 * i).astype(F32).astype(BF16) for i in range(m // 128)], axis=1))
    return jnp.concatenate(blocks, axis=0)


def scatter_block(fr_ref, at, rows):
    m = fr_ref.shape[1]
    ids = lax.broadcasted_iota(jnp.int32, (rows, m), 0) + at
    return (ids == fr_ref[...]).astype(F32).astype(BF16)


def gather_faces(fr, v):
    m, r = v.shape
    face = m // 4

    def body(fr_ref, v_ref, *refs):
        outs, (hi, lo) = refs[:4], refs[4:]
        hi[...], lo[...] = halves(v_ref[...])
        for k in range(4):
            pb = perm_block(fr_ref, k * face, face)
            outs[k][...] = one_pass(pb, hi[...], NN) + one_pass(pb, lo[...], NN)

    return call(body, [out(face, r)] * 4, [fr, v], scratch=[VMEM((m, r), BF16)] * 2, flops=4 * m * m * r, name="gather_faces")


def scatter_neumann(flags, fr, v, recv, nmat):
    m, r = v.shape
    face = m // 4
    step = 256

    def body(flags_ref, fr_ref, v_ref, a_ref, b_ref, c_ref, d_ref, n_ref, jump_ref, work_ref, hi, lo, fh, fl):
        i = pl.program_id(0)

        @pl.when(i == 0)
        def _():
            for k, ref in enumerate((a_ref, b_ref, c_ref, d_ref)):
                fh[k * face:(k + 1) * face], fl[k * face:(k + 1) * face] = halves(ref[...] * flags_ref[k])

            @pl.loop(0, m // step)
            def _(j):
                rows = pl.ds(pl.multiple_of(j * step, step), step)
                sb = scatter_block(fr_ref, j * step, step)
                jump = v_ref[rows, :] - (one_pass(sb, fh[...], NN) + one_pass(sb, fl[...], NN))
                jump_ref[rows, :] = jump
                hi[rows, :], lo[rows, :] = halves(jump)

        work_ref[...] = three(n_ref[...], (hi[...], lo[...]))

    whole = lambda shape: pl.BlockSpec(shape, lambda i: (0, 0), pipeline_mode=pl.Buffered(1))
    return call(
        body, [pltpu.HBM((m, r), F32)] * 2, [flags, fr, v, *recv, nmat], grid=(m // step,),
        in_specs=[pl.BlockSpec(memory_space=SMEM), whole(fr.shape), whole(v.shape)] + [whole((face, r))] * 4 + [pl.BlockSpec((step, m), lambda i: (i, 0))],
        out_specs=[whole((m, r)), pl.BlockSpec((step, r), lambda i: (i, 0))],
        scratch=[VMEM((m, r), BF16)] * 4, flops=10 * m * m * r, name="scatter_neumann",
    )


def dirichlet_gather(fr, work, jump, dmat, dptf, npr):
    m, r = work.shape
    face, p = m // 4, npr.shape[0]
    step = 256

    def body(fr_ref, w_ref, j_ref, d_ref, t_ref, n_ref, dw_ref, base_ref, a_ref, b_ref, c_ref, e_ref, np_ref, hi, lo):
        i = pl.program_id(0)

        @pl.when(i == 0)
        def _():
            hi[...], lo[...] = halves(w_ref[...])

        rows = pl.ds(pl.multiple_of(i * step, step), step)
        dw = three(d_ref[...], (hi[...], lo[...]))
        dw_ref[rows, :] = dw
        base_ref[rows, :] = j_ref[...] - 0.5 * dw

        @pl.when(i == m // step - 1)
        def _():
            hi[...], lo[...] = halves(base_ref[...])
            for k, ref in enumerate((a_ref, b_ref, c_ref, e_ref)):
                pb = perm_block(fr_ref, k * face, face)
                ref[:face] = one_pass(pb, hi[...], NN) + one_pass(pb, lo[...], NN)
                if k < 2:
                    ref[face:] = t_ref[:, k * face:(k + 1) * face]
            np_ref[...] = three(n_ref[...], (hi[...], lo[...]))

    whole = lambda shape: pl.BlockSpec(shape, lambda i: (0, 0), pipeline_mode=pl.Buffered(1))
    res = call(
        body, [out(m, r), out(m, r)] + [out(face + p, r)] * 2 + [out(face, r)] * 2 + [out(p, r)], [fr, in_hbm(work), in_hbm(jump), dmat, dptf, npr], grid=(m // step,),
        in_specs=[whole(fr.shape), whole((m, r)), pl.BlockSpec((step, r), lambda i: (i, 0)), pl.BlockSpec((step, m), lambda i: (i, 0)), whole(dptf.shape), whole(npr.shape)],
        out_specs=[whole((m, r))] * 2 + [whole((face + p, r))] * 2 + [whole((face, r))] * 2 + [whole((p, r))],
        scratch=[VMEM((m, r), BF16)] * 2, flops=10 * m * m * r, name="dirichlet_gather",
    )
    return res[0], res[1], res[2:6], res[6]


def first_cvec(flags, nprr, nprf, recv):
    p, r = nprr.shape
    face = recv[0].shape[0]

    def body(flags_ref, b_ref, *refs):
        total = b_ref[...]
        for k in range(4):
            total = total - flags_ref[k] * three(refs[4 + k][...], refs[k][...])
        refs[8][...] = total

    return call(body, [out(p, r)], [flags, nprr, *recv, *nprf], in_specs=[pl.BlockSpec(memory_space=SMEM)] + [pl.BlockSpec(memory_space=VMEM)] * 9,
                flops=6 * p * 4 * face * r, name="first_cvec")[0]


def coarse_product(core, cblk, blocks):
    width = cblk[0].shape[1]
    p, r = blocks[0].shape
    rows = NZ * p

    def body(core_ref, c0, c1, c2, c3, *refs):
        ins, outs, (hi, lo, ch, cl) = refs[:len(blocks)], refs[len(blocks):len(blocks) + NZ], refs[len(blocks) + NZ:]
        for k, ref in enumerate((c0, c1, c2, c3)):
            ch[k * p:(k + 1) * p], cl[k * p:(k + 1) * p] = halves(ref[...])
        second = core_ref[0] == 1
        for k in range(NY):
            a, b = halves(ins[2 * k][...]), halves(ins[2 * k + 1][...])
            for ref, u, w in zip((hi, lo), a, b):
                u, w = u.astype(F32), w.astype(F32)
                ref[2 * k * p:(2 * k + 1) * p] = jnp.where(second, w, u).astype(BF16)
                ref[(2 * k + 1) * p:(2 * k + 2) * p] = jnp.where(second, u, w).astype(BF16)
        total = three((ch[...], cl[...]), (hi[...], lo[...]))
        for k in range(NZ):
            outs[k][...] = total[k * p:(k + 1) * p]

    return call(body, [out(p, r)] * NZ, [core, *cblk, *blocks],
                in_specs=[pl.BlockSpec(memory_space=SMEM)] + [pl.BlockSpec(memory_space=VMEM)] * (NZ + len(blocks)),
                scratch=[VMEM((width, r), BF16)] * 2 + [VMEM((rows, width), BF16)] * 2, flops=6 * rows * width * r, name="coarse_product")


def couplings(flags, nprf, got, base_part, own):
    p, r = base_part.shape
    face = nprf[0].shape[1]

    def body(flags_ref, b_ref, o_ref, na, nb, a, b, total_ref, g_ref):
        total = b_ref[...]
        g_ref[0] = -0.5 * o_ref[...]
        for k, (n, ref) in enumerate(((na, a), (nb, b))):
            nk = halves(n[...])
            total = total - flags_ref[k] * three(nk, ref[:face])
            g_ref[k + 1] = (0.5 * flags_ref[k]) * three(nk, ref[face:], NT)
        total_ref[...] = total

    return call(body, [out(p, r), out(3, p, p)], [flags, base_part, own, *nprf[:2], *got],
                in_specs=[pl.BlockSpec(memory_space=SMEM)] + [pl.BlockSpec(memory_space=VMEM)] * 6,
                flops=12 * p * (face + p) * r, name="couplings")


def chain_faces(faces, dptf, chain):
    face, r = faces[0].shape

    def body(t_ref, c_ref, a, b, ao, bo):
        ch = halves(c_ref[...])
        for k, (ref, o) in enumerate(((a, ao), (b, bo))):
            o[...] = ref[...] - 0.5 * three(halves(t_ref[:, (k + 2) * face:(k + 3) * face]), ch, TN)

    return call(body, [out(face, r)] * 2, [dptf, chain, *faces], flops=12 * chain.shape[0] * face * r, name="chain_faces")


def next_cvec(flags, cbase, gmat, chains, nprf, got):
    p, r = cbase.shape

    def body(flags_ref, c_ref, g_ref, c0, c1, c2, n2, n3, a, b, o_ref):
        total = c_ref[...]
        for k, ref in enumerate((c0, c1, c2)):
            total = total + three(g_ref[k], ref[...])
        for k, (n, ref) in enumerate(((n2, a), (n3, b))):
            total = total - flags_ref[k + 2] * three(n[...], ref[...])
        o_ref[...] = total

    return call(body, [out(p, r)], [flags, cbase, gmat, *chains, *nprf[2:], *got],
                in_specs=[pl.BlockSpec(memory_space=SMEM)] + [pl.BlockSpec(memory_space=VMEM)] * 9, flops=40 * p * p * r, name="next_cvec")[0]


def second_neumann(flags, fr, base, got, dpt, chains, nmat):
    m, r = base.shape
    p = dpt.shape[0]
    face = m // 4
    step = 256

    def body(flags_ref, fr_ref, v_ref, a_ref, b_ref, c_ref, d_ref, t_ref, own_ref, q0, q1, n_ref, jump_ref, dc_ref, work_ref, hi, lo, fh, fl):
        i = pl.program_id(0)

        @pl.when(i == 0)
        def _():
            for k, (ref, q) in enumerate(zip((a_ref, b_ref, c_ref, d_ref), (q0, q1, None, None))):
                got_k = ref[...] if q is None else ref[:face] - 0.5 * three(ref[face:], q[...], TN)
                fh[k * face:(k + 1) * face], fl[k * face:(k + 1) * face] = halves(got_k * flags_ref[k])
                rows = slice(k * face, (k + 1) * face)
                dc_ref[rows, :] = three(t_ref[:, rows], own_ref[...], TN)

            @pl.loop(0, m // step)
            def _(j):
                rows = pl.ds(pl.multiple_of(j * step, step), step)
                sb = scatter_block(fr_ref, j * step, step)
                jump = v_ref[rows, :] - 0.5 * dc_ref[rows, :] - (one_pass(sb, fh[...], NN) + one_pass(sb, fl[...], NN))
                jump_ref[rows, :] = jump
                hi[rows, :], lo[rows, :] = halves(jump)

        work_ref[...] = three(n_ref[...], (hi[...], lo[...]))

    whole = lambda shape: pl.BlockSpec(shape, lambda i: (0, 0), pipeline_mode=pl.Buffered(1))
    return call(
        body, [pltpu.HBM((m, r), F32), out(m, r), pltpu.HBM((m, r), F32)], [flags, fr, base, *got, dpt, *chains, nmat], grid=(m // step,),
        in_specs=[pl.BlockSpec(memory_space=SMEM), whole(fr.shape), whole(base.shape)] + [whole(g.shape) for g in got] + [whole(dpt.shape)]
        + [whole((p, r))] * 3 + [pl.BlockSpec((step, m), lambda i: (i, 0))],
        out_specs=[whole((m, r)), whole((m, r)), pl.BlockSpec((step, r), lambda i: (i, 0))],
        scratch=[VMEM((m, r), BF16)] * 4, flops=11 * m * m * r, name="second_neumann",
    )


def second_dirichlet(work, jump, dw, dc, dmat):
    m, r = work.shape
    step = 256

    def body(w_ref, j_ref, p_ref, c_ref, d_ref, s_ref, r_ref, hi, lo):
        @pl.when(pl.program_id(0) == 0)
        def _():
            hi[...], lo[...] = halves(w_ref[...])

        dw1 = three(d_ref[...], (hi[...], lo[...]))
        s_ref[...] = p_ref[...] + c_ref[...] + dw1
        r_ref[...] = j_ref[...] - 0.5 * dw1

    blk = pl.BlockSpec((step, r), lambda i: (i, 0))
    return call(
        body, [out(m, r)] * 2, [in_hbm(work), in_hbm(jump), dw, dc, dmat], grid=(m // step,),
        in_specs=[pl.BlockSpec((m, r), lambda i: (0, 0), pipeline_mode=pl.Buffered(1)), blk, blk, blk, pl.BlockSpec((step, m), lambda i: (i, 0))],
        out_specs=[blk, blk], scratch=[VMEM((m, r), BF16)] * 2, flops=6 * m * m * r, name="second_dirichlet",
    )


def last_update(dpt, own, over, v, sol, res):
    p, m = dpt.shape
    r = own.shape[1]
    step = 256

    def body(t_ref, a_ref, o_ref, v_ref, s_ref, r_ref, so_ref, ro_ref, hi, lo):
        @pl.when(pl.program_id(0) == 0)
        def _():
            for k in range(r // 128):
                lanes = slice(k * 128, (k + 1) * 128)
                hi[:, lanes], lo[:, lanes] = halves(a_ref[:, lanes] + v_ref[0] * o_ref[:, lanes])

        u = three(t_ref[...], (hi[...], lo[...]), TN)
        so_ref[...] = s_ref[...] + u
        ro_ref[...] = r_ref[...] - 0.5 * u

    blk = pl.BlockSpec((step, r), lambda i: (i, 0))
    small = pl.BlockSpec((p, r), lambda i: (0, 0))
    return call(
        body, [out(m, r)] * 2, [dpt, own, over, v, sol, res], grid=(m // step,),
        in_specs=[pl.BlockSpec((p, step), lambda i: (0, i)), small, small, pl.BlockSpec(v.shape, lambda i: (0, 0, 0)), blk, blk],
        out_specs=[blk, blk], scratch=[VMEM((p, r), BF16)] * 2, flops=6 * m * p * r, name="last_update",
    )


def one_hot_rows(pr_ref, sel, p, m):
    ids = jnp.transpose(jnp.broadcast_to(pr_ref[...].astype(F32), (128, 128)))[:p]
    lane = lax.broadcasted_iota(jnp.int32, (p, 128), 1).astype(F32)
    for k in range(m // 128):
        sel[:, k * 128:(k + 1) * 128] = (ids == lane + 128.0 * k).astype(F32).astype(BF16)


def primal_rows(prow, nmat, fr, r0, p):
    m, r = r0.shape
    face = m // 4
    step = 256

    def body(pr_ref, n_ref, fr_ref, r_ref, rows_ref, a_ref, b_ref, c_ref, d_ref, prod_ref, sel):
        i = pl.program_id(0)

        @pl.when(i == 0)
        def _():
            one_hot_rows(pr_ref, sel, p, m)
            rows_ref[...] = jnp.zeros((p, m), F32)

        nh, nl = halves(n_ref[...])
        pick = sel[:, pl.ds(pl.multiple_of(i * step, step), step)]
        rows_ref[...] += one_pass(pick, nh, NN) + one_pass(pick, nl, NN)

        @pl.when(i == m // step - 1)
        def _():
            both = halves(rows_ref[...])
            for k, ref in enumerate((a_ref, b_ref, c_ref, d_ref)):
                ids = lax.broadcasted_iota(jnp.int32, (m, face), 0)
                sb = (ids == fr_ref[:, k * face:(k + 1) * face]).astype(F32).astype(BF16)
                ref[...] = one_pass(both[0], sb, NN) + one_pass(both[1], sb, NN)
            prod_ref[...] = three(both, r_ref[...])

    whole = lambda shape: pl.BlockSpec(shape, lambda i: (0, 0), pipeline_mode=pl.Buffered(1))
    res = call(
        body, [out(p, m)] + [out(p, face)] * 4 + [out(p, r)], [prow, nmat, fr, r0], grid=(m // step,),
        in_specs=[whole(prow.shape), pl.BlockSpec((step, m), lambda i: (i, 0)), whole(fr.shape), whole(r0.shape)],
        out_specs=[whole((p, m))] + [whole((p, face))] * 4 + [whole((p, r))], scratch=[VMEM((p, m), BF16)],
        flops=8 * p * m * m, name="primal_rows",
    )
    return res[0], res[1:5], res[5]


def primal_columns(prow, dmat, fr, npr):
    m = dmat.shape[0]
    p = npr.shape[0]
    step = 256

    def body(pr_ref, d_ref, fr_ref, n_ref, t_ref, f_ref, g_ref, sel):
        i = pl.program_id(0)

        @pl.when(i == 0)
        def _():
            one_hot_rows(pr_ref, sel, p, m)

        dh, dl = halves(d_ref[...])
        t_ref[:, pl.ds(pl.multiple_of(i * step, step), step)] = one_pass(sel[...], dh, NT) + one_pass(sel[...], dl, NT)

        @pl.when(i == m // step - 1)
        def _():
            both = halves(t_ref[...])
            for k in range(m // step):
                cols = slice(k * step, (k + 1) * step)
                ids = lax.broadcasted_iota(jnp.int32, (m, step), 0)
                sb = (ids == fr_ref[:, cols]).astype(F32).astype(BF16)
                f_ref[:, cols] = one_pass(both[0], sb, NN) + one_pass(both[1], sb, NN)
            g_ref[...] = three(n_ref[...], both, NT)

    whole = lambda shape: pl.BlockSpec(shape, lambda i: (0, 0), pipeline_mode=pl.Buffered(1))
    return call(
        body, [out(p, m), out(p, m), out(p, p)], [prow, dmat, fr, npr], grid=(m // step,),
        in_specs=[whole(prow.shape), pl.BlockSpec((step, m), lambda i: (i, 0)), whole(fr.shape), whole(npr.shape)],
        out_specs=[whole((p, m)), whole((p, m)), whole((p, p))], scratch=[VMEM((p, m), BF16)], flops=8 * p * m * m, name="primal_columns",
    )


def coarse_cut(place, crow):
    p, total = crow.shape
    width = total // (NZ * NY)

    def body(place_ref, c_ref, *refs):
        z, y = place_ref[0], place_ref[1]
        for k in range(NY):
            for j in range(NZ):
                at = (lax.rem(z + j, NZ) * NY + lax.rem(y + NY - k, NY)) * width
                refs[k][:, j * width:(j + 1) * width] = c_ref[:, pl.ds(pl.multiple_of(at, width), width)]

    return call(body, [out(p, NZ * width)] * NY, [place, crow],
                in_specs=[pl.BlockSpec(memory_space=SMEM), pl.BlockSpec(memory_space=VMEM)], name="coarse_cut")


def column(row, p):
    return jnp.transpose(jnp.broadcast_to(row, (128, 128)))[:p]


def sweep(ref, cols, loc, p, r):
    loc[0] = jnp.zeros((p, r), F32)
    for j in range(NX):
        for b in range(r // 128):
            lanes = slice(b * 128, (b + 1) * 128)
            loc[j + 1, :, lanes] = ref[j, :p, lanes] + cols[j] * loc[j, :, lanes]


def first_half(place, pieces, p):
    rows, r = pieces[0].shape

    def body(place_ref, a, b, c, d, send_ref, own_ref, low_ref, high_ref, v_ref, col_ref, q, loc, pv):
        h, x = place_ref[2], place_ref[3]
        for k, ref in enumerate((a, b, c, d)):
            q[lax.rem(x + k, NX)] = ref[...]
        pv[0] = jnp.ones((p, 128), F32)
        for j in range(NX):
            col_ref[j] = column(q[j, p:p + 1, :128], p)
            pv[j + 1] = pv[j] * col_ref[j]
        pv[NX + 1] = jnp.zeros((p, 128), F32)
        sweep(q, col_ref, loc, p, r)
        loc[NX + 1] = jnp.zeros((p, r), F32)
        upper = h == 1
        own_ref[...], low_ref[...], high_ref[...] = loc[x + 1], loc[x], loc[x + 2]
        for n, at in enumerate((x + 1, x, x + 2)):
            v_ref[n] = jnp.where(upper, pv[at], jnp.zeros((p, 128), F32))
        send_ref[:p] = jnp.where(upper, q[0, :p], loc[NX])
        send_ref[p:] = q[0, p:]

    return call(
        body, [out(rows, r)] + [out(p, r)] * 3 + [out(3, p, 128), out(NX, p, 128)], [place, *pieces],
        in_specs=[pl.BlockSpec(memory_space=SMEM)] + [pl.BlockSpec(memory_space=VMEM)] * 4,
        scratch=[VMEM((NX, rows, r), F32), VMEM((NX + 2, p, r), F32), VMEM((NX + 2, p, 128), F32)], name="first_half",
    )


def first_chains(place, over, own, low, high, v):
    p, r = own.shape

    def body(place_ref, over_ref, a, b, c, v_ref, ao, bo, co):
        last = jnp.logical_and(place_ref[2] == 0, place_ref[3] == NX - 1)
        rate = column(over_ref[p:p + 1, :128], p)
        for k in range(r // 128):
            lanes = slice(k * 128, (k + 1) * 128)
            came = over_ref[:p, lanes]
            ao[:, lanes] = a[:, lanes] + v_ref[0] * came
            bo[:, lanes] = b[:, lanes] + v_ref[1] * came
            co[:, lanes] = jnp.where(last, came + rate * a[:, lanes], c[:, lanes] + v_ref[2] * came)

    return call(body, [out(p, r)] * 3, [place, over, own, low, high, v],
                in_specs=[pl.BlockSpec(memory_space=SMEM)] + [pl.BlockSpec(memory_space=VMEM)] * 5, name="first_chains")


def second_half(place, pieces, cols):
    p, r = pieces[0].shape

    def body(place_ref, a, b, c, d, col_ref, send_ref, own_ref, q, loc):
        x = place_ref[3]
        for k, ref in enumerate((a, b, c, d)):
            q[lax.rem(x + k, NX)] = ref[...]
        sweep(q, col_ref, loc, p, r)
        own_ref[...] = loc[x + 1]
        send_ref[...] = loc[NX]

    return call(body, [out(p, r)] * 2, [place, *pieces, cols],
                in_specs=[pl.BlockSpec(memory_space=SMEM)] + [pl.BlockSpec(memory_space=VMEM)] * 5,
                scratch=[VMEM((NX, p, r), F32), VMEM((NX + 1, p, r), F32)], name="second_half")


def local(residual_in, neumann, dirichlet, coarse, decay, face_rows, primal):
    r0 = residual_in[0, 0]
    nmat = neumann[0, 0]
    dmat = dirichlet[0, 0]
    crow = coarse[0]
    dec = decay[0, 0]
    fr = face_rows[0]
    pr = primal[0, 0]
    m, r = r0.shape
    face = m // 4
    p = pr.shape[0]
    gx = lax.axis_index("gx")
    gy = lax.axis_index("gy")
    h, x = gx // NX, gx % NX
    z, y, c = gy // (NY * NC), (gy // NC) % NY, gy % NC
    flags = jnp.stack([gx > 0, gx < GX - 1, gy > 0, gy < GY - 1]).astype(F32)
    core = c.reshape(1).astype(jnp.int32)
    place = jnp.stack([z, y, h, x]).astype(jnp.int32)

    def exchange(blocks):
        return [ring(blocks[1], "gx", 1), ring(blocks[0], "gx", -1), ring(blocks[3], "gy", 1), ring(blocks[2], "gy", -1)]

    cut = coarse_cut(place, crow)
    fr = after(fr, cut)
    cblk = [cut[0]] + [pull_y(cut[k], k) for k in range(1, NY)]
    faces0 = gather_faces(fr, r0)
    recv0 = exchange(faces0)
    prow = jnp.pad(pr, (0, 128 - p))[None]
    prow = after(prow, cblk)
    npr, nprf, nprr = primal_rows(prow, nmat, fr, r0, p)
    dpt, dptf, g_own = primal_columns(prow, dmat, fr, npr)
    dec_rows = jnp.pad(dec[None], ((0, 7), (0, r - p)))

    def spread(cvec):
        return [cvec] + [pull_z(cvec, k) for k in range(1, NZ)]

    def product(own, gate, blk):
        own = after(own, *gate)
        twin = [pull_core(v) for v in own]
        return coarse_product(core, blk, [b for pair in zip(own, twin) for b in pair])

    def summed(part):
        total = part[0]
        for k in range(1, NY):
            total = total + pull_y(part[k], NY - k)
        return total

    cvec0 = first_cvec(flags, nprr, nprf, recv0)
    own0 = spread(cvec0)
    recv_g, fr_g, dpt, dptf, g_own = after((recv0, fr, dpt, dptf, g_own), cvec0)
    jump0, work0 = scatter_neumann(flags, fr_g, r0, recv_g, nmat)
    part0 = product(own0, [work0], cblk)
    work_g = after(work0, part0)
    dw0, base, packed, base_part = dirichlet_gather(fr, work_g, jump0, dmat, dptf, npr)
    got = [ring(packed[1], "gx", 1), ring(packed[0], "gx", -1)]
    cq0 = jnp.concatenate([summed(part0), dec_rows], axis=0)
    cq0 = after(cq0, packed)
    pieces = [cq0] + [pull_x(cq0, k) for k in range(1, NX)]
    send, own, low, high, v, cols = first_half(place, pieces, p)
    over = pull_half(send)
    v_late = after(v, got)
    chain0, low, high = first_chains(place, over, own, low, high, v_late)
    cols_r = chain_faces(packed[2:], dptf, chain0)
    got_y = [ring(cols_r[1], "gy", 1), ring(cols_r[0], "gy", -1)]
    chains = [chain0, low, high]
    cbase, gmat = couplings(flags, nprf, got, base_part, g_own)
    cvec1 = next_cvec(flags, cbase, gmat, chains, nprf, got_y)

    own1 = spread(cvec1)
    fr_h = after(fr, cvec1)
    jump1, dc0, work1 = second_neumann(flags, fr_h, base, got + got_y, dpt, chains, nmat)
    part1 = product(own1, [work1], cblk)
    work1 = after(work1, part1)
    sol, res = second_dirichlet(work1, jump1, dw0, dc0, dmat)
    cq1 = after(summed(part1), res)
    pieces = [cq1] + [pull_x(cq1, k) for k in range(1, NX)]
    send, own = second_half(place, pieces, cols)
    solution, residual = last_update(dpt, own, pull_half(send), v, sol, res)
    return (solution[None, None], residual[None, None])


def solution(mesh):
    lead = P("gx", "gy", None, None)
    vec = P("gx", "gy", None)
    return jax.shard_map(
        local,
        mesh=mesh,
        in_specs=(lead, lead, lead, vec, vec, vec, vec),
        out_specs=(lead, lead),
        check_vma=False,
    )
```

```python
import math

import jax
import jax.numpy as jnp
from jax import lax
from jax.experimental import pallas as pl
from jax.experimental.pallas import tpu as pltpu
from jax.sharding import PartitionSpec as P

NZ, NY, NC, NX, NH = 4, 4, 2, 4, 2
GY = NZ * NY * NC
GX = NX * NH
F32, BF16 = jnp.float32, jnp.bfloat16
COST = 1
GRANT = 20 * 2**20
VMEM, SMEM = pltpu.VMEM, pltpu.SMEM
NN, NT, TN = ((1,), (0,)), ((1,), (1,)), ((0,), (0,))


def gy_index(z, y, c):
    return (z * NY + y) * NC + c


def pull_y(v, k):
    return lax.ppermute(v, "gy", [(gy_index(z, (y + k) % NY, c), gy_index(z, y, c)) for z in range(NZ) for y in range(NY) for c in range(NC)])


def pull_z(v, k):
    return lax.ppermute(v, "gy", [(gy_index((z + k) % NZ, y, c), gy_index(z, y, c)) for z in range(NZ) for y in range(NY) for c in range(NC)])


def pull_core(v):
    return lax.ppermute(v, "gy", [(i, i ^ 1) for i in range(GY)])


def pull_x(v, k):
    return lax.ppermute(v, "gx", [(h * NX + (x + k) % NX, h * NX + x) for h in range(NH) for x in range(NX)])


def pull_half(v):
    return lax.ppermute(v, "gx", [(i, (i + NX) % GX) for i in range(GX)])


def ring(v, axis, by):
    n = GX if axis == "gx" else GY
    return lax.ppermute(v, axis, [(i, (i + by) % n) for i in range(n)])


def dot(a, b, dims=NN):
    return lax.dot_general(a, b, (dims, ((), ())), precision=lax.Precision.HIGH, preferred_element_type=F32)


def one_pass(a, b, dims):
    return lax.dot_general(a, b, (dims, ((), ())), preferred_element_type=F32)


def halves(v):
    hi = v.astype(BF16)
    return hi, (v - hi.astype(F32)).astype(BF16)


def three(a, b, dims=NN):
    ah, al = a if isinstance(a, tuple) else halves(a)
    bh, bl = b if isinstance(b, tuple) else halves(b)
    return one_pass(ah, bh, dims) + (one_pass(ah, bl, dims) + one_pass(al, bh, dims))


def after(values, *earlier):
    return lax.optimization_barrier((values, earlier))[0]


def call(body, outs, ins, *, grid=None, in_specs=None, out_specs=None, scratch=(), flops=0, name=None):
    whole = pl.BlockSpec(memory_space=VMEM)
    nbytes = sum(4 * v.size for v in ins) + sum(4 * math.prod(o.shape) for o in outs)
    kwargs = {} if grid is None else {"grid": grid}
    return pl.pallas_call(
        body,
        out_shape=outs,
        in_specs=in_specs or [whole] * len(ins),
        out_specs=out_specs or [whole] * len(outs),
        scratch_shapes=list(scratch),
        compiler_params=pltpu.CompilerParams(vmem_limit_bytes=GRANT),
        cost_estimate=pl.CostEstimate(flops=flops // COST, bytes_accessed=nbytes // COST, transcendentals=0),
        name=name,
        **kwargs,
    )(*ins)


def in_hbm(v):
    return pltpu.with_memory_space_constraint(v, pltpu.HBM)


def out(*shape):
    return jax.ShapeDtypeStruct(shape, F32)


def perm_block(fr_ref, at, face):
    m = fr_ref.shape[1]
    blocks = []
    for j in range(face // 128):
        ids = fr_ref[:, pl.ds(pl.multiple_of(at + j * 128, 128), 128)].astype(F32)
        ids = jnp.transpose(jnp.broadcast_to(ids, (128, 128)))
        lane = lax.broadcasted_iota(jnp.int32, (128, 128), 1).astype(F32)
        blocks.append(jnp.concatenate([(ids == lane + 128.0 * i).astype(F32).astype(BF16) for i in range(m // 128)], axis=1))
    return jnp.concatenate(blocks, axis=0)


def scatter_block(fr_ref, at, rows):
    m = fr_ref.shape[1]
    ids = lax.broadcasted_iota(jnp.int32, (rows, m), 0) + at
    return (ids == fr_ref[...]).astype(F32).astype(BF16)


def gather_faces(fr, v):
    m, r = v.shape
    face = m // 4

    def body(fr_ref, v_ref, *refs):
        outs, (hi, lo) = refs[:4], refs[4:]
        hi[...], lo[...] = halves(v_ref[...])
        for k in range(4):
            pb = perm_block(fr_ref, k * face, face)
            outs[k][...] = one_pass(pb, hi[...], NN) + one_pass(pb, lo[...], NN)

    return call(body, [out(face, r)] * 4, [fr, v], scratch=[VMEM((m, r), BF16)] * 2, flops=4 * m * m * r, name="gather_faces")


def scatter_neumann(flags, fr, v, recv, nmat):
    m, r = v.shape
    face = m // 4
    step = 256

    def body(flags_ref, fr_ref, v_ref, a_ref, b_ref, c_ref, d_ref, n_ref, jump_ref, work_ref, hi, lo, fh, fl):
        i = pl.program_id(0)

        @pl.when(i == 0)
        def _():
            for k, ref in enumerate((a_ref, b_ref, c_ref, d_ref)):
                fh[k * face:(k + 1) * face], fl[k * face:(k + 1) * face] = halves(ref[...] * flags_ref[k])

            @pl.loop(0, m // step)
            def _(j):
                rows = pl.ds(pl.multiple_of(j * step, step), step)
                sb = scatter_block(fr_ref, j * step, step)
                jump = v_ref[rows, :] - (one_pass(sb, fh[...], NN) + one_pass(sb, fl[...], NN))
                jump_ref[rows, :] = jump
                hi[rows, :], lo[rows, :] = halves(jump)

        work_ref[...] = three(n_ref[...], (hi[...], lo[...]))

    whole = lambda shape: pl.BlockSpec(shape, lambda i: (0, 0), pipeline_mode=pl.Buffered(1))
    return call(
        body, [pltpu.HBM((m, r), F32)] * 2, [flags, fr, v, *recv, nmat], grid=(m // step,),
        in_specs=[pl.BlockSpec(memory_space=SMEM), whole(fr.shape), whole(v.shape)] + [whole((face, r))] * 4 + [pl.BlockSpec((step, m), lambda i: (i, 0))],
        out_specs=[whole((m, r)), pl.BlockSpec((step, r), lambda i: (i, 0))],
        scratch=[VMEM((m, r), BF16)] * 4, flops=10 * m * m * r, name="scatter_neumann",
    )


def dirichlet_gather(fr, work, jump, dmat, dptf):
    m, r = work.shape
    face, p = m // 4, dptf.shape[0]
    step = 256

    def body(fr_ref, w_ref, j_ref, d_ref, t_ref, dw_ref, base_ref, a_ref, b_ref, hi, lo):
        i = pl.program_id(0)

        @pl.when(i == 0)
        def _():
            hi[...], lo[...] = halves(w_ref[...])

        rows = pl.ds(pl.multiple_of(i * step, step), step)
        dw = three(d_ref[...], (hi[...], lo[...]))
        dw_ref[rows, :] = dw
        base_ref[rows, :] = j_ref[...] - 0.5 * dw

        @pl.when(i == m // step - 1)
        def _():
            hi[...], lo[...] = halves(base_ref[...])
            for k, ref in enumerate((a_ref, b_ref)):
                pb = perm_block(fr_ref, k * face, face)
                ref[:face] = one_pass(pb, hi[...], NN) + one_pass(pb, lo[...], NN)
                ref[face:] = t_ref[:, k * face:(k + 1) * face]

    whole = lambda shape: pl.BlockSpec(shape, lambda i: (0, 0), pipeline_mode=pl.Buffered(1))
    res = call(
        body, [out(m, r), out(m, r)] + [out(face + p, r)] * 2, [fr, in_hbm(work), in_hbm(jump), dmat, dptf], grid=(m // step,),
        in_specs=[whole(fr.shape), whole((m, r)), pl.BlockSpec((step, r), lambda i: (i, 0)), pl.BlockSpec((step, m), lambda i: (i, 0)), whole(dptf.shape)],
        out_specs=[whole((m, r))] * 2 + [whole((face + p, r))] * 2,
        scratch=[VMEM((m, r), BF16)] * 2, flops=10 * m * m * r, name="dirichlet_gather",
    )
    return res[0], res[1], res[2:]


def column_faces(fr, base, npr):
    m, r = base.shape
    face, p = m // 4, npr.shape[0]

    def body(fr_ref, b_ref, n_ref, a_ref, c_ref, o_ref):
        both = halves(b_ref[...])
        for k, ref in enumerate((a_ref, c_ref)):
            pb = perm_block(fr_ref, (k + 2) * face, face)
            ref[...] = one_pass(pb, both[0], NN) + one_pass(pb, both[1], NN)
        o_ref[...] = three(n_ref[...], both)

    res = call(body, [out(face, r)] * 2 + [out(p, r)], [fr, base, npr], flops=2 * m * m * r, name="column_faces")
    return res[:2], res[2]


def first_cvec(flags, nprr, nprf, recv):
    p, r = nprr.shape
    face = recv[0].shape[0]

    def body(flags_ref, b_ref, *refs):
        total = b_ref[...]
        for k in range(4):
            total = total - flags_ref[k] * three(refs[4 + k][...], refs[k][...])
        refs[8][...] = total

    return call(body, [out(p, r)], [flags, nprr, *recv, *nprf], in_specs=[pl.BlockSpec(memory_space=SMEM)] + [pl.BlockSpec(memory_space=VMEM)] * 9,
                flops=6 * p * 4 * face * r, name="first_cvec")[0]


def coarse_product(core, cblk, blocks):
    width = cblk[0].shape[1]
    p, r = blocks[0].shape
    rows = NZ * p

    def body(core_ref, c0, c1, c2, c3, *refs):
        ins, outs, (hi, lo, ch, cl) = refs[:len(blocks)], refs[len(blocks):len(blocks) + NZ], refs[len(blocks) + NZ:]
        for k, ref in enumerate((c0, c1, c2, c3)):
            ch[k * p:(k + 1) * p], cl[k * p:(k + 1) * p] = halves(ref[...])
        second = core_ref[0] == 1
        for k in range(NY):
            a, b = halves(ins[2 * k][...]), halves(ins[2 * k + 1][...])
            for ref, u, w in zip((hi, lo), a, b):
                u, w = u.astype(F32), w.astype(F32)
                ref[2 * k * p:(2 * k + 1) * p] = jnp.where(second, w, u).astype(BF16)
                ref[(2 * k + 1) * p:(2 * k + 2) * p] = jnp.where(second, u, w).astype(BF16)
        total = three((ch[...], cl[...]), (hi[...], lo[...]))
        for k in range(NZ):
            outs[k][...] = total[k * p:(k + 1) * p]

    return call(body, [out(p, r)] * NZ, [core, *cblk, *blocks],
                in_specs=[pl.BlockSpec(memory_space=SMEM)] + [pl.BlockSpec(memory_space=VMEM)] * (NZ + len(blocks)),
                scratch=[VMEM((width, r), BF16)] * 2 + [VMEM((rows, width), BF16)] * 2, flops=6 * rows * width * r, name="coarse_product")


def couplings(flags, nprf, got, base_part, own):
    p, r = base_part.shape
    face = nprf[0].shape[1]

    def body(flags_ref, b_ref, o_ref, na, nb, a, b, total_ref, g_ref):
        total = b_ref[...]
        g_ref[0] = -0.5 * o_ref[...]
        for k, (n, ref) in enumerate(((na, a), (nb, b))):
            nk = halves(n[...])
            total = total - flags_ref[k] * three(nk, ref[:face])
            g_ref[k + 1] = (0.5 * flags_ref[k]) * three(nk, ref[face:], NT)
        total_ref[...] = total

    return call(body, [out(p, r), out(3, p, p)], [flags, base_part, own, *nprf[:2], *got],
                in_specs=[pl.BlockSpec(memory_space=SMEM)] + [pl.BlockSpec(memory_space=VMEM)] * 6,
                flops=12 * p * (face + p) * r, name="couplings")


def chain_faces(faces, dptf, chain):
    face, r = faces[0].shape

    def body(t_ref, c_ref, a, b, ao, bo):
        ch = halves(c_ref[...])
        for k, (ref, o) in enumerate(((a, ao), (b, bo))):
            o[...] = ref[...] - 0.5 * three(halves(t_ref[:, (k + 2) * face:(k + 3) * face]), ch, TN)

    return call(body, [out(face, r)] * 2, [dptf, chain, *faces], flops=12 * chain.shape[0] * face * r, name="chain_faces")


def next_cvec(flags, cbase, gmat, chains, nprf, got):
    p, r = cbase.shape

    def body(flags_ref, c_ref, g_ref, c0, c1, c2, n2, n3, a, b, o_ref):
        total = c_ref[...]
        for k, ref in enumerate((c0, c1, c2)):
            total = total + three(g_ref[k], ref[...])
        for k, (n, ref) in enumerate(((n2, a), (n3, b))):
            total = total - flags_ref[k + 2] * three(n[...], ref[...])
        o_ref[...] = total

    return call(body, [out(p, r)], [flags, cbase, gmat, *chains, *nprf[2:], *got],
                in_specs=[pl.BlockSpec(memory_space=SMEM)] + [pl.BlockSpec(memory_space=VMEM)] * 9, flops=40 * p * p * r, name="next_cvec")[0]


def second_neumann(flags, fr, base, got, dpt, chains, nmat):
    m, r = base.shape
    p = dpt.shape[0]
    face = m // 4
    step = 256

    def body(flags_ref, fr_ref, v_ref, a_ref, b_ref, c_ref, d_ref, t_ref, own_ref, q0, q1, n_ref, jump_ref, dc_ref, work_ref, hi, lo, fh, fl):
        i = pl.program_id(0)

        @pl.when(i == 0)
        def _():
            for k, (ref, q) in enumerate(zip((a_ref, b_ref, c_ref, d_ref), (q0, q1, None, None))):
                got_k = ref[...] if q is None else ref[:face] - 0.5 * three(ref[face:], q[...], TN)
                fh[k * face:(k + 1) * face], fl[k * face:(k + 1) * face] = halves(got_k * flags_ref[k])
                rows = slice(k * face, (k + 1) * face)
                dc_ref[rows, :] = three(t_ref[:, rows], own_ref[...], TN)

            @pl.loop(0, m // step)
            def _(j):
                rows = pl.ds(pl.multiple_of(j * step, step), step)
                sb = scatter_block(fr_ref, j * step, step)
                jump = v_ref[rows, :] - 0.5 * dc_ref[rows, :] - (one_pass(sb, fh[...], NN) + one_pass(sb, fl[...], NN))
                jump_ref[rows, :] = jump
                hi[rows, :], lo[rows, :] = halves(jump)

        work_ref[...] = three(n_ref[...], (hi[...], lo[...]))

    whole = lambda shape: pl.BlockSpec(shape, lambda i: (0, 0), pipeline_mode=pl.Buffered(1))
    return call(
        body, [out(m, r)] * 3, [flags, fr, base, *got, dpt, *chains, nmat], grid=(m // step,),
        in_specs=[pl.BlockSpec(memory_space=SMEM), whole(fr.shape), whole(base.shape)] + [whole(g.shape) for g in got] + [whole(dpt.shape)]
        + [whole((p, r))] * 3 + [pl.BlockSpec((step, m), lambda i: (i, 0))],
        out_specs=[whole((m, r)), whole((m, r)), pl.BlockSpec((step, r), lambda i: (i, 0))],
        scratch=[VMEM((m, r), BF16)] * 4, flops=11 * m * m * r, name="second_neumann",
    )


def second_dirichlet(work, jump, dw, dc, dmat):
    m, r = work.shape
    step = 256

    def body(w_ref, j_ref, p_ref, c_ref, d_ref, s_ref, r_ref, hi, lo):
        @pl.when(pl.program_id(0) == 0)
        def _():
            hi[...], lo[...] = halves(w_ref[...])

        dw1 = three(d_ref[...], (hi[...], lo[...]))
        s_ref[...] = p_ref[...] + c_ref[...] + dw1
        r_ref[...] = j_ref[...] - 0.5 * dw1

    blk = pl.BlockSpec((step, r), lambda i: (i, 0))
    return call(
        body, [out(m, r)] * 2, [work, jump, dw, dc, dmat], grid=(m // step,),
        in_specs=[pl.BlockSpec((m, r), lambda i: (0, 0), pipeline_mode=pl.Buffered(1)), blk, blk, blk, pl.BlockSpec((step, m), lambda i: (i, 0))],
        out_specs=[blk, blk], scratch=[VMEM((m, r), BF16)] * 2, flops=6 * m * m * r, name="second_dirichlet",
    )


def last_update(dpt, own, over, v, sol, res):
    p, m = dpt.shape
    r = own.shape[1]
    step = 512

    def body(t_ref, a_ref, o_ref, v_ref, s_ref, r_ref, so_ref, ro_ref, hi, lo):
        @pl.when(pl.program_id(0) == 0)
        def _():
            for k in range(r // 128):
                lanes = slice(k * 128, (k + 1) * 128)
                hi[:, lanes], lo[:, lanes] = halves(a_ref[:, lanes] + v_ref[0] * o_ref[:, lanes])

        u = three(t_ref[...], (hi[...], lo[...]), TN)
        so_ref[...] = s_ref[...] + u
        ro_ref[...] = r_ref[...] - 0.5 * u

    blk = pl.BlockSpec((step, r), lambda i: (i, 0))
    small = pl.BlockSpec((p, r), lambda i: (0, 0))
    return call(
        body, [out(m, r)] * 2, [dpt, own, over, v, sol, res], grid=(m // step,),
        in_specs=[pl.BlockSpec((p, step), lambda i: (0, i)), small, small, pl.BlockSpec(v.shape, lambda i: (0, 0, 0)), blk, blk],
        out_specs=[blk, blk], scratch=[VMEM((p, r), BF16)] * 2, flops=6 * m * p * r, name="last_update",
    )


def one_hot_rows(pr_ref, sel, p, m):
    ids = jnp.transpose(jnp.broadcast_to(pr_ref[...].astype(F32), (128, 128)))[:p]
    lane = lax.broadcasted_iota(jnp.int32, (p, 128), 1).astype(F32)
    for k in range(m // 128):
        sel[:, k * 128:(k + 1) * 128] = (ids == lane + 128.0 * k).astype(F32).astype(BF16)


def primal_rows(prow, nmat, fr, r0, p):
    m, r = r0.shape
    face = m // 4
    step = 256

    def body(pr_ref, n_ref, fr_ref, r_ref, rows_ref, a_ref, b_ref, c_ref, d_ref, prod_ref, sel):
        i = pl.program_id(0)

        @pl.when(i == 0)
        def _():
            one_hot_rows(pr_ref, sel, p, m)
            rows_ref[...] = jnp.zeros((p, m), F32)

        nh, nl = halves(n_ref[...])
        pick = sel[:, pl.ds(pl.multiple_of(i * step, step), step)]
        rows_ref[...] += one_pass(pick, nh, NN) + one_pass(pick, nl, NN)

        @pl.when(i == m // step - 1)
        def _():
            both = halves(rows_ref[...])
            for k, ref in enumerate((a_ref, b_ref, c_ref, d_ref)):
                ids = lax.broadcasted_iota(jnp.int32, (m, face), 0)
                sb = (ids == fr_ref[:, k * face:(k + 1) * face]).astype(F32).astype(BF16)
                ref[...] = one_pass(both[0], sb, NN) + one_pass(both[1], sb, NN)
            prod_ref[...] = three(both, r_ref[...])

    whole = lambda shape: pl.BlockSpec(shape, lambda i: (0, 0), pipeline_mode=pl.Buffered(1))
    res = call(
        body, [out(p, m)] + [out(p, face)] * 4 + [out(p, r)], [prow, nmat, fr, r0], grid=(m // step,),
        in_specs=[whole(prow.shape), pl.BlockSpec((step, m), lambda i: (i, 0)), whole(fr.shape), whole(r0.shape)],
        out_specs=[whole((p, m))] + [whole((p, face))] * 4 + [whole((p, r))], scratch=[VMEM((p, m), BF16)],
        flops=8 * p * m * m, name="primal_rows",
    )
    return res[0], res[1:5], res[5]


def primal_columns(prow, dmat, fr, npr):
    m = dmat.shape[0]
    p = npr.shape[0]
    step = 256

    def body(pr_ref, d_ref, fr_ref, n_ref, t_ref, f_ref, g_ref, sel):
        i = pl.program_id(0)

        @pl.when(i == 0)
        def _():
            one_hot_rows(pr_ref, sel, p, m)

        dh, dl = halves(d_ref[...])
        t_ref[:, pl.ds(pl.multiple_of(i * step, step), step)] = one_pass(sel[...], dh, NT) + one_pass(sel[...], dl, NT)

        @pl.when(i == m // step - 1)
        def _():
            both = halves(t_ref[...])
            for k in range(m // step):
                cols = slice(k * step, (k + 1) * step)
                ids = lax.broadcasted_iota(jnp.int32, (m, step), 0)
                sb = (ids == fr_ref[:, cols]).astype(F32).astype(BF16)
                f_ref[:, cols] = one_pass(both[0], sb, NN) + one_pass(both[1], sb, NN)
            g_ref[...] = three(n_ref[...], both, NT)

    whole = lambda shape: pl.BlockSpec(shape, lambda i: (0, 0), pipeline_mode=pl.Buffered(1))
    return call(
        body, [out(p, m), out(p, m), out(p, p)], [prow, dmat, fr, npr], grid=(m // step,),
        in_specs=[whole(prow.shape), pl.BlockSpec((step, m), lambda i: (i, 0)), whole(fr.shape), whole(npr.shape)],
        out_specs=[whole((p, m)), whole((p, m)), whole((p, p))], scratch=[VMEM((p, m), BF16)], flops=8 * p * m * m, name="primal_columns",
    )


def coarse_cut(place, crow):
    p, total = crow.shape
    width = total // (NZ * NY)

    def body(place_ref, c_ref, *refs):
        z, y = place_ref[0], place_ref[1]
        for k in range(NY):
            for j in range(NZ):
                at = (lax.rem(z + j, NZ) * NY + lax.rem(y + NY - k, NY)) * width
                refs[k][:, j * width:(j + 1) * width] = c_ref[:, pl.ds(pl.multiple_of(at, width), width)]

    return call(body, [out(p, NZ * width)] * NY, [place, crow],
                in_specs=[pl.BlockSpec(memory_space=SMEM), pl.BlockSpec(memory_space=VMEM)], name="coarse_cut")


def column(row, p):
    return jnp.transpose(jnp.broadcast_to(row, (128, 128)))[:p]


def sweep(ref, cols, loc, p, r):
    loc[0] = jnp.zeros((p, r), F32)
    for j in range(NX):
        for b in range(r // 128):
            lanes = slice(b * 128, (b + 1) * 128)
            loc[j + 1, :, lanes] = ref[j, :p, lanes] + cols[j] * loc[j, :, lanes]


def first_half(place, pieces, p):
    rows, r = pieces[0].shape

    def body(place_ref, a, b, c, d, send_ref, own_ref, low_ref, high_ref, v_ref, col_ref, q, loc, pv):
        h, x = place_ref[2], place_ref[3]
        for k, ref in enumerate((a, b, c, d)):
            q[lax.rem(x + k, NX)] = ref[...]
        pv[0] = jnp.ones((p, 128), F32)
        for j in range(NX):
            col_ref[j] = column(q[j, p:p + 1, :128], p)
            pv[j + 1] = pv[j] * col_ref[j]
        pv[NX + 1] = jnp.zeros((p, 128), F32)
        sweep(q, col_ref, loc, p, r)
        loc[NX + 1] = jnp.zeros((p, r), F32)
        upper = h == 1
        own_ref[...], low_ref[...], high_ref[...] = loc[x + 1], loc[x], loc[x + 2]
        for n, at in enumerate((x + 1, x, x + 2)):
            v_ref[n] = jnp.where(upper, pv[at], jnp.zeros((p, 128), F32))
        send_ref[:p] = jnp.where(upper, q[0, :p], loc[NX])
        send_ref[p:] = q[0, p:]

    return call(
        body, [out(rows, r)] + [out(p, r)] * 3 + [out(3, p, 128), out(NX, p, 128)], [place, *pieces],
        in_specs=[pl.BlockSpec(memory_space=SMEM)] + [pl.BlockSpec(memory_space=VMEM)] * 4,
        scratch=[VMEM((NX, rows, r), F32), VMEM((NX + 2, p, r), F32), VMEM((NX + 2, p, 128), F32)], name="first_half",
    )


def first_chains(place, over, own, low, high, v):
    p, r = own.shape

    def body(place_ref, over_ref, a, b, c, v_ref, ao, bo, co):
        last = jnp.logical_and(place_ref[2] == 0, place_ref[3] == NX - 1)
        rate = column(over_ref[p:p + 1, :128], p)
        for k in range(r // 128):
            lanes = slice(k * 128, (k + 1) * 128)
            came = over_ref[:p, lanes]
            ao[:, lanes] = a[:, lanes] + v_ref[0] * came
            bo[:, lanes] = b[:, lanes] + v_ref[1] * came
            co[:, lanes] = jnp.where(last, came + rate * a[:, lanes], c[:, lanes] + v_ref[2] * came)

    return call(body, [out(p, r)] * 3, [place, over, own, low, high, v],
                in_specs=[pl.BlockSpec(memory_space=SMEM)] + [pl.BlockSpec(memory_space=VMEM)] * 5, name="first_chains")


def second_half(place, pieces, cols):
    p, r = pieces[0].shape

    def body(place_ref, a, b, c, d, col_ref, send_ref, own_ref, q, loc):
        x = place_ref[3]
        for k, ref in enumerate((a, b, c, d)):
            q[lax.rem(x + k, NX)] = ref[...]
        sweep(q, col_ref, loc, p, r)
        own_ref[...] = loc[x + 1]
        send_ref[...] = loc[NX]

    return call(body, [out(p, r)] * 2, [place, *pieces, cols],
                in_specs=[pl.BlockSpec(memory_space=SMEM)] + [pl.BlockSpec(memory_space=VMEM)] * 5,
                scratch=[VMEM((NX, p, r), F32), VMEM((NX + 1, p, r), F32)], name="second_half")


def local(residual_in, neumann, dirichlet, coarse, decay, face_rows, primal):
    r0 = residual_in[0, 0]
    nmat = neumann[0, 0]
    dmat = dirichlet[0, 0]
    crow = coarse[0]
    dec = decay[0, 0]
    fr = face_rows[0]
    pr = primal[0, 0]
    m, r = r0.shape
    face = m // 4
    p = pr.shape[0]
    gx = lax.axis_index("gx")
    gy = lax.axis_index("gy")
    h, x = gx // NX, gx % NX
    z, y, c = gy // (NY * NC), (gy // NC) % NY, gy % NC
    flags = jnp.stack([gx > 0, gx < GX - 1, gy > 0, gy < GY - 1]).astype(F32)
    core = c.reshape(1).astype(jnp.int32)
    place = jnp.stack([z, y, h, x]).astype(jnp.int32)

    def exchange(blocks):
        return [ring(blocks[1], "gx", 1), ring(blocks[0], "gx", -1), ring(blocks[3], "gy", 1), ring(blocks[2], "gy", -1)]

    faces0 = gather_faces(fr, r0)
    cut = coarse_cut(place, after(crow, faces0))
    cblk = [cut[0]] + [pull_y(cut[k], k) for k in range(1, NY)]
    recv0 = exchange(faces0)
    prow = jnp.pad(pr, (0, 128 - p))[None]
    prow = after(prow, cblk)
    npr, nprf, nprr = primal_rows(prow, nmat, fr, r0, p)
    dpt, dptf, g_own = primal_columns(prow, dmat, fr, npr)
    dec_rows = jnp.pad(dec[None], ((0, 7), (0, r - p)))

    def spread(cvec):
        return [cvec] + [pull_z(cvec, k) for k in range(1, NZ)]

    def product(own, gate, blk):
        own = after(own, *gate)
        twin = [pull_core(v) for v in own]
        return coarse_product(core, blk, [b for pair in zip(own, twin) for b in pair])

    def summed(part):
        total = part[0]
        for k in range(1, NY):
            total = total + pull_y(part[k], NY - k)
        return total

    cvec0 = first_cvec(flags, nprr, nprf, recv0)
    own0 = spread(cvec0)
    recv_g, fr_g, dpt, dptf, g_own = after((recv0, fr, dpt, dptf, g_own), cvec0)
    jump0, work0 = scatter_neumann(flags, fr_g, r0, recv_g, nmat)
    part0 = product(own0, [work0], cblk)
    work_g = after(work0, part0)
    dw0, base, packed = dirichlet_gather(fr, work_g, jump0, dmat, dptf)
    got = [ring(packed[1], "gx", 1), ring(packed[0], "gx", -1)]
    cq0 = jnp.concatenate([summed(part0), dec_rows], axis=0)
    cq0 = after(cq0, packed)
    pieces = [cq0] + [pull_x(cq0, k) for k in range(1, NX)]
    send, own, low, high, v, cols = first_half(place, pieces, p)
    plain, base_part = column_faces(after(fr, cq0), base, npr)
    over = pull_half(send)
    v_late = after(v, got, plain)
    chain0, low, high = first_chains(place, over, own, low, high, v_late)
    cols_r = chain_faces(plain, dptf, chain0)
    got_y = [ring(cols_r[1], "gy", 1), ring(cols_r[0], "gy", -1)]
    chains = [chain0, low, high]
    cbase, gmat = couplings(flags, nprf, got, base_part, g_own)
    cvec1 = next_cvec(flags, cbase, gmat, chains, nprf, got_y)

    own1 = spread(cvec1)
    fr_h = after(fr, cvec1)
    jump1, dc0, work1 = second_neumann(flags, fr_h, base, got + got_y, dpt, chains, nmat)
    part1 = product(own1, [work1], cblk)
    work1 = after(work1, part1)
    sol, res = second_dirichlet(work1, jump1, dw0, dc0, dmat)
    cq1 = after(summed(part1), res)
    pieces = [cq1] + [pull_x(cq1, k) for k in range(1, NX)]
    send, own = second_half(place, pieces, cols)
    solution, residual = last_update(dpt, own, pull_half(send), v, sol, res)
    return (solution[None, None], residual[None, None])


def solution(mesh):
    lead = P("gx", "gy", None, None)
    vec = P("gx", "gy", None)
    return jax.shard_map(
        local,
        mesh=mesh,
        in_specs=(lead, lead, lead, vec, vec, vec, vec),
        out_specs=(lead, lead),
        check_vma=False,
    )
```

```python
import math

import jax
import jax.numpy as jnp
from jax import lax
from jax.experimental import pallas as pl
from jax.experimental.pallas import tpu as pltpu
from jax.sharding import PartitionSpec as P

NZ, NY, NC, NX, NH = 4, 4, 2, 4, 2
GY = NZ * NY * NC
GX = NX * NH
F32, BF16 = jnp.float32, jnp.bfloat16
COST = 1
GRANT = 20 * 2**20
VMEM, SMEM = pltpu.VMEM, pltpu.SMEM
NN, NT, TN = ((1,), (0,)), ((1,), (1,)), ((0,), (0,))


def gy_index(z, y, c):
    return (z * NY + y) * NC + c


def pull_y(v, k):
    return lax.ppermute(v, "gy", [(gy_index(z, (y + k) % NY, c), gy_index(z, y, c)) for z in range(NZ) for y in range(NY) for c in range(NC)])


def pull_z(v, k):
    return lax.ppermute(v, "gy", [(gy_index((z + k) % NZ, y, c), gy_index(z, y, c)) for z in range(NZ) for y in range(NY) for c in range(NC)])


def pull_core(v):
    return lax.ppermute(v, "gy", [(i, i ^ 1) for i in range(GY)])


def pull_x(v, k):
    return lax.ppermute(v, "gx", [(h * NX + (x + k) % NX, h * NX + x) for h in range(NH) for x in range(NX)])


def pull_half(v):
    return lax.ppermute(v, "gx", [(i, (i + NX) % GX) for i in range(GX)])


def ring(v, axis, by):
    n = GX if axis == "gx" else GY
    return lax.ppermute(v, axis, [(i, (i + by) % n) for i in range(n)])


def dot(a, b, dims=NN):
    return lax.dot_general(a, b, (dims, ((), ())), precision=lax.Precision.HIGH, preferred_element_type=F32)


def one_pass(a, b, dims):
    return lax.dot_general(a, b, (dims, ((), ())), preferred_element_type=F32)


def halves(v):
    hi = v.astype(BF16)
    return hi, (v - hi.astype(F32)).astype(BF16)


def three(a, b, dims=NN):
    ah, al = a if isinstance(a, tuple) else halves(a)
    bh, bl = b if isinstance(b, tuple) else halves(b)
    return one_pass(ah, bh, dims) + (one_pass(ah, bl, dims) + one_pass(al, bh, dims))


def after(values, *earlier):
    return lax.optimization_barrier((values, earlier))[0]


def call(body, outs, ins, *, grid=None, in_specs=None, out_specs=None, scratch=(), flops=0, name=None):
    whole = pl.BlockSpec(memory_space=VMEM)
    nbytes = sum(4 * v.size for v in ins) + sum(4 * math.prod(o.shape) for o in outs)
    kwargs = {} if grid is None else {"grid": grid}
    return pl.pallas_call(
        body,
        out_shape=outs,
        in_specs=in_specs or [whole] * len(ins),
        out_specs=out_specs or [whole] * len(outs),
        scratch_shapes=list(scratch),
        compiler_params=pltpu.CompilerParams(vmem_limit_bytes=GRANT),
        cost_estimate=pl.CostEstimate(flops=flops // COST, bytes_accessed=nbytes // COST, transcendentals=0),
        name=name,
        **kwargs,
    )(*ins)


def in_hbm(v):
    return pltpu.with_memory_space_constraint(v, pltpu.HBM)


def out(*shape):
    return jax.ShapeDtypeStruct(shape, F32)


def perm_block(fr_ref, at, face):
    m = fr_ref.shape[1]
    blocks = []
    for j in range(face // 128):
        ids = fr_ref[:, pl.ds(pl.multiple_of(at + j * 128, 128), 128)].astype(F32)
        ids = jnp.transpose(jnp.broadcast_to(ids, (128, 128)))
        lane = lax.broadcasted_iota(jnp.int32, (128, 128), 1).astype(F32)
        blocks.append(jnp.concatenate([(ids == lane + 128.0 * i).astype(F32).astype(BF16) for i in range(m // 128)], axis=1))
    return jnp.concatenate(blocks, axis=0)


def scatter_block(fr_ref, at, rows):
    m = fr_ref.shape[1]
    ids = lax.broadcasted_iota(jnp.int32, (rows, m), 0) + at
    return (ids == fr_ref[...]).astype(F32).astype(BF16)


def gather_faces(fr, v):
    m, r = v.shape
    face = m // 4

    def body(fr_ref, v_ref, *refs):
        outs, (hi, lo) = refs[:4], refs[4:]
        hi[...], lo[...] = halves(v_ref[...])
        for k in range(4):
            pb = perm_block(fr_ref, k * face, face)
            outs[k][...] = one_pass(pb, hi[...], NN) + one_pass(pb, lo[...], NN)

    return call(body, [out(face, r)] * 4, [fr, v], scratch=[VMEM((m, r), BF16)] * 2, flops=4 * m * m * r, name="gather_faces")


def scatter_neumann(flags, fr, v, recv, nmat):
    m, r = v.shape
    face = m // 4
    step = 256

    def body(flags_ref, fr_ref, v_ref, a_ref, b_ref, c_ref, d_ref, n_ref, jump_ref, work_ref, hi, lo, fh, fl):
        i = pl.program_id(0)

        @pl.when(i == 0)
        def _():
            for k, ref in enumerate((a_ref, b_ref, c_ref, d_ref)):
                fh[k * face:(k + 1) * face], fl[k * face:(k + 1) * face] = halves(ref[...] * flags_ref[k])

            @pl.loop(0, m // step)
            def _(j):
                rows = pl.ds(pl.multiple_of(j * step, step), step)
                sb = scatter_block(fr_ref, j * step, step)
                jump = v_ref[rows, :] - (one_pass(sb, fh[...], NN) + one_pass(sb, fl[...], NN))
                jump_ref[rows, :] = jump
                hi[rows, :], lo[rows, :] = halves(jump)

        work_ref[...] = three(n_ref[...], (hi[...], lo[...]))

    whole = lambda shape: pl.BlockSpec(shape, lambda i: (0, 0), pipeline_mode=pl.Buffered(1))
    return call(
        body, [pltpu.HBM((m, r), F32)] * 2, [flags, fr, v, *recv, nmat], grid=(m // step,),
        in_specs=[pl.BlockSpec(memory_space=SMEM), whole(fr.shape), whole(v.shape)] + [whole((face, r))] * 4 + [pl.BlockSpec((step, m), lambda i: (i, 0))],
        out_specs=[whole((m, r)), pl.BlockSpec((step, r), lambda i: (i, 0))],
        scratch=[VMEM((m, r), BF16)] * 4, flops=10 * m * m * r, name="scatter_neumann",
    )


def dirichlet_gather(fr, work, jump, dmat, dptf):
    m, r = work.shape
    face, p = m // 4, dptf.shape[0]
    step = 256

    def body(fr_ref, w_ref, j_ref, d_ref, t_ref, dw_ref, base_ref, a_ref, b_ref, hi, lo):
        i = pl.program_id(0)

        @pl.when(i == 0)
        def _():
            hi[...], lo[...] = halves(w_ref[...])

        rows = pl.ds(pl.multiple_of(i * step, step), step)
        dw = three(d_ref[...], (hi[...], lo[...]))
        dw_ref[rows, :] = dw
        base_ref[rows, :] = j_ref[...] - 0.5 * dw

        @pl.when(i == m // step - 1)
        def _():
            hi[...], lo[...] = halves(base_ref[...])
            for k, ref in enumerate((a_ref, b_ref)):
                pb = perm_block(fr_ref, k * face, face)
                ref[:face] = one_pass(pb, hi[...], NN) + one_pass(pb, lo[...], NN)
                ref[face:] = t_ref[:, k * face:(k + 1) * face]

    whole = lambda shape: pl.BlockSpec(shape, lambda i: (0, 0), pipeline_mode=pl.Buffered(1))
    res = call(
        body, [out(m, r), out(m, r)] + [out(face + p, r)] * 2, [fr, in_hbm(work), in_hbm(jump), dmat, dptf], grid=(m // step,),
        in_specs=[whole(fr.shape), whole((m, r)), pl.BlockSpec((step, r), lambda i: (i, 0)), pl.BlockSpec((step, m), lambda i: (i, 0)), whole(dptf.shape)],
        out_specs=[whole((m, r))] * 2 + [whole((face + p, r))] * 2,
        scratch=[VMEM((m, r), BF16)] * 2, flops=10 * m * m * r, name="dirichlet_gather",
    )
    return res[0], res[1], res[2:]


def column_faces(fr, base, npr):
    m, r = base.shape
    face, p = m // 4, npr.shape[0]

    def body(fr_ref, b_ref, n_ref, a_ref, c_ref, o_ref):
        both = halves(b_ref[...])
        for k, ref in enumerate((a_ref, c_ref)):
            pb = perm_block(fr_ref, (k + 2) * face, face)
            ref[...] = one_pass(pb, both[0], NN) + one_pass(pb, both[1], NN)
        o_ref[...] = three(n_ref[...], both)

    res = call(body, [out(face, r)] * 2 + [out(p, r)], [fr, base, npr], flops=2 * m * m * r, name="column_faces")
    return res[:2], res[2]


def first_cvec(flags, nprr, nprf, recv):
    p, r = nprr.shape
    face = recv[0].shape[0]

    def body(flags_ref, b_ref, *refs):
        total = b_ref[...]
        for k in range(4):
            total = total - flags_ref[k] * three(refs[4 + k][...], refs[k][...])
        refs[8][...] = total

    return call(body, [out(p, r)], [flags, nprr, *recv, *nprf], in_specs=[pl.BlockSpec(memory_space=SMEM)] + [pl.BlockSpec(memory_space=VMEM)] * 9,
                flops=6 * p * 4 * face * r, name="first_cvec")[0]


def coarse_product(core, cblk, blocks):
    width = cblk[0].shape[1]
    p, r = blocks[0].shape
    rows = NZ * p

    def body(core_ref, c0, c1, c2, c3, *refs):
        ins, outs, (hi, lo, ch, cl) = refs[:len(blocks)], refs[len(blocks):len(blocks) + NZ], refs[len(blocks) + NZ:]
        for k, ref in enumerate((c0, c1, c2, c3)):
            ch[k * p:(k + 1) * p], cl[k * p:(k + 1) * p] = halves(ref[...])
        second = core_ref[0] == 1
        for k in range(NY):
            a, b = halves(ins[2 * k][...]), halves(ins[2 * k + 1][...])
            for ref, u, w in zip((hi, lo), a, b):
                u, w = u.astype(F32), w.astype(F32)
                ref[2 * k * p:(2 * k + 1) * p] = jnp.where(second, w, u).astype(BF16)
                ref[(2 * k + 1) * p:(2 * k + 2) * p] = jnp.where(second, u, w).astype(BF16)
        total = three((ch[...], cl[...]), (hi[...], lo[...]))
        for k in range(NZ):
            outs[k][...] = total[k * p:(k + 1) * p]

    return call(body, [out(p, r)] * NZ, [core, *cblk, *blocks],
                in_specs=[pl.BlockSpec(memory_space=SMEM)] + [pl.BlockSpec(memory_space=VMEM)] * (NZ + len(blocks)),
                scratch=[VMEM((width, r), BF16)] * 2 + [VMEM((rows, width), BF16)] * 2, flops=6 * rows * width * r, name="coarse_product")


def couplings(flags, nprf, got, base_part, own):
    p, r = base_part.shape
    face = nprf[0].shape[1]

    def body(flags_ref, b_ref, o_ref, na, nb, a, b, total_ref, g_ref):
        total = b_ref[...]
        g_ref[0] = -0.5 * o_ref[...]
        for k, (n, ref) in enumerate(((na, a), (nb, b))):
            nk = halves(n[...])
            total = total - flags_ref[k] * three(nk, ref[:face])
            g_ref[k + 1] = (0.5 * flags_ref[k]) * three(nk, ref[face:], NT)
        total_ref[...] = total

    return call(body, [out(p, r), out(3, p, p)], [flags, base_part, own, *nprf[:2], *got],
                in_specs=[pl.BlockSpec(memory_space=SMEM)] + [pl.BlockSpec(memory_space=VMEM)] * 6,
                flops=12 * p * (face + p) * r, name="couplings")


def chain_faces(faces, dptf, chain):
    face, r = faces[0].shape

    def body(t_ref, c_ref, a, b, ao, bo):
        ch = halves(c_ref[...])
        for k, (ref, o) in enumerate(((a, ao), (b, bo))):
            o[...] = ref[...] - 0.5 * three(halves(t_ref[:, (k + 2) * face:(k + 3) * face]), ch, TN)

    return call(body, [out(face, r)] * 2, [dptf, chain, *faces], flops=12 * chain.shape[0] * face * r, name="chain_faces")


def next_cvec(flags, cbase, gmat, chains, nprf, got):
    p, r = cbase.shape

    def body(flags_ref, c_ref, g_ref, c0, c1, c2, n2, n3, a, b, o_ref):
        total = c_ref[...]
        for k, ref in enumerate((c0, c1, c2)):
            total = total + three(g_ref[k], ref[...])
        for k, (n, ref) in enumerate(((n2, a), (n3, b))):
            total = total - flags_ref[k + 2] * three(n[...], ref[...])
        o_ref[...] = total

    return call(body, [out(p, r)], [flags, cbase, gmat, *chains, *nprf[2:], *got],
                in_specs=[pl.BlockSpec(memory_space=SMEM)] + [pl.BlockSpec(memory_space=VMEM)] * 9, flops=40 * p * p * r, name="next_cvec")[0]


def second_neumann(flags, fr, base, got, dpt, chains, nmat):
    m, r = base.shape
    p = dpt.shape[0]
    face = m // 4
    step = 256

    def body(flags_ref, fr_ref, v_ref, a_ref, b_ref, c_ref, d_ref, t_ref, own_ref, q0, q1, n_ref, jump_ref, dc_ref, work_ref, hi, lo, fh, fl):
        i = pl.program_id(0)

        @pl.when(i == 0)
        def _():
            for k, (ref, q) in enumerate(zip((a_ref, b_ref, c_ref, d_ref), (q0, q1, None, None))):
                got_k = ref[...] if q is None else ref[:face] - 0.5 * three(ref[face:], q[...], TN)
                fh[k * face:(k + 1) * face], fl[k * face:(k + 1) * face] = halves(got_k * flags_ref[k])
                rows = slice(k * face, (k + 1) * face)
                dc_ref[rows, :] = three(t_ref[:, rows], own_ref[...], TN)

            @pl.loop(0, m // step)
            def _(j):
                rows = pl.ds(pl.multiple_of(j * step, step), step)
                sb = scatter_block(fr_ref, j * step, step)
                jump = v_ref[rows, :] - 0.5 * dc_ref[rows, :] - (one_pass(sb, fh[...], NN) + one_pass(sb, fl[...], NN))
                jump_ref[rows, :] = jump
                hi[rows, :], lo[rows, :] = halves(jump)

        work_ref[...] = three(n_ref[...], (hi[...], lo[...]))

    whole = lambda shape: pl.BlockSpec(shape, lambda i: (0, 0), pipeline_mode=pl.Buffered(1))
    return call(
        body, [out(m, r)] * 3, [flags, fr, base, *got, dpt, *chains, nmat], grid=(m // step,),
        in_specs=[pl.BlockSpec(memory_space=SMEM), whole(fr.shape), whole(base.shape)] + [whole(g.shape) for g in got] + [whole(dpt.shape)]
        + [whole((p, r))] * 3 + [pl.BlockSpec((step, m), lambda i: (i, 0))],
        out_specs=[whole((m, r)), whole((m, r)), pl.BlockSpec((step, r), lambda i: (i, 0))],
        scratch=[VMEM((m, r), BF16)] * 4, flops=11 * m * m * r, name="second_neumann",
    )


def second_dirichlet(work, jump, dw, dc, dmat):
    m, r = work.shape
    step = 256

    def body(w_ref, j_ref, p_ref, c_ref, d_ref, s_ref, r_ref, hi, lo):
        @pl.when(pl.program_id(0) == 0)
        def _():
            hi[...], lo[...] = halves(w_ref[...])

        dw1 = three(d_ref[...], (hi[...], lo[...]))
        s_ref[...] = p_ref[...] + c_ref[...] + dw1
        r_ref[...] = j_ref[...] - 0.5 * dw1

    blk = pl.BlockSpec((step, r), lambda i: (i, 0))
    return call(
        body, [out(m, r)] * 2, [work, jump, dw, dc, dmat], grid=(m // step,),
        in_specs=[pl.BlockSpec((m, r), lambda i: (0, 0), pipeline_mode=pl.Buffered(1)), blk, blk, blk, pl.BlockSpec((step, m), lambda i: (i, 0))],
        out_specs=[blk, blk], scratch=[VMEM((m, r), BF16)] * 2, flops=6 * m * m * r, name="second_dirichlet",
    )


def last_update(dpt, own, over, v, sol, res):
    p, m = dpt.shape
    r = own.shape[1]
    step = 512

    def body(t_ref, a_ref, o_ref, v_ref, s_ref, r_ref, so_ref, ro_ref, hi, lo):
        @pl.when(pl.program_id(0) == 0)
        def _():
            for k in range(r // 128):
                lanes = slice(k * 128, (k + 1) * 128)
                hi[:, lanes], lo[:, lanes] = halves(a_ref[:, lanes] + v_ref[0] * o_ref[:, lanes])

        u = three(t_ref[...], (hi[...], lo[...]), TN)
        so_ref[...] = s_ref[...] + u
        ro_ref[...] = r_ref[...] - 0.5 * u

    blk = pl.BlockSpec((step, r), lambda i: (i, 0))
    small = pl.BlockSpec((p, r), lambda i: (0, 0))
    return call(
        body, [out(m, r)] * 2, [dpt, own, over, v, sol, res], grid=(m // step,),
        in_specs=[pl.BlockSpec((p, step), lambda i: (0, i)), small, small, pl.BlockSpec(v.shape, lambda i: (0, 0, 0)), blk, blk],
        out_specs=[blk, blk], scratch=[VMEM((p, r), BF16)] * 2, flops=6 * m * p * r, name="last_update",
    )


def one_hot_rows(pr_ref, sel, p, m):
    ids = jnp.transpose(jnp.broadcast_to(pr_ref[...].astype(F32), (128, 128)))[:p]
    lane = lax.broadcasted_iota(jnp.int32, (p, 128), 1).astype(F32)
    for k in range(m // 128):
        sel[:, k * 128:(k + 1) * 128] = (ids == lane + 128.0 * k).astype(F32).astype(BF16)


def primal_rows(prow, nmat, fr, r0, p):
    m, r = r0.shape
    face = m // 4
    step = 256

    def body(pr_ref, n_ref, fr_ref, r_ref, rows_ref, a_ref, b_ref, c_ref, d_ref, prod_ref, sel):
        i = pl.program_id(0)

        @pl.when(i == 0)
        def _():
            one_hot_rows(pr_ref, sel, p, m)
            rows_ref[...] = jnp.zeros((p, m), F32)

        nh, nl = halves(n_ref[...])
        pick = sel[:, pl.ds(pl.multiple_of(i * step, step), step)]
        rows_ref[...] += one_pass(pick, nh, NN) + one_pass(pick, nl, NN)

        @pl.when(i == m // step - 1)
        def _():
            both = halves(rows_ref[...])
            for k, ref in enumerate((a_ref, b_ref, c_ref, d_ref)):
                ids = lax.broadcasted_iota(jnp.int32, (m, face), 0)
                sb = (ids == fr_ref[:, k * face:(k + 1) * face]).astype(F32).astype(BF16)
                ref[...] = one_pass(both[0], sb, NN) + one_pass(both[1], sb, NN)
            prod_ref[...] = three(both, r_ref[...])

    whole = lambda shape: pl.BlockSpec(shape, lambda i: (0, 0), pipeline_mode=pl.Buffered(1))
    res = call(
        body, [out(p, m)] + [out(p, face)] * 4 + [out(p, r)], [prow, nmat, fr, r0], grid=(m // step,),
        in_specs=[whole(prow.shape), pl.BlockSpec((step, m), lambda i: (i, 0)), whole(fr.shape), whole(r0.shape)],
        out_specs=[whole((p, m))] + [whole((p, face))] * 4 + [whole((p, r))], scratch=[VMEM((p, m), BF16)],
        flops=8 * p * m * m, name="primal_rows",
    )
    return res[0], res[1:5], res[5]


def primal_columns(prow, dmat, fr, npr):
    m = dmat.shape[0]
    p = npr.shape[0]
    step = 256

    def body(pr_ref, d_ref, fr_ref, n_ref, t_ref, f_ref, g_ref, sel):
        i = pl.program_id(0)

        @pl.when(i == 0)
        def _():
            one_hot_rows(pr_ref, sel, p, m)

        dh, dl = halves(d_ref[...])
        t_ref[:, pl.ds(pl.multiple_of(i * step, step), step)] = one_pass(sel[...], dh, NT) + one_pass(sel[...], dl, NT)

        @pl.when(i == m // step - 1)
        def _():
            both = halves(t_ref[...])
            for k in range(m // step):
                cols = slice(k * step, (k + 1) * step)
                ids = lax.broadcasted_iota(jnp.int32, (m, step), 0)
                sb = (ids == fr_ref[:, cols]).astype(F32).astype(BF16)
                f_ref[:, cols] = one_pass(both[0], sb, NN) + one_pass(both[1], sb, NN)
            g_ref[...] = three(n_ref[...], both, NT)

    whole = lambda shape: pl.BlockSpec(shape, lambda i: (0, 0), pipeline_mode=pl.Buffered(1))
    return call(
        body, [out(p, m), out(p, m), out(p, p)], [prow, dmat, fr, npr], grid=(m // step,),
        in_specs=[whole(prow.shape), pl.BlockSpec((step, m), lambda i: (i, 0)), whole(fr.shape), whole(npr.shape)],
        out_specs=[whole((p, m)), whole((p, m)), whole((p, p))], scratch=[VMEM((p, m), BF16)], flops=8 * p * m * m, name="primal_columns",
    )


def coarse_cut(place, crow):
    p, total = crow.shape
    width = total // (NZ * NY)

    def body(place_ref, c_ref, *refs):
        z, y = place_ref[0], place_ref[1]
        for k in range(NY):
            for j in range(NZ):
                at = (lax.rem(z + j, NZ) * NY + lax.rem(y + NY - k, NY)) * width
                refs[k][:, j * width:(j + 1) * width] = c_ref[:, pl.ds(pl.multiple_of(at, width), width)]

    return call(body, [out(p, NZ * width)] * NY, [place, crow],
                in_specs=[pl.BlockSpec(memory_space=SMEM), pl.BlockSpec(memory_space=VMEM)], name="coarse_cut")


def column(row, p):
    return jnp.transpose(jnp.broadcast_to(row, (128, 128)))[:p]


def sweep(ref, cols, loc, p, r):
    loc[0] = jnp.zeros((p, r), F32)
    for j in range(NX):
        for b in range(r // 128):
            lanes = slice(b * 128, (b + 1) * 128)
            loc[j + 1, :, lanes] = ref[j, :p, lanes] + cols[j] * loc[j, :, lanes]


def first_half(place, pieces, p):
    rows, r = pieces[0].shape

    def body(place_ref, a, b, c, d, send_ref, own_ref, low_ref, high_ref, v_ref, col_ref, q, loc, pv):
        h, x = place_ref[2], place_ref[3]
        for k, ref in enumerate((a, b, c, d)):
            q[lax.rem(x + k, NX)] = ref[...]
        pv[0] = jnp.ones((p, 128), F32)
        for j in range(NX):
            col_ref[j] = column(q[j, p:p + 1, :128], p)
            pv[j + 1] = pv[j] * col_ref[j]
        pv[NX + 1] = jnp.zeros((p, 128), F32)
        sweep(q, col_ref, loc, p, r)
        loc[NX + 1] = jnp.zeros((p, r), F32)
        upper = h == 1
        own_ref[...], low_ref[...], high_ref[...] = loc[x + 1], loc[x], loc[x + 2]
        for n, at in enumerate((x + 1, x, x + 2)):
            v_ref[n] = jnp.where(upper, pv[at], jnp.zeros((p, 128), F32))
        send_ref[:p] = jnp.where(upper, q[0, :p], loc[NX])
        send_ref[p:] = q[0, p:]

    return call(
        body, [out(rows, r)] + [out(p, r)] * 3 + [out(3, p, 128), out(NX, p, 128)], [place, *pieces],
        in_specs=[pl.BlockSpec(memory_space=SMEM)] + [pl.BlockSpec(memory_space=VMEM)] * 4,
        scratch=[VMEM((NX, rows, r), F32), VMEM((NX + 2, p, r), F32), VMEM((NX + 2, p, 128), F32)], name="first_half",
    )


def first_chains(place, over, own, low, high, v):
    p, r = own.shape

    def body(place_ref, over_ref, a, b, c, v_ref, ao, bo, co):
        last = jnp.logical_and(place_ref[2] == 0, place_ref[3] == NX - 1)
        rate = column(over_ref[p:p + 1, :128], p)
        for k in range(r // 128):
            lanes = slice(k * 128, (k + 1) * 128)
            came = over_ref[:p, lanes]
            ao[:, lanes] = a[:, lanes] + v_ref[0] * came
            bo[:, lanes] = b[:, lanes] + v_ref[1] * came
            co[:, lanes] = jnp.where(last, came + rate * a[:, lanes], c[:, lanes] + v_ref[2] * came)

    return call(body, [out(p, r)] * 3, [place, over, own, low, high, v],
                in_specs=[pl.BlockSpec(memory_space=SMEM)] + [pl.BlockSpec(memory_space=VMEM)] * 5, name="first_chains")


def second_half(place, pieces, cols):
    p, r = pieces[0].shape

    def body(place_ref, a, b, c, d, col_ref, send_ref, own_ref, q, loc):
        x = place_ref[3]
        for k, ref in enumerate((a, b, c, d)):
            q[lax.rem(x + k, NX)] = ref[...]
        sweep(q, col_ref, loc, p, r)
        own_ref[...] = loc[x + 1]
        send_ref[...] = loc[NX]

    return call(body, [out(p, r)] * 2, [place, *pieces, cols],
                in_specs=[pl.BlockSpec(memory_space=SMEM)] + [pl.BlockSpec(memory_space=VMEM)] * 5,
                scratch=[VMEM((NX, p, r), F32), VMEM((NX + 1, p, r), F32)], name="second_half")


def local(residual_in, neumann, dirichlet, coarse, decay, face_rows, primal):
    r0 = residual_in[0, 0]
    nmat = neumann[0, 0]
    dmat = dirichlet[0, 0]
    crow = coarse[0]
    dec = decay[0, 0]
    fr = face_rows[0]
    pr = primal[0, 0]
    m, r = r0.shape
    face = m // 4
    p = pr.shape[0]
    gx = lax.axis_index("gx")
    gy = lax.axis_index("gy")
    h, x = gx // NX, gx % NX
    z, y, c = gy // (NY * NC), (gy // NC) % NY, gy % NC
    flags = jnp.stack([gx > 0, gx < GX - 1, gy > 0, gy < GY - 1]).astype(F32)
    core = c.reshape(1).astype(jnp.int32)
    place = jnp.stack([z, y, h, x]).astype(jnp.int32)

    def exchange(blocks):
        return [ring(blocks[1], "gx", 1), ring(blocks[0], "gx", -1), ring(blocks[3], "gy", 1), ring(blocks[2], "gy", -1)]

    faces0 = gather_faces(fr, r0)
    cut = coarse_cut(place, after(crow, faces0))
    cblk = [cut[0]] + [pull_y(cut[k], k) for k in range(1, NY)]
    recv0 = exchange(faces0)
    prow = jnp.pad(pr, (0, 128 - p))[None]
    npr, nprf, nprr = primal_rows(prow, nmat, fr, r0, p)
    dpt, dptf, g_own = primal_columns(prow, dmat, fr, npr)
    dec_rows = jnp.pad(dec[None], ((0, 7), (0, r - p)))

    def spread(cvec):
        return [cvec] + [pull_z(cvec, k) for k in range(1, NZ)]

    def product(own, gate, blk):
        own = after(own, *gate)
        twin = [pull_core(v) for v in own]
        return coarse_product(core, blk, [b for pair in zip(own, twin) for b in pair])

    def summed(part):
        total = part[0]
        for k in range(1, NY):
            total = total + pull_y(part[k], NY - k)
        return total

    cvec0 = first_cvec(flags, after(nprr, cblk), nprf, recv0)
    own0 = spread(cvec0)
    recv_g, fr_g, dpt, dptf, g_own = after((recv0, fr, dpt, dptf, g_own), cvec0)
    jump0, work0 = scatter_neumann(flags, fr_g, r0, recv_g, nmat)
    part0 = product(own0, [work0], cblk)
    work_g = after(work0, part0)
    dw0, base, packed = dirichlet_gather(fr, work_g, jump0, dmat, dptf)
    got = [ring(packed[1], "gx", 1), ring(packed[0], "gx", -1)]
    cq0 = jnp.concatenate([summed(part0), dec_rows], axis=0)
    cq0 = after(cq0, packed)
    pieces = [cq0] + [pull_x(cq0, k) for k in range(1, NX)]
    send, own, low, high, v, cols = first_half(place, pieces, p)
    plain, base_part = column_faces(after(fr, cq0), base, npr)
    over = pull_half(send)
    v_late = after(v, got, plain)
    chain0, low, high = first_chains(place, over, own, low, high, v_late)
    cols_r = chain_faces(plain, dptf, chain0)
    got_y = [ring(cols_r[1], "gy", 1), ring(cols_r[0], "gy", -1)]
    chains = [chain0, low, high]
    cbase, gmat = couplings(flags, nprf, got, base_part, g_own)
    cvec1 = next_cvec(flags, cbase, gmat, chains, nprf, got_y)

    own1 = spread(cvec1)
    part1 = product(own1, [], cblk)
    cq1 = summed(part1)
    fr_h = after(fr, cq1)
    jump1, dc0, work1 = second_neumann(flags, fr_h, base, got + got_y, dpt, chains, nmat)
    pieces = [cq1] + [pull_x(cq1, k) for k in range(1, NX)]
    send, own = second_half(place, pieces, after(cols, work1))
    over = pull_half(send)
    work1 = after(work1, send)
    sol, res = second_dirichlet(work1, jump1, dw0, dc0, dmat)
    solution, residual = last_update(dpt, own, over, v, sol, res)
    return (solution[None, None], residual[None, None])


def solution(mesh):
    lead = P("gx", "gy", None, None)
    vec = P("gx", "gy", None)
    return jax.shard_map(
        local,
        mesh=mesh,
        in_specs=(lead, lead, lead, vec, vec, vec, vec),
        out_specs=(lead, lead),
        check_vma=False,
    )
```

```python
import math

import jax
import jax.numpy as jnp
from jax import lax
from jax.experimental import pallas as pl
from jax.experimental.pallas import tpu as pltpu
from jax.sharding import PartitionSpec as P

NZ, NY, NC, NX, NH = 4, 4, 2, 4, 2
GY = NZ * NY * NC
GX = NX * NH
F32, BF16 = jnp.float32, jnp.bfloat16
COST = 1
GRANT = 20 * 2**20
VMEM, SMEM = pltpu.VMEM, pltpu.SMEM
NN, NT, TN = ((1,), (0,)), ((1,), (1,)), ((0,), (0,))


def gy_index(z, y, c):
    return (z * NY + y) * NC + c


def pull_y(v, k):
    return lax.ppermute(v, "gy", [(gy_index(z, (y + k) % NY, c), gy_index(z, y, c)) for z in range(NZ) for y in range(NY) for c in range(NC)])


def pull_z(v, k):
    return lax.ppermute(v, "gy", [(gy_index((z + k) % NZ, y, c), gy_index(z, y, c)) for z in range(NZ) for y in range(NY) for c in range(NC)])


def pull_core(v):
    return lax.ppermute(v, "gy", [(i, i ^ 1) for i in range(GY)])


def pull_x(v, k):
    return lax.ppermute(v, "gx", [(h * NX + (x + k) % NX, h * NX + x) for h in range(NH) for x in range(NX)])


def pull_half(v):
    return lax.ppermute(v, "gx", [(i, (i + NX) % GX) for i in range(GX)])


def ring(v, axis, by):
    n = GX if axis == "gx" else GY
    return lax.ppermute(v, axis, [(i, (i + by) % n) for i in range(n)])


def dot(a, b, dims=NN):
    return lax.dot_general(a, b, (dims, ((), ())), precision=lax.Precision.HIGH, preferred_element_type=F32)


def one_pass(a, b, dims):
    return lax.dot_general(a, b, (dims, ((), ())), preferred_element_type=F32)


def halves(v):
    hi = v.astype(BF16)
    return hi, (v - hi.astype(F32)).astype(BF16)


def three(a, b, dims=NN):
    ah, al = a if isinstance(a, tuple) else halves(a)
    bh, bl = b if isinstance(b, tuple) else halves(b)
    return one_pass(ah, bh, dims) + (one_pass(ah, bl, dims) + one_pass(al, bh, dims))


def after(values, *earlier):
    return lax.optimization_barrier((values, earlier))[0]


def call(body, outs, ins, *, grid=None, in_specs=None, out_specs=None, scratch=(), flops=0, name=None):
    whole = pl.BlockSpec(memory_space=VMEM)
    nbytes = sum(4 * v.size for v in ins) + sum(4 * math.prod(o.shape) for o in outs)
    kwargs = {} if grid is None else {"grid": grid}
    return pl.pallas_call(
        body,
        out_shape=outs,
        in_specs=in_specs or [whole] * len(ins),
        out_specs=out_specs or [whole] * len(outs),
        scratch_shapes=list(scratch),
        compiler_params=pltpu.CompilerParams(vmem_limit_bytes=GRANT),
        cost_estimate=pl.CostEstimate(flops=flops // COST, bytes_accessed=nbytes // COST, transcendentals=0),
        name=name,
        **kwargs,
    )(*ins)


def in_hbm(v):
    return pltpu.with_memory_space_constraint(v, pltpu.HBM)


def out(*shape):
    return jax.ShapeDtypeStruct(shape, F32)


def perm_block(fr_ref, at, face):
    m = fr_ref.shape[1]
    blocks = []
    for j in range(face // 128):
        ids = fr_ref[:, pl.ds(pl.multiple_of(at + j * 128, 128), 128)].astype(F32)
        ids = jnp.transpose(jnp.broadcast_to(ids, (128, 128)))
        lane = lax.broadcasted_iota(jnp.int32, (128, 128), 1).astype(F32)
        blocks.append(jnp.concatenate([(ids == lane + 128.0 * i).astype(F32).astype(BF16) for i in range(m // 128)], axis=1))
    return jnp.concatenate(blocks, axis=0)


def scatter_block(fr_ref, at, rows):
    m = fr_ref.shape[1]
    ids = lax.broadcasted_iota(jnp.int32, (rows, m), 0) + at
    return (ids == fr_ref[...]).astype(F32).astype(BF16)


def gather_faces(fr, v):
    m, r = v.shape
    face = m // 4

    def body(fr_ref, v_ref, *refs):
        outs, (hi, lo) = refs[:4], refs[4:]
        hi[...], lo[...] = halves(v_ref[...])
        for k in range(4):
            pb = perm_block(fr_ref, k * face, face)
            outs[k][...] = one_pass(pb, hi[...], NN) + one_pass(pb, lo[...], NN)

    return call(body, [out(face, r)] * 4, [fr, v], scratch=[VMEM((m, r), BF16)] * 2, flops=4 * m * m * r, name="gather_faces")


def scatter_neumann(flags, fr, v, recv, nmat):
    m, r = v.shape
    face = m // 4
    step = 256

    def body(flags_ref, fr_ref, v_ref, a_ref, b_ref, c_ref, d_ref, n_ref, jump_ref, work_ref, hi, lo, fh, fl):
        i = pl.program_id(0)

        @pl.when(i == 0)
        def _():
            for k, ref in enumerate((a_ref, b_ref, c_ref, d_ref)):
                fh[k * face:(k + 1) * face], fl[k * face:(k + 1) * face] = halves(ref[...] * flags_ref[k])

            @pl.loop(0, m // step)
            def _(j):
                rows = pl.ds(pl.multiple_of(j * step, step), step)
                sb = scatter_block(fr_ref, j * step, step)
                jump = v_ref[rows, :] - (one_pass(sb, fh[...], NN) + one_pass(sb, fl[...], NN))
                jump_ref[rows, :] = jump
                hi[rows, :], lo[rows, :] = halves(jump)

        work_ref[...] = three(n_ref[...], (hi[...], lo[...]))

    whole = lambda shape: pl.BlockSpec(shape, lambda i: (0, 0), pipeline_mode=pl.Buffered(1))
    return call(
        body, [pltpu.HBM((m, r), F32)] * 2, [flags, fr, v, *recv, nmat], grid=(m // step,),
        in_specs=[pl.BlockSpec(memory_space=SMEM), whole(fr.shape), whole(v.shape)] + [whole((face, r))] * 4 + [pl.BlockSpec((step, m), lambda i: (i, 0))],
        out_specs=[whole((m, r)), pl.BlockSpec((step, r), lambda i: (i, 0))],
        scratch=[VMEM((m, r), BF16)] * 4, flops=10 * m * m * r, name="scatter_neumann",
    )


def dirichlet_gather(fr, work, jump, dmat, dptf, npr):
    m, r = work.shape
    face, p = m // 4, npr.shape[0]
    step = 256

    def body(fr_ref, w_ref, j_ref, d_ref, t_ref, n_ref, dw_ref, base_ref, a_ref, b_ref, c_ref, e_ref, np_ref, hi, lo):
        i = pl.program_id(0)

        @pl.when(i == 0)
        def _():
            hi[...], lo[...] = halves(w_ref[...])

        rows = pl.ds(pl.multiple_of(i * step, step), step)
        dw = three(d_ref[...], (hi[...], lo[...]))
        dw_ref[rows, :] = dw
        base_ref[rows, :] = j_ref[...] - 0.5 * dw

        @pl.when(i == m // step - 1)
        def _():
            hi[...], lo[...] = halves(base_ref[...])
            for k, ref in enumerate((a_ref, b_ref, c_ref, e_ref)):
                pb = perm_block(fr_ref, k * face, face)
                ref[:face] = one_pass(pb, hi[...], NN) + one_pass(pb, lo[...], NN)
                if k < 2:
                    ref[face:] = t_ref[:, k * face:(k + 1) * face]
            np_ref[...] = three(n_ref[...], (hi[...], lo[...]))

    whole = lambda shape: pl.BlockSpec(shape, lambda i: (0, 0), pipeline_mode=pl.Buffered(1))
    res = call(
        body, [out(m, r), out(m, r)] + [out(face + p, r)] * 2 + [out(face, r)] * 2 + [out(p, r)], [fr, in_hbm(work), in_hbm(jump), dmat, dptf, npr], grid=(m // step,),
        in_specs=[whole(fr.shape), whole((m, r)), pl.BlockSpec((step, r), lambda i: (i, 0)), pl.BlockSpec((step, m), lambda i: (i, 0)), whole(dptf.shape), whole(npr.shape)],
        out_specs=[whole((m, r))] * 2 + [whole((face + p, r))] * 2 + [whole((face, r))] * 2 + [whole((p, r))],
        scratch=[VMEM((m, r), BF16)] * 2, flops=10 * m * m * r, name="dirichlet_gather",
    )
    return res[0], res[1], res[2:6], res[6]


def first_cvec(flags, nprr, nprf, recv):
    p, r = nprr.shape
    face = recv[0].shape[0]

    def body(flags_ref, b_ref, *refs):
        total = b_ref[...]
        for k in range(4):
            total = total - flags_ref[k] * three(refs[4 + k][...], refs[k][...])
        refs[8][...] = total

    return call(body, [out(p, r)], [flags, nprr, *recv, *nprf], in_specs=[pl.BlockSpec(memory_space=SMEM)] + [pl.BlockSpec(memory_space=VMEM)] * 9,
                flops=6 * p * 4 * face * r, name="first_cvec")[0]


def coarse_product(core, cblk, blocks):
    width = cblk[0].shape[1]
    p, r = blocks[0].shape
    rows = NZ * p

    def body(core_ref, c0, c1, c2, c3, *refs):
        ins, outs, (hi, lo, ch, cl) = refs[:len(blocks)], refs[len(blocks):len(blocks) + NZ], refs[len(blocks) + NZ:]
        for k, ref in enumerate((c0, c1, c2, c3)):
            ch[k * p:(k + 1) * p], cl[k * p:(k + 1) * p] = halves(ref[...])
        second = core_ref[0] == 1
        for k in range(NY):
            a, b = halves(ins[2 * k][...]), halves(ins[2 * k + 1][...])
            for ref, u, w in zip((hi, lo), a, b):
                u, w = u.astype(F32), w.astype(F32)
                ref[2 * k * p:(2 * k + 1) * p] = jnp.where(second, w, u).astype(BF16)
                ref[(2 * k + 1) * p:(2 * k + 2) * p] = jnp.where(second, u, w).astype(BF16)
        total = three((ch[...], cl[...]), (hi[...], lo[...]))
        for k in range(NZ):
            outs[k][...] = total[k * p:(k + 1) * p]

    return call(body, [out(p, r)] * NZ, [core, *cblk, *blocks],
                in_specs=[pl.BlockSpec(memory_space=SMEM)] + [pl.BlockSpec(memory_space=VMEM)] * (NZ + len(blocks)),
                scratch=[VMEM((width, r), BF16)] * 2 + [VMEM((rows, width), BF16)] * 2, flops=6 * rows * width * r, name="coarse_product")


def couplings(flags, nprf, got, base_part, own):
    p, r = base_part.shape
    face = nprf[0].shape[1]

    def body(flags_ref, b_ref, o_ref, na, nb, a, b, total_ref, g_ref):
        total = b_ref[...]
        g_ref[0] = -0.5 * o_ref[...]
        for k, (n, ref) in enumerate(((na, a), (nb, b))):
            nk = halves(n[...])
            total = total - flags_ref[k] * three(nk, ref[:face])
            g_ref[k + 1] = (0.5 * flags_ref[k]) * three(nk, ref[face:], NT)
        total_ref[...] = total

    return call(body, [out(p, r), out(3, p, p)], [flags, base_part, own, *nprf[:2], *got],
                in_specs=[pl.BlockSpec(memory_space=SMEM)] + [pl.BlockSpec(memory_space=VMEM)] * 6,
                flops=12 * p * (face + p) * r, name="couplings")


def chain_faces(faces, dptf, chain):
    face, r = faces[0].shape

    def body(t_ref, c_ref, a, b, ao, bo):
        ch = halves(c_ref[...])
        for k, (ref, o) in enumerate(((a, ao), (b, bo))):
            o[...] = ref[...] - 0.5 * three(halves(t_ref[:, (k + 2) * face:(k + 3) * face]), ch, TN)

    return call(body, [out(face, r)] * 2, [dptf, chain, *faces], flops=12 * chain.shape[0] * face * r, name="chain_faces")


def next_cvec(flags, cbase, gmat, chains, nprf, got):
    p, r = cbase.shape

    def body(flags_ref, c_ref, g_ref, c0, c1, c2, n2, n3, a, b, o_ref):
        total = c_ref[...]
        for k, ref in enumerate((c0, c1, c2)):
            total = total + three(g_ref[k], ref[...])
        for k, (n, ref) in enumerate(((n2, a), (n3, b))):
            total = total - flags_ref[k + 2] * three(n[...], ref[...])
        o_ref[...] = total

    return call(body, [out(p, r)], [flags, cbase, gmat, *chains, *nprf[2:], *got],
                in_specs=[pl.BlockSpec(memory_space=SMEM)] + [pl.BlockSpec(memory_space=VMEM)] * 9, flops=40 * p * p * r, name="next_cvec")[0]


def second_neumann(flags, fr, base, got, dpt, chains, nmat):
    m, r = base.shape
    p = dpt.shape[0]
    face = m // 4
    step = 256

    def body(flags_ref, fr_ref, v_ref, a_ref, b_ref, c_ref, d_ref, t_ref, own_ref, q0, q1, n_ref, jump_ref, dc_ref, work_ref, hi, lo, fh, fl):
        i = pl.program_id(0)

        @pl.when(i == 0)
        def _():
            for k, (ref, q) in enumerate(zip((a_ref, b_ref, c_ref, d_ref), (q0, q1, None, None))):
                got_k = ref[...] if q is None else ref[:face] - 0.5 * three(ref[face:], q[...], TN)
                fh[k * face:(k + 1) * face], fl[k * face:(k + 1) * face] = halves(got_k * flags_ref[k])
                rows = slice(k * face, (k + 1) * face)
                dc_ref[rows, :] = three(t_ref[:, rows], own_ref[...], TN)

            @pl.loop(0, m // step)
            def _(j):
                rows = pl.ds(pl.multiple_of(j * step, step), step)
                sb = scatter_block(fr_ref, j * step, step)
                jump = v_ref[rows, :] - 0.5 * dc_ref[rows, :] - (one_pass(sb, fh[...], NN) + one_pass(sb, fl[...], NN))
                jump_ref[rows, :] = jump
                hi[rows, :], lo[rows, :] = halves(jump)

        work_ref[...] = three(n_ref[...], (hi[...], lo[...]))

    whole = lambda shape: pl.BlockSpec(shape, lambda i: (0, 0), pipeline_mode=pl.Buffered(1))
    return call(
        body, [out(m, r)] * 3, [flags, fr, base, *got, dpt, *chains, nmat], grid=(m // step,),
        in_specs=[pl.BlockSpec(memory_space=SMEM), whole(fr.shape), whole(base.shape)] + [whole(g.shape) for g in got] + [whole(dpt.shape)]
        + [whole((p, r))] * 3 + [pl.BlockSpec((step, m), lambda i: (i, 0))],
        out_specs=[whole((m, r)), whole((m, r)), pl.BlockSpec((step, r), lambda i: (i, 0))],
        scratch=[VMEM((m, r), BF16)] * 4, flops=11 * m * m * r, name="second_neumann",
    )


def second_dirichlet(work, jump, dw, dc, dmat):
    m, r = work.shape
    step = 256

    def body(w_ref, j_ref, p_ref, c_ref, d_ref, s_ref, r_ref, hi, lo):
        @pl.when(pl.program_id(0) == 0)
        def _():
            hi[...], lo[...] = halves(w_ref[...])

        dw1 = three(d_ref[...], (hi[...], lo[...]))
        s_ref[...] = p_ref[...] + c_ref[...] + dw1
        r_ref[...] = j_ref[...] - 0.5 * dw1

    blk = pl.BlockSpec((step, r), lambda i: (i, 0))
    return call(
        body, [out(m, r)] * 2, [work, jump, dw, dc, dmat], grid=(m // step,),
        in_specs=[pl.BlockSpec((m, r), lambda i: (0, 0), pipeline_mode=pl.Buffered(1)), blk, blk, blk, pl.BlockSpec((step, m), lambda i: (i, 0))],
        out_specs=[blk, blk], scratch=[VMEM((m, r), BF16)] * 2, flops=6 * m * m * r, name="second_dirichlet",
    )


def last_update(dpt, own, over, v, sol, res):
    p, m = dpt.shape
    r = own.shape[1]
    step = 512

    def body(t_ref, a_ref, o_ref, v_ref, s_ref, r_ref, so_ref, ro_ref, hi, lo):
        @pl.when(pl.program_id(0) == 0)
        def _():
            for k in range(r // 128):
                lanes = slice(k * 128, (k + 1) * 128)
                hi[:, lanes], lo[:, lanes] = halves(a_ref[:, lanes] + v_ref[0] * o_ref[:, lanes])

        u = three(t_ref[...], (hi[...], lo[...]), TN)
        so_ref[...] = s_ref[...] + u
        ro_ref[...] = r_ref[...] - 0.5 * u

    blk = pl.BlockSpec((step, r), lambda i: (i, 0))
    small = pl.BlockSpec((p, r), lambda i: (0, 0))
    return call(
        body, [out(m, r)] * 2, [dpt, own, over, v, sol, res], grid=(m // step,),
        in_specs=[pl.BlockSpec((p, step), lambda i: (0, i)), small, small, pl.BlockSpec(v.shape, lambda i: (0, 0, 0)), blk, blk],
        out_specs=[blk, blk], scratch=[VMEM((p, r), BF16)] * 2, flops=6 * m * p * r, name="last_update",
    )


def one_hot_rows(pr_ref, sel, p, m):
    ids = jnp.transpose(jnp.broadcast_to(pr_ref[...].astype(F32), (128, 128)))[:p]
    lane = lax.broadcasted_iota(jnp.int32, (p, 128), 1).astype(F32)
    for k in range(m // 128):
        sel[:, k * 128:(k + 1) * 128] = (ids == lane + 128.0 * k).astype(F32).astype(BF16)


def primal_rows(prow, nmat, fr, r0, p):
    m, r = r0.shape
    face = m // 4
    step = 256

    def body(pr_ref, n_ref, fr_ref, r_ref, rows_ref, a_ref, b_ref, c_ref, d_ref, prod_ref, sel):
        i = pl.program_id(0)

        @pl.when(i == 0)
        def _():
            one_hot_rows(pr_ref, sel, p, m)
            rows_ref[...] = jnp.zeros((p, m), F32)

        nh, nl = halves(n_ref[...])
        pick = sel[:, pl.ds(pl.multiple_of(i * step, step), step)]
        rows_ref[...] += one_pass(pick, nh, NN) + one_pass(pick, nl, NN)

        @pl.when(i == m // step - 1)
        def _():
            both = halves(rows_ref[...])
            for k, ref in enumerate((a_ref, b_ref, c_ref, d_ref)):
                ids = lax.broadcasted_iota(jnp.int32, (m, face), 0)
                sb = (ids == fr_ref[:, k * face:(k + 1) * face]).astype(F32).astype(BF16)
                ref[...] = one_pass(both[0], sb, NN) + one_pass(both[1], sb, NN)
            prod_ref[...] = three(both, r_ref[...])

    whole = lambda shape: pl.BlockSpec(shape, lambda i: (0, 0), pipeline_mode=pl.Buffered(1))
    res = call(
        body, [out(p, m)] + [out(p, face)] * 4 + [out(p, r)], [prow, nmat, fr, r0], grid=(m // step,),
        in_specs=[whole(prow.shape), pl.BlockSpec((step, m), lambda i: (i, 0)), whole(fr.shape), whole(r0.shape)],
        out_specs=[whole((p, m))] + [whole((p, face))] * 4 + [whole((p, r))], scratch=[VMEM((p, m), BF16)],
        flops=8 * p * m * m, name="primal_rows",
    )
    return res[0], res[1:5], res[5]


def primal_columns(prow, dmat, fr, npr):
    m = dmat.shape[0]
    p = npr.shape[0]
    step = 256

    def body(pr_ref, d_ref, fr_ref, n_ref, t_ref, f_ref, g_ref, sel):
        i = pl.program_id(0)

        @pl.when(i == 0)
        def _():
            one_hot_rows(pr_ref, sel, p, m)

        dh, dl = halves(d_ref[...])
        t_ref[:, pl.ds(pl.multiple_of(i * step, step), step)] = one_pass(sel[...], dh, NT) + one_pass(sel[...], dl, NT)

        @pl.when(i == m // step - 1)
        def _():
            both = halves(t_ref[...])
            for k in range(m // step):
                cols = slice(k * step, (k + 1) * step)
                ids = lax.broadcasted_iota(jnp.int32, (m, step), 0)
                sb = (ids == fr_ref[:, cols]).astype(F32).astype(BF16)
                f_ref[:, cols] = one_pass(both[0], sb, NN) + one_pass(both[1], sb, NN)
            g_ref[...] = three(n_ref[...], both, NT)

    whole = lambda shape: pl.BlockSpec(shape, lambda i: (0, 0), pipeline_mode=pl.Buffered(1))
    return call(
        body, [out(p, m), out(p, m), out(p, p)], [prow, dmat, fr, npr], grid=(m // step,),
        in_specs=[whole(prow.shape), pl.BlockSpec((step, m), lambda i: (i, 0)), whole(fr.shape), whole(npr.shape)],
        out_specs=[whole((p, m)), whole((p, m)), whole((p, p))], scratch=[VMEM((p, m), BF16)], flops=8 * p * m * m, name="primal_columns",
    )


def coarse_cut(place, crow):
    p, total = crow.shape
    width = total // (NZ * NY)

    def body(place_ref, c_ref, *refs):
        z, y = place_ref[0], place_ref[1]
        for k in range(NY):
            for j in range(NZ):
                at = (lax.rem(z + j, NZ) * NY + lax.rem(y + NY - k, NY)) * width
                refs[k][:, j * width:(j + 1) * width] = c_ref[:, pl.ds(pl.multiple_of(at, width), width)]

    return call(body, [out(p, NZ * width)] * NY, [place, crow],
                in_specs=[pl.BlockSpec(memory_space=SMEM), pl.BlockSpec(memory_space=VMEM)], name="coarse_cut")


def column(row, p):
    return jnp.transpose(jnp.broadcast_to(row, (128, 128)))[:p]


def sweep(ref, cols, loc, p, r):
    loc[0] = jnp.zeros((p, r), F32)
    for j in range(NX):
        for b in range(r // 128):
            lanes = slice(b * 128, (b + 1) * 128)
            loc[j + 1, :, lanes] = ref[j, :p, lanes] + cols[j] * loc[j, :, lanes]


def first_half(place, pieces, p):
    rows, r = pieces[0].shape

    def body(place_ref, a, b, c, d, send_ref, own_ref, low_ref, high_ref, v_ref, col_ref, q, loc, pv):
        h, x = place_ref[2], place_ref[3]
        for k, ref in enumerate((a, b, c, d)):
            q[lax.rem(x + k, NX)] = ref[...]
        pv[0] = jnp.ones((p, 128), F32)
        for j in range(NX):
            col_ref[j] = column(q[j, p:p + 1, :128], p)
            pv[j + 1] = pv[j] * col_ref[j]
        pv[NX + 1] = jnp.zeros((p, 128), F32)
        sweep(q, col_ref, loc, p, r)
        loc[NX + 1] = jnp.zeros((p, r), F32)
        upper = h == 1
        own_ref[...], low_ref[...], high_ref[...] = loc[x + 1], loc[x], loc[x + 2]
        for n, at in enumerate((x + 1, x, x + 2)):
            v_ref[n] = jnp.where(upper, pv[at], jnp.zeros((p, 128), F32))
        send_ref[:p] = jnp.where(upper, q[0, :p], loc[NX])
        send_ref[p:] = q[0, p:]

    return call(
        body, [out(rows, r)] + [out(p, r)] * 3 + [out(3, p, 128), out(NX, p, 128)], [place, *pieces],
        in_specs=[pl.BlockSpec(memory_space=SMEM)] + [pl.BlockSpec(memory_space=VMEM)] * 4,
        scratch=[VMEM((NX, rows, r), F32), VMEM((NX + 2, p, r), F32), VMEM((NX + 2, p, 128), F32)], name="first_half",
    )


def first_chains(place, over, own, low, high, v):
    p, r = own.shape

    def body(place_ref, over_ref, a, b, c, v_ref, ao, bo, co):
        last = jnp.logical_and(place_ref[2] == 0, place_ref[3] == NX - 1)
        rate = column(over_ref[p:p + 1, :128], p)
        for k in range(r // 128):
            lanes = slice(k * 128, (k + 1) * 128)
            came = over_ref[:p, lanes]
            ao[:, lanes] = a[:, lanes] + v_ref[0] * came
            bo[:, lanes] = b[:, lanes] + v_ref[1] * came
            co[:, lanes] = jnp.where(last, came + rate * a[:, lanes], c[:, lanes] + v_ref[2] * came)

    return call(body, [out(p, r)] * 3, [place, over, own, low, high, v],
                in_specs=[pl.BlockSpec(memory_space=SMEM)] + [pl.BlockSpec(memory_space=VMEM)] * 5, name="first_chains")


def second_half(place, pieces, cols):
    p, r = pieces[0].shape

    def body(place_ref, a, b, c, d, col_ref, send_ref, own_ref, q, loc):
        x = place_ref[3]
        for k, ref in enumerate((a, b, c, d)):
            q[lax.rem(x + k, NX)] = ref[...]
        sweep(q, col_ref, loc, p, r)
        own_ref[...] = loc[x + 1]
        send_ref[...] = loc[NX]

    return call(body, [out(p, r)] * 2, [place, *pieces, cols],
                in_specs=[pl.BlockSpec(memory_space=SMEM)] + [pl.BlockSpec(memory_space=VMEM)] * 5,
                scratch=[VMEM((NX, p, r), F32), VMEM((NX + 1, p, r), F32)], name="second_half")


def local(residual_in, neumann, dirichlet, coarse, decay, face_rows, primal):
    r0 = residual_in[0, 0]
    nmat = neumann[0, 0]
    dmat = dirichlet[0, 0]
    crow = coarse[0]
    dec = decay[0, 0]
    fr = face_rows[0]
    pr = primal[0, 0]
    m, r = r0.shape
    face = m // 4
    p = pr.shape[0]
    gx = lax.axis_index("gx")
    gy = lax.axis_index("gy")
    h, x = gx // NX, gx % NX
    z, y, c = gy // (NY * NC), (gy // NC) % NY, gy % NC
    flags = jnp.stack([gx > 0, gx < GX - 1, gy > 0, gy < GY - 1]).astype(F32)
    core = c.reshape(1).astype(jnp.int32)
    place = jnp.stack([z, y, h, x]).astype(jnp.int32)

    def exchange(blocks):
        return [ring(blocks[1], "gx", 1), ring(blocks[0], "gx", -1), ring(blocks[3], "gy", 1), ring(blocks[2], "gy", -1)]

    cut = coarse_cut(place, crow)
    fr = after(fr, cut)
    cblk = [cut[0]] + [pull_y(cut[k], k) for k in range(1, NY)]
    faces0 = gather_faces(fr, r0)
    recv0 = exchange(faces0)
    prow = jnp.pad(pr, (0, 128 - p))[None]
    prow = after(prow, cblk)
    npr, nprf, nprr = primal_rows(prow, nmat, fr, r0, p)
    dpt, dptf, g_own = primal_columns(prow, dmat, fr, npr)
    dec_rows = jnp.pad(dec[None], ((0, 7), (0, r - p)))

    def spread(cvec):
        return [cvec] + [pull_z(cvec, k) for k in range(1, NZ)]

    def product(own, gate, blk):
        own = after(own, *gate)
        twin = [pull_core(v) for v in own]
        return coarse_product(core, blk, [b for pair in zip(own, twin) for b in pair])

    def summed(part):
        total = part[0]
        for k in range(1, NY):
            total = total + pull_y(part[k], NY - k)
        return total

    cvec0 = first_cvec(flags, nprr, nprf, recv0)
    own0 = spread(cvec0)
    recv_g, fr_g, dpt, dptf, g_own = after((recv0, fr, dpt, dptf, g_own), cvec0)
    jump0, work0 = scatter_neumann(flags, fr_g, r0, recv_g, nmat)
    part0 = product(own0, [work0], cblk)
    work_g = after(work0, part0)
    dw0, base, packed, base_part = dirichlet_gather(fr, work_g, jump0, dmat, dptf, npr)
    got = [ring(packed[1], "gx", 1), ring(packed[0], "gx", -1)]
    cq0 = jnp.concatenate([summed(part0), dec_rows], axis=0)
    cq0 = after(cq0, packed)
    pieces = [cq0] + [pull_x(cq0, k) for k in range(1, NX)]
    send, own, low, high, v, cols = first_half(place, pieces, p)
    over = pull_half(send)
    v_late = after(v, got)
    chain0, low, high = first_chains(place, over, own, low, high, v_late)
    cols_r = chain_faces(packed[2:], dptf, chain0)
    got_y = [ring(cols_r[1], "gy", 1), ring(cols_r[0], "gy", -1)]
    chains = [chain0, low, high]
    cbase, gmat = couplings(flags, nprf, got, base_part, g_own)
    cvec1 = next_cvec(flags, cbase, gmat, chains, nprf, got_y)

    own1 = spread(cvec1)
    part1 = product(own1, [], cblk)
    cq1 = summed(part1)
    fr_h = after(fr, cq1)
    jump1, dc0, work1 = second_neumann(flags, fr_h, base, got + got_y, dpt, chains, nmat)
    pieces = [cq1] + [pull_x(cq1, k) for k in range(1, NX)]
    send, own = second_half(place, pieces, after(cols, work1))
    over = pull_half(send)
    work1 = after(work1, send)
    sol, res = second_dirichlet(work1, jump1, dw0, dc0, dmat)
    solution, residual = last_update(dpt, own, over, v, sol, res)
    return (solution[None, None], residual[None, None])


def solution(mesh):
    lead = P("gx", "gy", None, None)
    vec = P("gx", "gy", None)
    return jax.shard_map(
        local,
        mesh=mesh,
        in_specs=(lead, lead, lead, vec, vec, vec, vec),
        out_specs=(lead, lead),
        check_vma=False,
    )
```
